32 devices in a mesh: blk: 8 (over z, x), grp: 4 (over y, core).
Axes of the slice: x: 2, y: 2, z: 4, core: 2. Of those that a mesh axis runs over, the one named last changes fastest.
Arguments:
- tokens: bfloat16 [512, 8192], P(('blk', 'grp')), may hold values from -6 to 6
- cotangent: bfloat16 [512, 8192], P(('blk', 'grp')), may hold values from -6 to 6
- gate_weight: bfloat16 [8192, 4096], P(None, 'blk'), may hold values from -0.0625 to 0.0625
- up_weight: bfloat16 [8192, 4096], P(None, 'blk'), may hold values from -0.0625 to 0.0625
- down_weight: bfloat16 [4096, 8192], P('blk'), may hold values from -0.09375 to 0.09375
- a_gate: bfloat16 [256, 16, 8192], P('blk'), may hold values from -0.0625 to 0.0625
- a_up: bfloat16 [256, 16, 8192], P('blk'), may hold values from -0.0625 to 0.0625
- down_output_factors: bfloat16 [256, 16, 8192], P('blk'), may hold values from -0.375 to 0.375
- b_gate: bfloat16 [256, 16, 4096], P(None, None, 'blk'), may hold values from -0.375 to 0.375
- b_up: bfloat16 [256, 16, 4096], P(None, None, 'blk'), may hold values from -0.375 to 0.375
- a_down: bfloat16 [256, 16, 4096], P(None, None, 'blk'), may hold values from -0.09375 to 0.09375
- tenant_of_row: int32 [512], replicated, may hold values from 0 to 255, as said below
- adapter_slot: int32 [256], replicated, may hold values from 0 to 255, as said below
Outputs:
- mixed: bfloat16 [512, 8192], P(('blk', 'grp'))
- input_grad: bfloat16 [512, 8192], P(('blk', 'grp'))
- grad_a_gate: float32 [256, 16, 8192], P(('blk', 'grp'))
- grad_a_up: float32 [256, 16, 8192], P(('blk', 'grp'))
- grad_b_down: float32 [256, 16, 8192], P(('blk', 'grp'))
- grad_b_gate: float32 [256, 16, 4096], P('grp', None, 'blk')
- grad_b_up: float32 [256, 16, 4096], P('grp', None, 'blk')
- grad_a_down: float32 [256, 16, 4096], P('grp', None, 'blk')
The draws below stay inside these ranges and needn't reach their ends.
Inputs may be any that keep to these rules, and one draw needn't show every extreme that they name: `tenant_of_row`: among the rows held by the devices of one index of grp, for each index b of blk at most 32 rows have tenants whose adapter slot s has s // 32 == b, and for some b exactly 32 do. A permutation: tenant t's factors in a_gate, a_up and down_output_factors, and its gradients of them, stand at index adapter_slot[t].
All inputs are finite; a program needn't handle non-finite values.
Results may differ from the reference program's by a relative error of at most 0.02.
Values may be sent and summed in bfloat16 or wider, within the bound.
A program may use at most 192 MiB of HBM per device.

```python
import jax
import jax.numpy as jnp
from jax import lax

D = 8192
FF = 4096
RANK = 16
TENANTS = 256
TOK_DEV = 16
TOKENS = 512
GROUP_ROWS = 128
N_BLK = 8


def tenant_layout(key):
    base_key = jax.random.fold_in(key, 7013)
    slot_perm = jax.random.permutation(jax.random.fold_in(base_key, 1), TENANTS).astype(jnp.int32)
    tenant_at = jnp.argsort(slot_perm, stable=True).astype(jnp.int32)
    blocks = GROUP_ROWS // TOK_DEV
    groups = TOKENS // GROUP_ROWS
    per_owner = TENANTS // blocks
    capacity = 2 * TOK_DEV

    def one_group(group_key):
        sub_keys = jax.random.split(group_key, 4)
        owner_sorting = jax.random.permutation(sub_keys[0], blocks).astype(jnp.int32)
        pair_split = jax.random.randint(sub_keys[1], (blocks // 2,), 0, capacity + 1).astype(jnp.int32)
        pair_split = pair_split.at[0].set(0)
        owner_loads = jnp.zeros((blocks,), jnp.int32).at[owner_sorting[0::2]].set(pair_split)
        owner_loads = owner_loads.at[owner_sorting[1::2]].set(capacity - pair_split)
        bounds = jnp.cumsum(owner_loads).astype(jnp.int32)
        row_owner = jnp.searchsorted(bounds, jnp.arange(GROUP_ROWS, dtype=jnp.int32), side='right').astype(jnp.int32)
        row_owner = row_owner[jax.random.permutation(sub_keys[2], GROUP_ROWS)]
        local_pick = jax.random.randint(sub_keys[3], (GROUP_ROWS,), 0, per_owner).astype(jnp.int32)
        return tenant_at[row_owner * per_owner + local_pick]
    group_keys = jax.random.split(jax.random.fold_in(base_key, 2), groups)
    layout_rows = jax.vmap(one_group)(group_keys)
    layout_rows = layout_rows.reshape(groups, blocks, TOK_DEV).transpose(1, 0, 2).reshape(TOKENS)
    return (layout_rows.astype(jnp.int32), slot_perm)


def draw_tenant_of_row(key, part):
    return tenant_layout(key)[0]


def draw_adapter_slot(key, part):
    return tenant_layout(key)[1]


def block_levels(stream_key, extent, pieces, least, high):
    level, own = 1.0, jax.random.fold_in(stream_key, 6)
    for axis_at, blocks in pieces:
        draws = jnp.exp(jax.random.uniform(jax.random.fold_in(own, axis_at), (blocks,), jnp.float32, least / len(pieces), high / len(pieces)))
        level = level * jnp.repeat(draws, extent[axis_at] // blocks).reshape([-1 if axis == axis_at else 1 for axis in range(len(extent))])
    return level


def centred(rng, extent, width, most, shards=(), kind=jnp.bfloat16):
    loudness = block_levels(rng, extent, shards, -0.22, 0.18) if shards else 1.0
    result = jax.random.normal(rng, extent, jnp.float32) * width * loudness
    return jnp.minimum(jnp.maximum(result, -most), most).astype(kind)


def setup_inputs(seed: int = 0) -> dict:
    streams_of = jax.random.split(jax.random.key(seed), 14)
    tokens = centred(streams_of[0], (TOKENS, D), 1.0, 6.0, ((0, 32),))
    cotangent = centred(streams_of[1], (TOKENS, D), 0.5, 6.0, ((0, 32),))
    gate_weight = centred(streams_of[2], (D, FF), D ** -0.5, 0.0625, ((1, 8),))
    up_weight = centred(streams_of[3], (D, FF), D ** -0.5, 0.0625, ((1, 8),))
    down_weight = centred(streams_of[4], (FF, D), FF ** -0.5, 0.09375, ((0, 8),))
    a_gate = centred(streams_of[5], (TENANTS, RANK, D), D ** -0.5, 0.0625, ((0, 8),))
    a_up = centred(streams_of[6], (TENANTS, RANK, D), D ** -0.5, 0.0625, ((0, 8),))
    down_output_factors = centred(streams_of[7], (TENANTS, RANK, D), (16 * RANK) ** -0.5, 0.375, ((0, 8),))
    b_gate = centred(streams_of[8], (TENANTS, RANK, FF), (16 * RANK) ** -0.5, 0.375, ((2, 8),))
    b_up = centred(streams_of[9], (TENANTS, RANK, FF), (16 * RANK) ** -0.5, 0.375, ((2, 8),))
    a_down = centred(streams_of[10], (TENANTS, RANK, FF), FF ** -0.5, 0.09375, ((2, 8),))
    tenant_of_row = draw_tenant_of_row(jax.random.fold_in(streams_of[13], 71), 0)
    adapter_slot = draw_adapter_slot(jax.random.fold_in(streams_of[13], 71), 0)
    return {"tokens": tokens, "cotangent": cotangent, "gate_weight": gate_weight, "up_weight": up_weight, "down_weight": down_weight, "a_gate": a_gate, "a_up": a_up, "down_output_factors": down_output_factors, "b_gate": b_gate, "b_up": b_up, "a_down": a_down, "tenant_of_row": tenant_of_row, "adapter_slot": adapter_slot}


adapter_scale = 2.0


def silu_pair(gate_in):
    sigmoid_val = jax.nn.sigmoid(gate_in)
    return gate_in * sigmoid_val, sigmoid_val * (1.0 + gate_in * (1.0 - sigmoid_val))


def contract_dims(left_op, right_op, form):
    return jnp.einsum(form, left_op.astype(jnp.float32), right_op.astype(jnp.float32), precision=lax.Precision.HIGHEST)


def round_sum(parts):
    rounded = lax.optimization_barrier(parts.astype(jnp.bfloat16))
    return jnp.sum(rounded.astype(jnp.float32), axis=1).astype(jnp.bfloat16)


def reference(tokens, cotangent, gate_weight, up_weight, down_weight, a_gate, a_up, down_output_factors, b_gate, b_up, a_down, tenant_of_row, adapter_slot):
    per_owner = TENANTS // N_BLK
    unit_width = FF // N_BLK
    block_rows = 128 if TOKENS % 128 == 0 else TOKENS
    num_blocks = TOKENS // block_rows
    slot_of_row = adapter_slot[tenant_of_row].astype(jnp.int32)
    gate_blocks = gate_weight.reshape(D, N_BLK, unit_width)
    up_blocks = up_weight.reshape(D, N_BLK, unit_width)
    down_blocks = down_weight.reshape(N_BLK, unit_width, D)

    def one_block(totals, block_id):
        first_row = (block_id * block_rows).astype(jnp.int32)
        row_x = lax.dynamic_slice_in_dim(tokens, first_row, block_rows, 0)
        row_dy = lax.dynamic_slice_in_dim(cotangent, first_row, block_rows, 0)
        row_slot = lax.dynamic_slice_in_dim(slot_of_row, first_row, block_rows, 0)
        row_tenant = lax.dynamic_slice_in_dim(tenant_of_row.astype(jnp.int32), first_row, block_rows, 0)
        row_owner = row_slot // per_owner
        fac_ag = a_gate[row_slot]
        fac_au = a_up[row_slot]
        fac_bd = down_output_factors[row_slot]
        fac_bg = b_gate[row_tenant]
        fac_bu = b_up[row_tenant]
        fac_ad = a_down[row_tenant]
        p_gate = contract_dims(row_x, fac_ag, "nd,nrd->nr").astype(jnp.bfloat16)
        p_up = contract_dims(row_x, fac_au, "nd,nrd->nr").astype(jnp.bfloat16)
        grad_q = (adapter_scale * contract_dims(row_dy, fac_bd, "nd,nrd->nr")).astype(jnp.bfloat16)
        gate_val = jnp.dot(row_x, gate_weight, preferred_element_type=jnp.float32) + adapter_scale * contract_dims(p_gate, fac_bg, "nr,nrf->nf")
        up_val = jnp.dot(row_x, up_weight, preferred_element_type=jnp.float32) + adapter_scale * contract_dims(p_up, fac_bu, "nr,nrf->nf")
        act_val, act_slope = silu_pair(gate_val)
        hidden = (act_val * up_val).astype(jnp.bfloat16)
        low_q = contract_dims(hidden, fac_ad, "nf,nrf->nr").astype(jnp.bfloat16)
        owner_hot = (row_owner[:, None] == jnp.arange(N_BLK, dtype=jnp.int32)[None, :]).astype(jnp.float32)
        mixed_extra = adapter_scale * contract_dims(low_q, fac_bd, "nr,nrd->nd")
        mixed_parts = contract_dims(hidden.reshape(block_rows, N_BLK, unit_width), down_blocks, "nkf,kfd->nkd") + owner_hot[:, :, None] * mixed_extra[:, None, :]
        mixed_rows = round_sum(mixed_parts)
        grad_h = lax.dot_general(row_dy, down_weight, (((1,), (1,)), ((), ())), preferred_element_type=jnp.float32) + contract_dims(grad_q, fac_ad, "nr,nrf->nf")
        grad_gate = (grad_h * up_val * act_slope).astype(jnp.bfloat16)
        grad_up = (grad_h * act_val).astype(jnp.bfloat16)
        dp_gate = (adapter_scale * contract_dims(grad_gate, fac_bg, "nf,nrf->nr")).astype(jnp.bfloat16)
        dp_up = (adapter_scale * contract_dims(grad_up, fac_bu, "nf,nrf->nr")).astype(jnp.bfloat16)
        input_extra = contract_dims(dp_gate, fac_ag, "nr,nrd->nd") + contract_dims(dp_up, fac_au, "nr,nrd->nd")
        input_parts = contract_dims(grad_gate.reshape(block_rows, N_BLK, unit_width), gate_blocks, "nkf,dkf->nkd")
        input_parts = input_parts + contract_dims(grad_up.reshape(block_rows, N_BLK, unit_width), up_blocks, "nkf,dkf->nkd")
        input_parts = input_parts + owner_hot[:, :, None] * input_extra[:, None, :]
        input_rows = round_sum(input_parts)
        sum_ag = totals[0] + jax.ops.segment_sum(contract_dims(dp_gate, row_x, "nr,nd->nrd"), row_slot, num_segments=TENANTS)
        sum_au = totals[1] + jax.ops.segment_sum(contract_dims(dp_up, row_x, "nr,nd->nrd"), row_slot, num_segments=TENANTS)
        sum_bd = totals[2] + adapter_scale * jax.ops.segment_sum(contract_dims(low_q, row_dy, "nr,nd->nrd"), row_slot, num_segments=TENANTS)
        sum_bg = totals[3] + adapter_scale * jax.ops.segment_sum(contract_dims(p_gate, grad_gate, "nr,nf->nrf"), row_tenant, num_segments=TENANTS)
        sum_bu = totals[4] + adapter_scale * jax.ops.segment_sum(contract_dims(p_up, grad_up, "nr,nf->nrf"), row_tenant, num_segments=TENANTS)
        sum_ad = totals[5] + jax.ops.segment_sum(contract_dims(grad_q, hidden, "nr,nf->nrf"), row_tenant, num_segments=TENANTS)
        return (sum_ag, sum_au, sum_bd, sum_bg, sum_bu, sum_ad), (mixed_rows, input_rows)

    zeros_d = jnp.zeros((TENANTS, RANK, D), jnp.float32)
    zero_feature_block = jnp.zeros((TENANTS, RANK, FF), jnp.float32)
    totals, stacked = lax.scan(one_block, (zeros_d, zeros_d, zeros_d, zero_feature_block, zero_feature_block, zero_feature_block), jnp.arange(num_blocks, dtype=jnp.int32))
    mixed = stacked[0].reshape(TOKENS, D)
    input_grad = stacked[1].reshape(TOKENS, D)
    return (mixed, input_grad, totals[0], totals[1], totals[2], totals[3], totals[4], totals[5])
```

```python
import functools

import jax
import jax.numpy as jnp
from jax import lax
from jax.experimental import pallas as pl
from jax.experimental.pallas import tpu as pltpu
from jax.sharding import PartitionSpec as P

MESH = pl.DeviceIdType.MESH
bf16 = jnp.bfloat16
vmem_grant = 60 * 2**20
f32 = jnp.float32


def remote(src, dst, send, recv, to):
    return pltpu.make_async_remote_copy(
        src_ref=src,
        dst_ref=dst,
        send_sem=send,
        recv_sem=recv,
        device_id={"blk": to},
        device_id_type=MESH,
    )


def place(blocks):
    me = lax.axis_index("blk")
    line = blocks // 2
    row = me // 2
    col = me - 2 * row
    partner = me + 1 - 2 * col
    return me, line, row, col, partner


def greet(me, line, row, partner):
    barrier = pltpu.get_barrier_semaphore()
    pl.semaphore_signal(barrier, inc=1, device_id={"blk": partner}, device_id_type=MESH)

    @pl.when(row < line - 1)
    def _():
        pl.semaphore_signal(barrier, inc=1, device_id={"blk": me + 2}, device_id_type=MESH)

    @pl.when(row > 0)
    def _():
        pl.semaphore_signal(barrier, inc=1, device_id={"blk": me - 2}, device_id_type=MESH)

    peers = 1 + (row < line - 1).astype(jnp.int32) + (row > 0).astype(jnp.int32)
    pl.semaphore_wait(barrier, peers)


def gather_kernel(
    blocks, x_ref, d_ref, xo_ref, do_ref, hold, own_sem, up_s, up_r, dn_s, dn_r, ac_s, ac_r, ex_s, ex_r
):
    me, line, row, col, partner = place(blocks)
    outs = (xo_ref, do_ref)
    ins = (x_ref, d_ref)
    above, below = me + 2, me - 2

    def up_copy(c, src, block, s):
        return remote(src, outs[c].at[block], up_s.at[c, s], up_r.at[c, s], above)

    def dn_copy(c, src, block, s):
        return remote(src, outs[c].at[block], dn_s.at[c, s], dn_r.at[c, s], below)

    def ac_copy(c, src, at):
        return remote(
            src, outs[c].at[2 * at + col], ac_s.at[c, at], ac_r.at[c, at], partner
        )

    def ac_arrival(c, at):
        ref = outs[c].at[2 * at + 1 - col]
        return remote(ref, ref, ac_s.at[c, at], ac_r.at[c, at], partner)

    def ex_copy(direction, to):
        ref = do_ref.at[partner]
        return remote(ref, ref, ex_s.at[direction], ex_r.at[direction], to)

    def ex_arrival(direction, block, to):
        ref = do_ref.at[block]
        return remote(ref, ref, ex_s.at[direction], ex_r.at[direction], to)

    greet(me, line, row, partner)
    own = []
    for c in range(2):
        ac_copy(c, ins[c], row).start()

        @pl.when(row < line - 1)
        def _():
            up_copy(c, ins[c], me, 0).start()

        @pl.when(row > 0)
        def _():
            dn_copy(c, ins[c], me, 0).start()

    loads = []
    for c in range(2):
        copy = pltpu.make_async_copy(ins[c], hold.at[c], own_sem.at[0, c])
        copy.start()
        loads.append(copy)
    for c in range(2):
        loads[c].wait()
        copy = pltpu.make_async_copy(hold.at[c], outs[c].at[me], own_sem.at[1, c])
        copy.start()
        own.append(copy)
    for s in range(1, line):
        for c in range(2):

            @pl.when(row >= s)
            def _():
                block = me - 2 * s
                ref = outs[c].at[block]
                up_copy(c, ref, block, s - 1).wait_recv()
                if s < line - 1:

                    @pl.when(row < line - 1)
                    def _():
                        up_copy(c, ref, block, s).start()

                if c == 0 or s > 1:
                    ac_copy(c, ref, row - s).start()

            @pl.when(row + s < line)
            def _():
                block = me + 2 * s
                ref = outs[c].at[block]
                dn_copy(c, ref, block, s - 1).wait_recv()
                if s < line - 1:

                    @pl.when(row > 0)
                    def _():
                        dn_copy(c, ref, block, s).start()

                if c == 0 or s > 1:
                    ac_copy(c, ref, row + s).start()

        if s == 1:
            ac_arrival(1, row).wait_recv()

            @pl.when(row < line - 1)
            def _():
                ex_copy(0, above).start()

            @pl.when(row > 0)
            def _():
                ex_copy(1, below).start()

    ac_arrival(0, row).wait_recv()
    ac_copy(0, x_ref, row).wait_send()
    ac_copy(1, d_ref, row).wait_send()
    for s in range(1, line):
        for c in range(2):
            for ok, at in ((row >= s, row - s), (row + s < line, row + s)):

                @pl.when(ok)
                def _():
                    if c == 0 or s > 1:
                        ac_arrival(c, at).wait_recv()
                        ac_copy(c, outs[c].at[2 * at + col], at).wait_send()

    @pl.when(row > 0)
    def _():
        ex_arrival(0, partner - 2, above).wait_recv()
        ex_copy(1, below).wait_send()

    @pl.when(row < line - 1)
    def _():
        ex_arrival(1, partner + 2, below).wait_recv()
        ex_copy(0, above).wait_send()

    for s in range(line - 1):
        for c in range(2):

            @pl.when((row >= s) & (row < line - 1))
            def _():
                src = ins[c] if s == 0 else outs[c].at[me - 2 * s]
                up_copy(c, src, me - 2 * s, s).wait_send()

            @pl.when((row + s < line) & (row > 0))
            def _():
                src = ins[c] if s == 0 else outs[c].at[me + 2 * s]
                dn_copy(c, src, me + 2 * s, s).wait_send()

    for copy in own:
        copy.wait()


def gather_rows(blocks, x, dy):
    line = blocks // 2
    shape = jax.ShapeDtypeStruct((blocks,) + x.shape, x.dtype)
    dma = pltpu.SemaphoreType.DMA
    got = pl.pallas_call(
        functools.partial(gather_kernel, blocks),
        out_shape=(shape, shape),
        in_specs=[pl.BlockSpec(memory_space=pl.ANY)] * 2,
        out_specs=(pl.BlockSpec(memory_space=pl.ANY),) * 2,
        scratch_shapes=[pltpu.VMEM((2,) + x.shape, x.dtype), dma((2, 2))] + [dma((2, line))] * 6 + [dma((2,))] * 2,
        compiler_params=pltpu.CompilerParams(
            collective_id=0, has_side_effects=True, vmem_limit_bytes=vmem_grant
        ),
        name="gather_rows",
    )(x, dy)
    return [part.reshape((-1,) + x.shape[1:]) for part in got]


def scatter_kernel(
    blocks,
    m_ref,
    b_ref,
    mo_ref,
    bo_ref,
    pair_buf,
    line_buf,
    top_buf,
    ex_buf,
    cross_buf,
    ac_s,
    ac_r,
    up_s,
    up_r,
    dn_s,
    dn_r,
    ex_s,
    ex_r,
):
    me, line, row, col, partner = place(blocks)
    parts = (m_ref, b_ref)
    outs = (mo_ref, bo_ref)
    above, below = me + 2, me - 2
    width = m_ref.shape[-1]
    tile = width // 8

    def total(dst, srcs):
        def body(k, carry):
            at = pl.ds(pl.multiple_of(k * tile, tile), tile)
            acc = srcs[0][:, at].astype(f32)
            for src in srcs[1:]:
                acc = acc + src[:, at].astype(f32)
            dst[:, at] = acc.astype(dst.dtype)
            return carry

        lax.fori_loop(0, width // tile, body, 0)

    def ac_copy(c, src, at):
        return remote(src, pair_buf.at[c, at], ac_s.at[c, at], ac_r.at[c, at], partner)

    def up_copy(c, at):
        return remote(
            pair_buf.at[c, at], line_buf.at[c, at], up_s.at[c, at], up_r.at[c, at], above
        )

    def dn_copy(c, at, landing):
        return remote(pair_buf.at[c, at], landing, dn_s.at[c, at], dn_r.at[c, at], below)

    def ex_copy(direction, block, to):
        return remote(
            b_ref.at[block], ex_buf.at[direction], ex_s.at[direction], ex_r.at[direction], to
        )

    greet(me, line, row, partner)

    @pl.when(row < line - 1)
    def _():
        ex_copy(0, partner + 2, above).start()

    @pl.when(row > 0)
    def _():
        ex_copy(1, partner - 2, below).start()

    def spots(s):
        if s == 0:
            return ((None, row),)
        return ((row + s < line, row + s), (row >= s, row - s))

    def crossing(c, s):
        return c == 0 or s > 1

    def guard(ok, body):
        if ok is None:
            body()
        else:
            pl.when(ok)(body)

    for s in range(line - 1, -1, -1):
        for c in range(2):
            for ok, at in spots(s):
                if crossing(c, s):
                    guard(ok, lambda: ac_copy(c, parts[c].at[2 * at + 1 - col], at).start())

    @pl.when(row > 0)
    def _():
        ex_copy(0, partner, above).wait_recv()

    @pl.when(row < line - 1)
    def _():
        ex_copy(1, partner, below).wait_recv()

    @pl.when((row > 0) & (row < line - 1))
    def _():
        total(cross_buf, (b_ref.at[partner], ex_buf.at[0], ex_buf.at[1]))

    @pl.when(row == 0)
    def _():
        total(cross_buf, (b_ref.at[partner], ex_buf.at[1]))

    @pl.when((row > 0) & (row == line - 1))
    def _():
        total(cross_buf, (b_ref.at[partner], ex_buf.at[0]))

    ac_copy(1, cross_buf, row).start()

    for s in range(line - 1, 0, -1):
        for c in range(2):

            @pl.when(row + s < line)
            def _():
                at = row + s
                slot = pair_buf.at[c, at]
                mine = parts[c].at[2 * at + col]
                base = (mine,)
                if crossing(c, s):
                    ac_copy(c, mine, at).wait_recv()
                    base = (mine, slot)
                if s < line - 1:

                    @pl.when(row > 0)
                    def _():
                        up_copy(c, at).wait_recv()
                        total(slot, base + (line_buf.at[c, at],))

                @pl.when(row == 0)
                def _():
                    total(slot, base)

                up_copy(c, at).start()

            @pl.when(row >= s)
            def _():
                at = row - s
                slot = pair_buf.at[c, at]
                mine = parts[c].at[2 * at + col]
                base = (mine,)
                if crossing(c, s):
                    ac_copy(c, mine, at).wait_recv()
                    base = (mine, slot)
                if s < line - 1:

                    @pl.when(row < line - 1)
                    def _():
                        dn_copy(c, at, line_buf.at[c, at]).wait_recv()
                        total(slot, base + (line_buf.at[c, at],))

                @pl.when(row == line - 1)
                def _():
                    total(slot, base)

                if s == 1:
                    dn_copy(c, at, top_buf.at[c]).start()
                else:
                    dn_copy(c, at, line_buf.at[c, at]).start()

    for c in range(2):
        mine = parts[c].at[me]
        slot = pair_buf.at[c, row]
        from_below = line_buf.at[c, row]
        from_above = top_buf.at[c]
        ac_copy(c, mine, row).wait_recv()

        @pl.when(row > 0)
        def _():
            up_copy(c, row).wait_recv()

        @pl.when(row < line - 1)
        def _():
            dn_copy(c, row, from_above).wait_recv()

        @pl.when((row > 0) & (row < line - 1))
        def _():
            total(outs[c], (mine, slot, from_below, from_above))

        @pl.when(row == 0)
        def _():
            total(outs[c], (mine, slot, from_above))

        @pl.when((row > 0) & (row == line - 1))
        def _():
            total(outs[c], (mine, slot, from_below))

    ac_copy(0, m_ref.at[partner], row).wait_send()
    ac_copy(1, cross_buf, row).wait_send()
    for s in range(1, line):
        for c in range(2):
            for ok, at in spots(s):
                if crossing(c, s):
                    guard(ok, lambda: ac_copy(c, parts[c].at[2 * at + 1 - col], at).wait_send())

            @pl.when(row + s < line)
            def _():
                up_copy(c, row + s).wait_send()

            @pl.when(row >= s)
            def _():
                dn_copy(c, row - s, line_buf.at[c, row - s]).wait_send()

    @pl.when(row < line - 1)
    def _():
        ex_copy(0, partner + 2, above).wait_send()

    @pl.when(row > 0)
    def _():
        ex_copy(1, partner - 2, below).wait_send()


def scatter_rows(blocks, mixed_terms, back_terms):
    line = blocks // 2
    rows = mixed_terms.shape[0] // blocks
    width = mixed_terms.shape[1]
    dma = pltpu.SemaphoreType.DMA
    block = jax.ShapeDtypeStruct((rows, width), bf16)
    block_bytes = 2 * rows * width
    return pl.pallas_call(
        functools.partial(scatter_kernel, blocks),
        out_shape=(block, block),
        in_specs=[pl.BlockSpec(memory_space=pltpu.VMEM)] * 2,
        out_specs=(pl.BlockSpec(memory_space=pltpu.VMEM),) * 2,
        scratch_shapes=[
            pltpu.VMEM((2, line, rows, width), bf16),
            pltpu.VMEM((2, line, rows, width), bf16),
            pltpu.VMEM((2, rows, width), bf16),
            pltpu.VMEM((2, rows, width), bf16),
            pltpu.VMEM((rows, width), bf16),
        ]
        + [dma((2, line))] * 6
        + [dma((2,))] * 2,
        compiler_params=pltpu.CompilerParams(
            collective_id=3,
            has_side_effects=True,
            vmem_limit_bytes=block_bytes * (2 * blocks + 4 * line + 12) + 2 * 2**20,
        ),
        name="scatter_rows",
    )(
        mixed_terms.reshape(blocks, rows, width),
        back_terms.reshape(blocks, rows, width),
    )


def sum_kernel(blocks, c_ref, o_ref, land, send_sem, recv_sem):
    me = lax.axis_index("blk")
    barrier = pltpu.get_barrier_semaphore()
    for k in range(1, blocks):
        pl.semaphore_signal(
            barrier, inc=1, device_id={"blk": lax.rem(me + k, blocks)}, device_id_type=MESH
        )
    pl.semaphore_wait(barrier, blocks - 1)
    copies = []
    for k in range(1, blocks):
        copy = remote(
            c_ref, land.at[k], send_sem.at[k], recv_sem.at[k], lax.rem(me + k, blocks)
        )
        copy.start()
        copies.append(copy)
    acc = c_ref[...].astype(f32)
    for k in range(1, blocks):
        copies[k - 1].wait_recv()
        acc = acc + land[k].astype(f32)
    o_ref[...] = acc.astype(o_ref.dtype)
    for copy in copies:
        copy.wait_send()


def sum_over_blk(blocks, coeffs, collective_id):
    dma = pltpu.SemaphoreType.DMA
    return pl.pallas_call(
        functools.partial(sum_kernel, blocks),
        out_shape=jax.ShapeDtypeStruct(coeffs.shape, coeffs.dtype),
        in_specs=[pl.BlockSpec(memory_space=pltpu.VMEM)],
        out_specs=pl.BlockSpec(memory_space=pltpu.VMEM),
        scratch_shapes=[
            pltpu.VMEM((blocks,) + coeffs.shape, coeffs.dtype),
            dma((blocks,)),
            dma((blocks,)),
        ],
        compiler_params=pltpu.CompilerParams(
            collective_id=collective_id, has_side_effects=True, vmem_limit_bytes=8 * 2**20
        ),
        name="sum_over_blk",
    )(coeffs)


adapter_scale = 2.0


def silu_pair(gate_in):
    sigmoid_val = jax.nn.sigmoid(gate_in)
    return (gate_in * sigmoid_val, sigmoid_val * (1.0 + gate_in * (1.0 - sigmoid_val)))


def dot(a, b, dims=((1,), (0,))):
    return lax.dot_general(a, b, (dims, ((), ())), preferred_element_type=f32)


def ranks_pattern(rank, entries):
    column = lax.broadcasted_iota(jnp.int32, (rank, entries * rank), 1)
    row = lax.broadcasted_iota(jnp.int32, (rank, entries * rank), 0)
    return (column % rank == row).astype(bf16)


def lanes_entry(rank, first, count):
    return (lax.broadcasted_iota(jnp.int32, (1, count), 1) // rank) + first


def spread_kernel(coeffs, mask, pattern):
    return jnp.where(mask, dot(coeffs, pattern), 0.0).astype(bf16)


def select_kernel(full, mask, pattern):
    kept = jnp.where(mask, full, 0.0).astype(bf16)
    return dot(pattern, kept, ((1,), (1,)))


def inputs_kernel(
    rank, x, d, gw, uw, dw, ag, au, bd, slot, pat, gate_o, up_o, gh_o, low_o, qg, qu, qd
):
    step = pl.program_id(0)
    xv, dv = x[...], d[...]
    terms = (
        (gate_o, lambda: dot(xv, gw[...])),
        (up_o, lambda: dot(xv, uw[...])),
        (gh_o, lambda: dot(dv, dw[...], ((1,), (1,)))),
        (qg, lambda: dot(xv, ag[...], ((1,), (1,)))),
        (qu, lambda: dot(xv, au[...], ((1,), (1,)))),
        (qd, lambda: dot(dv, bd[...], ((1,), (1,)))),
    )

    @pl.when(step == 0)
    def _():
        for ref, _term in terms:
            ref[...] = jnp.zeros_like(ref)

    for ref, term in terms:
        ref[...] += term()

    @pl.when(step == pl.num_programs(0) - 1)
    def _():
        mask = slot[...] == lanes_entry(rank, 0, qg.shape[1])
        for k, (ref, scale) in enumerate(((qg, 1.0), (qu, 1.0), (qd, adapter_scale))):
            low_o[k * rank : (k + 1) * rank, :] = (
                scale * select_kernel(ref[...], mask, pat[...])
            ).astype(bf16)


def input_terms(rank, x, dy, gw, uw, dw, ag, au, bd, slot, pat):
    rows, width = x.shape
    units, own = gw.shape[1], ag.shape[0]
    tile = min(512, width)
    across = lambda n: pl.BlockSpec((n, tile), lambda i: (0, i))
    down = lambda n: pl.BlockSpec((tile, n), lambda i: (i, 0))
    whole = lambda *shape: pl.BlockSpec(shape, lambda i: (0, 0))
    acc = jax.ShapeDtypeStruct((rows, units), f32)
    return pl.pallas_call(
        functools.partial(inputs_kernel, rank),
        grid=(width // tile,),
        out_shape=(acc, acc, acc, jax.ShapeDtypeStruct((3 * rank, rows), bf16)),
        in_specs=[
            across(rows),
            across(rows),
            down(units),
            down(units),
            across(units),
            across(own),
            across(own),
            across(own),
            whole(rows, 1),
            whole(*pat.shape),
        ],
        out_specs=(whole(rows, units),) * 3 + (whole(3 * rank, rows),),
        scratch_shapes=[pltpu.VMEM((rows, own), f32)] * 3,
        compiler_params=pltpu.CompilerParams(vmem_limit_bytes=vmem_grant),
        cost_estimate=pl.CostEstimate(
            flops=6 * rows * width * (units + own),
            bytes_accessed=6 * width * (units + own),
            transcendentals=0,
        ),
        name="input_terms",
    )(x, dy, gw, uw, dw, ag, au, bd, slot, pat)


def middle_kernel(
    rank, gate, up, gh, coeffs, tenant, pat, bg, bu, ad, hid_o, gg_o, gu_o, low_o, sg, su, sh, low
):
    half, step = pl.program_id(0), pl.program_id(1)
    last = pl.num_programs(1) - 1
    count = bg.shape[0]
    mask = tenant[...] == lanes_entry(rank, step * (count // rank), count)

    @pl.when((half == 0) & (step == 0))
    def _():
        sg[...] = gate[...]
        su[...] = up[...]
        sh[...] = gh[...]

    @pl.when(half == 0)
    def _():
        for k, (acc, fac, scale) in enumerate(
            ((sg, bg, adapter_scale), (su, bu, adapter_scale), (sh, ad, 1.0))
        ):
            given = coeffs[:, k * rank : (k + 1) * rank]
            acc[...] += scale * dot(spread_kernel(given, mask, pat[...]), fac[...])

    @pl.when((half == 0) & (step == last))
    def _():
        act_val, act_slope = silu_pair(sg[...])
        up_val, grad_h = su[...], sh[...]
        hid_o[...] = (act_val * up_val).astype(bf16)
        gg_o[...] = (grad_h * up_val * act_slope).astype(bf16)
        gu_o[...] = (grad_h * act_val).astype(bf16)
        low[...] = jnp.zeros_like(low)

    @pl.when(half == 1)
    def _():
        for k, (rows, fac, scale) in enumerate(
            ((hid_o, ad, 1.0), (gg_o, bg, adapter_scale), (gu_o, bu, adapter_scale))
        ):
            full = dot(rows[...], fac[...], ((1,), (1,)))
            low[k * rank : (k + 1) * rank, :] += scale * select_kernel(full, mask, pat[...])

    @pl.when((half == 1) & (step == last))
    def _():
        low_o[...] = low[...].astype(bf16)


def middle_terms(rank, gate, up, gh, coeffs, tenant, bg, bu, ad):
    rows, units = gate.shape
    total = bg.shape[0]
    tile = min(1024, total)
    pat = ranks_pattern(rank, tile // rank)
    whole = lambda *shape: pl.BlockSpec(shape, lambda h, i: (0, 0))
    down = pl.BlockSpec((tile, units), lambda h, i: (i, 0))
    block = jax.ShapeDtypeStruct((rows, units), bf16)
    return pl.pallas_call(
        functools.partial(middle_kernel, rank),
        grid=(2, total // tile),
        out_shape=(block, block, block, jax.ShapeDtypeStruct((3 * rank, rows), bf16)),
        in_specs=[whole(rows, units)] * 3
        + [whole(rows, 3 * rank), whole(rows, 1), whole(*pat.shape)]
        + [down] * 3,
        out_specs=(whole(rows, units),) * 3 + (whole(3 * rank, rows),),
        scratch_shapes=[pltpu.VMEM((rows, units), f32)] * 3
        + [pltpu.VMEM((3 * rank, rows), f32)],
        compiler_params=pltpu.CompilerParams(vmem_limit_bytes=vmem_grant),
        cost_estimate=pl.CostEstimate(
            flops=12 * rows * total * units,
            bytes_accessed=12 * total * units,
            transcendentals=rows * units,
        ),
        name="middle_terms",
    )(gate, up, gh, coeffs, tenant, pat, bg, bu, ad)


def outputs_kernel(
    rank, hid, gg, gu, sums, slot, pat, gw, uw, dw, ag, au, bd, mixed_o, back_o, eq, eg, eu
):
    @pl.when(pl.program_id(0) == 0)
    def _():
        mask = slot[...] == lanes_entry(rank, 0, eq.shape[1])
        for k, (ref, scale) in enumerate(((eq, adapter_scale), (eg, 1.0), (eu, 1.0))):
            given = sums[:, k * rank : (k + 1) * rank]
            ref[...] = (
                scale * jnp.where(mask, dot(given, pat[...]), 0.0)
            ).astype(bf16)

    mixed_o[...] = (dot(hid[...], dw[...]) + dot(eq[...], bd[...])).astype(bf16)
    back_o[...] = (
        dot(gg[...], gw[...], ((1,), (1,)))
        + dot(gu[...], uw[...], ((1,), (1,)))
        + dot(eg[...], ag[...])
        + dot(eu[...], au[...])
    ).astype(bf16)


def output_terms(rank, hid, gg, gu, sums, slot, pat, gw, uw, dw, ag, au, bd):
    rows, units = hid.shape
    width, own = ag.shape[1], ag.shape[0]
    tile = min(512, width)
    across = lambda n: pl.BlockSpec((n, tile), lambda i: (0, i))
    down = lambda n: pl.BlockSpec((tile, n), lambda i: (i, 0))
    whole = lambda *shape: pl.BlockSpec(shape, lambda i: (0, 0))
    block = jax.ShapeDtypeStruct((rows, width), bf16)
    return pl.pallas_call(
        functools.partial(outputs_kernel, rank),
        grid=(width // tile,),
        out_shape=(block, block),
        in_specs=[whole(rows, units)] * 3
        + [whole(rows, 3 * rank), whole(rows, 1), whole(*pat.shape)]
        + [down(units), down(units), across(units), across(own), across(own), across(own)],
        out_specs=(across(rows), across(rows)),
        scratch_shapes=[pltpu.VMEM((rows, own), bf16)] * 3,
        compiler_params=pltpu.CompilerParams(vmem_limit_bytes=vmem_grant),
        cost_estimate=pl.CostEstimate(
            flops=6 * rows * width * (units + own),
            bytes_accessed=6 * width * (units + own),
            transcendentals=0,
        ),
        name="output_terms",
    )(hid, gg, gu, sums, slot, pat, gw, uw, dw, ag, au, bd)


def grads_kernel(rank, coeffs, owner, pat, *refs):
    count = len(refs) // 3
    values, outs, weights = refs[:count], refs[count : 2 * count], refs[2 * count :]

    @pl.when(pl.program_id(1) == 0)
    def _():
        entries = pat.shape[0]
        line = lax.broadcasted_iota(jnp.int32, (entries, 1), 0) // rank
        mask = line + pl.program_id(0) * (entries // rank) == owner[...]
        for k, ref in enumerate(weights):
            given = coeffs[:, k * rank : (k + 1) * rank]
            ref[...] = jnp.where(mask, dot(pat[...], given, ((1,), (1,))), 0.0).astype(bf16)

    for value, out, weight in zip(values, outs, weights):
        out[...] = dot(weight[...], value[...])


def outer_sums(rank, entries, coeffs, owner, values, columns, name):
    rows, width = values[0][0].shape[0], columns
    tall = min(256, entries * rank)
    tile = min(1024, width)
    pat = jnp.transpose(ranks_pattern(rank, tall // rank))
    whole = lambda *shape: pl.BlockSpec(shape, lambda i, j: (0, 0))
    out = jax.ShapeDtypeStruct((entries * rank, width), f32)
    found = pl.pallas_call(
        functools.partial(grads_kernel, rank),
        grid=(entries * rank // tall, width // tile),
        out_shape=(out,) * len(values),
        in_specs=[whole(rows, coeffs.shape[1]), whole(1, rows), whole(*pat.shape)]
        + [
            pl.BlockSpec((rows, tile), lambda i, j, at=start // tile: (0, at + j))
            for _, start in values
        ],
        out_specs=(pl.BlockSpec((tall, tile), lambda i, j: (i, j)),) * len(values),
        scratch_shapes=[pltpu.VMEM((tall, rows), bf16)] * len(values),
        compiler_params=pltpu.CompilerParams(vmem_limit_bytes=vmem_grant),
        name=name,
    )(coeffs, owner, pat, *[value for value, _ in values])
    return [part.reshape(entries, rank, width) for part in found]


def local(
    tokens,
    cotangent,
    gate_weight,
    up_weight,
    down_weight,
    a_gate,
    a_up,
    down_output_factors,
    b_gate,
    b_up,
    a_down,
    tenant_of_row,
    adapter_slot,
):
    own_rows, width = tokens.shape
    blocks = lax.axis_size("blk")
    grp_count = lax.axis_size("grp")
    blk_index = lax.axis_index("blk")
    grp_index = lax.axis_index("grp")
    per_owner, rank = a_gate.shape[:2]
    tenant_count, _, units = b_gate.shape
    capacity = 2 * own_rows
    group_rows = own_rows * blocks
    x, dy = gather_rows(blocks, tokens, cotangent)

    layout = tenant_of_row.reshape(blocks, grp_count, own_rows)
    all_tenants = jnp.transpose(layout, (1, 0, 2)).reshape(grp_count, group_rows)
    tenant_hot = all_tenants[:, :, None] == jnp.arange(tenant_count, dtype=jnp.int32)
    all_slots = jnp.sum(jnp.where(tenant_hot, adapter_slot, 0), axis=2)
    mine = all_slots // per_owner == blk_index
    order = jnp.arange(group_rows, dtype=jnp.int32)
    before = order[None, :] < order[:, None]
    within = jnp.sum((mine[:, None, :] & before[None]).astype(jnp.int32), axis=2)
    choose = mine[:, None, :] & (
        within[:, None, :] == jnp.arange(capacity, dtype=jnp.int32)[None, :, None]
    )
    choose_bf = choose.astype(bf16)
    picked_slot = (
        jnp.max(jnp.where(choose, all_slots[:, None, :], -1), axis=2).reshape(1, -1)
    )
    tenants = lax.dynamic_index_in_dim(all_tenants, grp_index, 0, keepdims=False)
    slots = lax.dynamic_index_in_dim(all_slots, grp_index, 0, keepdims=False)
    choose_own = lax.dynamic_index_in_dim(choose_bf, grp_index, 0, keepdims=False)

    local_slot = (slots - blk_index * per_owner)[:, None]
    slot_pattern = ranks_pattern(rank, per_owner)

    own_x = dot(choose_own, x).astype(bf16)
    own_dy = dot(choose_own, dy).astype(bf16)

    ag = a_gate.reshape(per_owner * rank, width)
    au = a_up.reshape(per_owner * rank, width)
    bd = down_output_factors.reshape(per_owner * rank, width)
    bg = b_gate.reshape(tenant_count * rank, units)
    bu = b_up.reshape(tenant_count * rank, units)
    ad = a_down.reshape(tenant_count * rank, units)

    gate_in, up_in, grad_in, low_in = input_terms(
        rank, x, dy, gate_weight, up_weight, down_weight, ag, au, bd, local_slot, slot_pattern
    )
    low_in, own_x, own_dy = lax.optimization_barrier((low_in, own_x, own_dy))
    all_x = lax.all_gather(own_x, "grp", axis=0, tiled=True)
    all_dy = lax.all_gather(own_dy, "grp", axis=0, tiled=True)
    twice = jnp.asarray(adapter_scale, bf16)
    coeffs = jnp.transpose(sum_over_blk(blocks, low_in, 1))
    hidden, grad_gate, grad_up, low_out = middle_terms(
        rank, gate_in, up_in, grad_in, coeffs, tenants[:, None], bg, bu, ad
    )
    sums = jnp.transpose(sum_over_blk(blocks, low_out, 2))

    packed = jnp.concatenate((hidden, grad_gate, grad_up, coeffs, sums), axis=1)
    spare = -packed.shape[1] % 128
    packed = jnp.pad(packed, ((0, 0), (0, spare)))
    everyone = lax.all_gather(packed, "grp", axis=0, tiled=True)

    mixed_terms, back_terms = output_terms(
        rank,
        hidden,
        grad_gate,
        grad_up,
        sums,
        local_slot,
        slot_pattern,
        gate_weight,
        up_weight,
        down_weight,
        ag,
        au,
        bd,
    )
    mixed, input_grad = scatter_rows(blocks, mixed_terms, back_terms)

    all_small = everyone[:, 3 * units : 3 * units + 6 * rank]
    picked = jnp.einsum(
        "gcn,gnk->gck",
        choose_bf,
        all_small[:, 3 * rank :].reshape(grp_count, group_rows, 3 * rank),
        preferred_element_type=f32,
    ).astype(bf16)
    picked = picked.reshape(grp_count * capacity, 3 * rank)
    slots_dev = per_owner // grp_count
    first_slot = blk_index * per_owner + grp_index * slots_dev
    picked = jnp.concatenate((twice * picked[:, :rank], picked[:, rank:]), axis=1)
    grad_bd, grad_ag, grad_au = outer_sums(
        rank,
        slots_dev,
        picked,
        picked_slot - first_slot,
        ((all_dy, 0), (all_x, 0), (all_x, 0)),
        width,
        "slot_grads",
    )
    tenant_dev = tenant_count // grp_count
    given = jnp.concatenate(
        (twice * all_small[:, : 2 * rank], all_small[:, 2 * rank : 3 * rank]), axis=1
    )
    grad_bg, grad_bu, grad_ad = outer_sums(
        rank,
        tenant_dev,
        given,
        all_tenants.reshape(1, -1) - grp_index * tenant_dev,
        ((everyone, units), (everyone, 2 * units), (everyone, 0)),
        units,
        "tenant_grads",
    )
    return (mixed, input_grad, grad_ag, grad_au, grad_bd, grad_bg, grad_bu, grad_ad)


def solution(mesh):
    placed = (
        P(("blk", "grp"), None),
        P(("blk", "grp"), None),
        P(None, "blk"),
        P(None, "blk"),
        P("blk", None),
        P("blk", None, None),
        P("blk", None, None),
        P("blk", None, None),
        P(None, None, "blk"),
        P(None, None, "blk"),
        P(None, None, "blk"),
        P(),
        P(),
    )
    return jax.shard_map(
        local,
        mesh=mesh,
        in_specs=placed,
        out_specs=(
            P(("blk", "grp"), None),
            P(("blk", "grp"), None),
            P(("blk", "grp"), None, None),
            P(("blk", "grp"), None, None),
            P(("blk", "grp"), None, None),
            P("grp", None, "blk"),
            P("grp", None, "blk"),
            P("grp", None, "blk"),
        ),
        check_vma=False,
    )
```

```python
import functools

import jax
import jax.numpy as jnp
from jax import lax
from jax.experimental import pallas as pl
from jax.experimental.pallas import tpu as pltpu
from jax.sharding import PartitionSpec as P

MESH = pl.DeviceIdType.MESH
bf16 = jnp.bfloat16
vmem_grant = 60 * 2**20
f32 = jnp.float32
slack = 2


def remote(src, dst, send, recv, to):
    return pltpu.make_async_remote_copy(
        src_ref=src,
        dst_ref=dst,
        send_sem=send,
        recv_sem=recv,
        device_id={"blk": to},
        device_id_type=MESH,
    )


def place(blocks):
    me = lax.axis_index("blk")
    line = blocks // 2
    row = me // 2
    col = me - 2 * row
    partner = me + 1 - 2 * col
    return me, line, row, col, partner


def gather_kernel(
    blocks,
    rank,
    chunks,
    x_ref,
    d_ref,
    gw,
    uw,
    dw,
    ag,
    au,
    bd,
    choose,
    slot,
    pat,
    gate_o,
    up_o,
    gh_o,
    low_o,
    ox_o,
    od_o,
    held,
    wide_g,
    wide_u,
    tall_a,
    tall_b,
    qa,
    qb,
    give,
    land,
    own_sem,
    w_sem,
    up_s,
    up_r,
    dn_s,
    dn_r,
    ac_s,
    ac_r,
    ex_s,
    ex_r,
    sum_s,
    sum_r,
):
    me, line, row, col, partner = place(blocks)
    above, below = me + 2, me - 2
    own_rows, width = x_ref.shape
    step_width = width // chunks
    total = 2 * chunks
    depth = wide_g.shape[0]
    rows = blocks * own_rows
    units, factors = dw.shape[0], bd.shape[0]

    def columns(j):
        return pl.ds(pl.multiple_of(lax.rem(j, chunks) * step_width, step_width), step_width)

    def part(block, j):
        return held.at[j // chunks, block, :, columns(j)]

    def up_copy(block, s, j):
        ref = part(block, j)
        return remote(ref, ref, up_s.at[s], up_r.at[s, j], above)

    def dn_copy(block, s, j):
        ref = part(block, j)
        return remote(ref, ref, dn_s.at[s], dn_r.at[s, j], below)

    def ac_copy(at, j):
        ref = part(2 * at + col, j)
        return remote(ref, ref, ac_s.at[at], ac_r.at[at, j], partner)

    def ac_arrival(at, j):
        ref = part(2 * at + 1 - col, j)
        return remote(ref, ref, ac_s.at[at], ac_r.at[at, j], partner)

    def ex_copy(direction, block, j, to):
        ref = part(block, j)
        return remote(ref, ref, ex_s.at[direction], ex_r.at[direction, j], to)

    def loads(j, a_phase):
        at, k = columns(j), lax.rem(j, depth)
        if a_phase:
            pairs = (
                (gw.at[at, :], wide_g.at[k]),
                (uw.at[at, :], wide_u.at[k]),
                (ag.at[:, at], tall_a.at[k, pl.ds(0, factors)]),
                (au.at[:, at], tall_b.at[k]),
            )
        else:
            pairs = ((dw.at[:, at], tall_a.at[k, pl.ds(0, units)]), (bd.at[:, at], tall_b.at[k]))
        return [
            pltpu.make_async_copy(src, dst, w_sem.at[i, k]) for i, (src, dst) in enumerate(pairs)
        ]

    def fetch(j):
        @pl.when(j < chunks)
        def _():
            for copy in loads(j, True):
                copy.start()

        @pl.when((j >= chunks) & (j < total))
        def _():
            for copy in loads(j, False):
                copy.start()

    own = [
        pltpu.make_async_copy(ref, held.at[c, me], own_sem.at[c])
        for c, ref in enumerate((x_ref, d_ref))
    ]
    for copy in own:
        copy.start()
    barrier = pltpu.get_barrier_semaphore()
    for k in range(1, blocks):
        pl.semaphore_signal(
            barrier, inc=1, device_id={"blk": lax.rem(me + k, blocks)}, device_id_type=MESH
        )
    for j in range(depth):
        fetch(j)
    for ref in (gate_o, up_o, gh_o, qa, qb):
        ref[...] = jnp.zeros_like(ref)
    for copy in own:
        copy.wait()
    pl.semaphore_wait(barrier, blocks - 1)

    def send_own(j):
        ac_copy(row, j).start()

        @pl.when(row < line - 1)
        def _():
            up_copy(me, 0, j).start()

        @pl.when(row > 0)
        def _():
            dn_copy(me, 0, j).start()

    def doubled(j):
        return lax.rem(j, 2) == 1

    def relay(s, j):
        crossing = lax.rem(j, 2) == 0 if s == 1 else j >= 0

        @pl.when(row >= s)
        def _():
            block = me - 2 * s
            up_copy(block, s - 1, j).wait_recv()
            if s < line - 1:

                @pl.when(row < line - 1)
                def _():
                    up_copy(block, s, j).start()

            @pl.when(crossing)
            def _():
                ac_copy(row - s, j).start()

        @pl.when(row + s < line)
        def _():
            block = me + 2 * s
            dn_copy(block, s - 1, j).wait_recv()
            if s < line - 1:

                @pl.when(row > 0)
                def _():
                    dn_copy(block, s, j).start()

            @pl.when(crossing)
            def _():
                ac_copy(row + s, j).start()

        if s == 1:
            ac_arrival(row, j).wait_recv()

            @pl.when(doubled(j))
            def _():
                @pl.when(row < line - 1)
                def _():
                    ex_copy(0, partner, j, above).start()

                @pl.when(row > 0)
                def _():
                    ex_copy(1, partner, j, below).start()

    def arrive(j):
        for s in range(1, line):
            crossing = lax.rem(j, 2) == 0 if s == 1 else j >= 0

            @pl.when(crossing & (row >= s))
            def _():
                ac_arrival(row - s, j).wait_recv()

            @pl.when(crossing & (row + s < line))
            def _():
                ac_arrival(row + s, j).wait_recv()

        @pl.when(doubled(j) & (row > 0))
        def _():
            ex_copy(0, partner - 2, j, above).wait_recv()

        @pl.when(doubled(j) & (row < line - 1))
        def _():
            ex_copy(1, partner + 2, j, below).wait_recv()

    def take(j):
        arrive(j)
        at, k = columns(j), lax.rem(j, depth)

        @pl.when(j < chunks)
        def _():
            for copy in loads(j, True):
                copy.wait()
            value = held[0, :, :, at].reshape(rows, step_width)
            gate_o[...] += dot(value, wide_g[k])
            up_o[...] += dot(value, wide_u[k])
            mine = dot(choose[...], value).astype(bf16)
            ox_o[:, at] = mine
            qa[...] += dot(mine, tall_a[k, :factors], ((1,), (1,)))
            qb[...] += dot(mine, tall_b[k], ((1,), (1,)))

        @pl.when(j >= chunks)
        def _():
            for copy in loads(j, False):
                copy.wait()
            value = held[1, :, :, at].reshape(rows, step_width)
            gh_o[...] += dot(value, tall_a[k, :units], ((1,), (1,)))
            mine = dot(choose[...], value).astype(bf16)
            od_o[:, at] = mine
            qb[...] += dot(mine, tall_b[k], ((1,), (1,)))

        fetch(j + depth)

    def pick(ref, scale):
        mask = slot[...] == lanes_entry(rank, 0, ref.shape[1])
        kept = jnp.where(mask, scale * ref[...], 0.0).astype(bf16)
        found = dot(pat[...], kept, ((1,), (1,))).astype(bf16)
        return dot(found, choose[...]).astype(bf16)

    def spread(first, count, c):
        copies = []
        for k in range(1, blocks):
            copy = remote(
                give.at[pl.ds(first, count)],
                land.at[k, pl.ds(first, count)],
                sum_s.at[c, k],
                sum_r.at[c, k],
                lax.rem(me + k, blocks),
            )
            copies.append(copy)
        return copies

    def step(t, carry):
        @pl.when(t < total)
        def _():
            send_own(t)

        for s in range(1, line):
            j = t - slack * s

            @pl.when((j >= 0) & (j < total))
            def _():
                relay(s, j)

        j = t - slack * line

        @pl.when(j >= 0)
        def _():
            take(j)

            @pl.when(j == chunks - 1)
            def _():
                give[:rank, :] = pick(qa, 1.0)
                give[rank : 2 * rank, :] = pick(qb, 1.0)
                for copy in spread(0, 2 * rank, 0):
                    copy.start()
                qb[...] = jnp.zeros_like(qb)

        return carry

    lax.fori_loop(0, total + slack * line, step, 0)
    give[2 * rank :, :] = pick(qb, adapter_scale)
    for copy in spread(2 * rank, rank, 1):
        copy.start()

    for c, (first, count) in enumerate(((0, 2 * rank), (2 * rank, rank))):
        acc = give[first : first + count, :].astype(f32)
        for k, copy in enumerate(spread(first, count, c)):
            copy.wait_recv()
            acc = acc + land[k + 1, first : first + count, :].astype(f32)
        low_o[first : first + count, :] = acc.astype(low_o.dtype)

    for c, (first, count) in enumerate(((0, 2 * rank), (2 * rank, rank))):
        for copy in spread(first, count, c):
            copy.wait_send()

    def sent(ref, sem):
        remote(ref, ref, sem, sum_r.at[0, 0], partner).wait_send()

    both, half = held.at[:, me], held.at[0, me]
    sent(both, ac_s.at[row])
    for s in range(1, line):
        for ok, at in ((row >= s, row - s), (row + s < line, row + s)):

            @pl.when(ok)
            def _():
                sent(half if s == 1 else both, ac_s.at[at])

    for s in range(line - 1):

        @pl.when((row >= s) & (row < line - 1))
        def _():
            sent(both, up_s.at[s])

        @pl.when((row + s < line) & (row > 0))
        def _():
            sent(both, dn_s.at[s])

    @pl.when(row < line - 1)
    def _():
        sent(half, ex_s.at[0])

    @pl.when(row > 0)
    def _():
        sent(half, ex_s.at[1])


def gather_terms(blocks, rank, x, dy, gw, uw, dw, ag, au, bd, choose, slot, pat):
    line = blocks // 2
    own_rows, width = x.shape
    units, factors = gw.shape[1], ag.shape[0]
    rows, own = blocks * own_rows, choose.shape[0]
    chunks = 8
    step_width = width // chunks
    depth = 3
    dma = pltpu.SemaphoreType.DMA
    vmem = pltpu.VMEM
    acc = jax.ShapeDtypeStruct((rows, units), f32)
    picked = jax.ShapeDtypeStruct((own, width), bf16)
    anywhere, inside = pl.BlockSpec(memory_space=pl.ANY), pl.BlockSpec(memory_space=vmem)
    return pl.pallas_call(
        functools.partial(gather_kernel, blocks, rank, chunks),
        out_shape=(acc, acc, acc, jax.ShapeDtypeStruct((3 * rank, rows), bf16), picked, picked),
        in_specs=[anywhere] * 8 + [inside] * 3,
        out_specs=(inside,) * 6,
        scratch_shapes=[
            vmem((2, blocks, own_rows, width), bf16),
            vmem((depth, step_width, units), bf16),
            vmem((depth, step_width, units), bf16),
            vmem((depth, max(units, factors), step_width), bf16),
            vmem((depth, factors, step_width), bf16),
            vmem((own, factors), f32),
            vmem((own, factors), f32),
            vmem((3 * rank, rows), bf16),
            vmem((blocks, 3 * rank, rows), bf16),
            dma((2,)),
            dma((4, depth)),
            dma((line,)),
            dma((line, 2 * chunks)),
            dma((line,)),
            dma((line, 2 * chunks)),
            dma((line,)),
            dma((line, 2 * chunks)),
            dma((2,)),
            dma((2, 2 * chunks)),
            dma((2, blocks)),
            dma((2, blocks)),
        ],
        compiler_params=pltpu.CompilerParams(
            collective_id=0, has_side_effects=True, vmem_limit_bytes=vmem_grant
        ),
        cost_estimate=pl.CostEstimate(
            flops=6 * rows * width * (units + factors),
            bytes_accessed=6 * width * (units + factors),
            transcendentals=0,
        ),
        name="gather_terms",
    )(x, dy, gw, uw, dw, ag, au, bd, choose, slot, pat)


def scatter_kernel(
    blocks,
    groups,
    rank,
    chunks,
    mid,
    small,
    slot,
    pat,
    ox,
    od,
    gw,
    uw,
    dw,
    ag,
    au,
    bd,
    out,
    all_x,
    all_d,
    all_mid,
    all_small,
    terms,
    pair_buf,
    line_buf,
    top_buf,
    ex_buf,
    cross_buf,
    acc,
    extra,
    wide_g,
    wide_u,
    tall_a,
    tall_b,
    w_sem,
    own_sem,
    ac_s,
    ac_r,
    up_s,
    up_r,
    dn_s,
    dn_r,
    ex_s,
    ex_r,
    gc_s,
    gc_r,
    gy_s,
    gy_r,
    gr_s,
    gr_r,
):
    me, line, row, col, partner = place(blocks)
    above, below = me + 2, me - 2
    _, own_rows, width = out.shape
    step_width = width // chunks
    total = 2 * chunks
    depth = wide_g.shape[0]
    rows = blocks * own_rows
    units, factors = dw.shape[0], bd.shape[0]
    group = lax.axis_index("grp")
    pairs_g, high = groups // 2, group // 2
    low = group - 2 * high
    twin = group + 1 - 2 * low

    def columns(j):
        return pl.ds(pl.multiple_of(lax.rem(j, chunks) * step_width, step_width), step_width)

    def loads(j, back):
        at, k = columns(j), lax.rem(j, depth)
        if back:
            moves = (
                (ag.at[:, at], tall_a.at[k, pl.ds(0, factors)]),
                (au.at[:, at], tall_b.at[k]),
                (gw.at[at, :], wide_g.at[k]),
                (uw.at[at, :], wide_u.at[k]),
            )
        else:
            moves = (
                (dw.at[:, at], tall_a.at[k, pl.ds(0, units)]),
                (bd.at[:, at], tall_b.at[k]),
            )
        return [
            pltpu.make_async_copy(src, dst, w_sem.at[i, k]) for i, (src, dst) in enumerate(moves)
        ]

    def fetch(j):
        @pl.when(j < chunks)
        def _():
            for copy in loads(j, False):
                copy.start()

        @pl.when((j >= chunks) & (j < total))
        def _():
            for copy in loads(j, True):
                copy.start()

    for j in range(depth):
        fetch(j)

    pieces = ((small, all_small), (mid, all_mid), (ox, all_x), (od, all_d))
    own = [
        pltpu.make_async_copy(src, dst.at[group], own_sem.at[i])
        for i, (src, dst) in enumerate(pieces)
    ]
    for copy in own:
        copy.start()

    def to_group(src, dst, send, recv, to):
        return pltpu.make_async_remote_copy(
            src_ref=src,
            dst_ref=dst,
            send_sem=send,
            recv_sem=recv,
            device_id={"grp": to},
            device_id_type=MESH,
        )

    def twin_copy(i):
        src, dst = pieces[i]
        return to_group(src, dst.at[group], gc_s.at[i], gc_r.at[i], twin)

    def far_copy(i, k):
        src, dst = pieces[i]
        to = 2 * lax.rem(high + k, pairs_g) + low
        return to_group(src, dst.at[group], gy_s.at[i, k], gy_r.at[i, k], to)

    def hand_on(i, k):
        ref = pieces[i][1].at[2 * lax.rem(high + pairs_g - k, pairs_g) + low]
        return to_group(ref, ref, gr_s.at[i, k], gr_r.at[i, k], twin)

    barrier = pltpu.get_barrier_semaphore()
    pl.semaphore_signal(barrier, inc=1, device_id={"grp": twin}, device_id_type=MESH)
    for k in range(1, pairs_g):
        to = 2 * lax.rem(high + k, pairs_g) + low
        pl.semaphore_signal(barrier, inc=1, device_id={"grp": to}, device_id_type=MESH)
    pl.semaphore_signal(barrier, inc=1, device_id={"blk": partner}, device_id_type=MESH)

    @pl.when(row < line - 1)
    def _():
        pl.semaphore_signal(barrier, inc=1, device_id={"blk": above}, device_id_type=MESH)

    @pl.when(row > 0)
    def _():
        pl.semaphore_signal(barrier, inc=1, device_id={"blk": below}, device_id_type=MESH)

    peers = 1 + (row < line - 1).astype(jnp.int32) + (row > 0).astype(jnp.int32)

    mask = slot[...] == lanes_entry(rank, 0, factors)
    same = lax.broadcasted_iota(jnp.int32, (rows, rows), 0) == lax.broadcasted_iota(
        jnp.int32, (rows, rows), 1
    )
    sums = dot(same.astype(bf16), small[3 * rank :, :], ((1,), (1,))).astype(bf16)
    for k, scale in enumerate((adapter_scale, 1.0, 1.0)):
        given = sums[:, k * rank : (k + 1) * rank]
        extra[k] = (scale * jnp.where(mask, dot(given, pat[...]), 0.0)).astype(bf16)
    pl.semaphore_wait(barrier, peers + pairs_g)
    for i in range(len(pieces)):
        twin_copy(i).start()
        for k in range(1, pairs_g):
            far_copy(i, k).start()

    def part(block, j):
        return terms.at[j // chunks, block, :, columns(j)]

    def piece(buf, at, j):
        return buf.at[j // chunks, at, :, columns(j)]

    def ac_copy(src, at, j):
        return remote(src, piece(pair_buf, at, j), ac_s.at[at], ac_r.at[at, j], partner)

    def up_copy(at, j):
        return remote(
            piece(pair_buf, at, j), piece(line_buf, at, j), up_s.at[at], up_r.at[at, j], above
        )

    def dn_copy(at, j, landing):
        return remote(piece(pair_buf, at, j), landing, dn_s.at[at], dn_r.at[at, j], below)

    def ex_copy(direction, block, j, to):
        return remote(
            part(block, j),
            piece(ex_buf, direction, j),
            ex_s.at[direction],
            ex_r.at[direction, j],
            to,
        )

    def top(j):
        return top_buf.at[j // chunks, :, columns(j)]

    def cross(j):
        return cross_buf.at[j // chunks, :, columns(j)]

    def doubled(j):
        return lax.rem(j, 2) == 1

    def plain(s, j):
        return lax.rem(j, 2) == 0 if s == 1 else j >= 0

    def make(j):
        at, k = columns(j), lax.rem(j, depth)

        @pl.when(j < chunks)
        def _():
            for copy in loads(j, False):
                copy.wait()
            value = dot(mid[0], tall_a[k, :units]) + dot(extra[0], tall_b[k])
            terms[0, :, :, at] = value.astype(bf16).reshape(blocks, own_rows, step_width)

        @pl.when(j >= chunks)
        def _():
            for copy in loads(j, True):
                copy.wait()
            value = (
                dot(mid[1], wide_g[k], ((1,), (1,)))
                + dot(mid[2], wide_u[k], ((1,), (1,)))
                + dot(extra[1], tall_a[k, :factors])
                + dot(extra[2], tall_b[k])
            )
            terms[1, :, :, at] = value.astype(bf16).reshape(blocks, own_rows, step_width)

        for s in range(line - 1, 0, -1):
            for ok, to in ((row + s < line, row + s), (row >= s, row - s)):

                @pl.when(ok & plain(s, j))
                def _():
                    ac_copy(part(2 * to + 1 - col, j), to, j).start()

        @pl.when(doubled(j))
        def _():
            @pl.when(row < line - 1)
            def _():
                ex_copy(0, partner + 2, j, above).start()

            @pl.when(row > 0)
            def _():
                ex_copy(1, partner - 2, j, below).start()

        @pl.when(lax.rem(j, 2) == 0)
        def _():
            ac_copy(part(partner, j), row, j).start()

        fetch(j + depth)

    def cross_over(j):
        @pl.when(doubled(j))
        def _():
            acc[...] = part(partner, j)[...].astype(f32)

            @pl.when(row > 0)
            def _():
                ex_copy(0, partner, j, above).wait_recv()
                acc[...] += piece(ex_buf, 0, j)[...].astype(f32)

            @pl.when(row < line - 1)
            def _():
                ex_copy(1, partner, j, below).wait_recv()
                acc[...] += piece(ex_buf, 1, j)[...].astype(f32)

            cross(j)[...] = acc[...].astype(bf16)
            ac_copy(cross(j), row, j).start()

    def pair_up(s, at, j):
        mine = part(2 * at + col, j)
        acc[...] = mine[...].astype(f32)

        @pl.when(plain(s, j))
        def _():
            ac_copy(mine, at, j).wait_recv()
            acc[...] += piece(pair_buf, at, j)[...].astype(f32)

    def relay(s, j):
        @pl.when(row + s < line)
        def _():
            at = row + s
            pair_up(s, at, j)
            if s < line - 1:

                @pl.when(row > 0)
                def _():
                    up_copy(at, j).wait_recv()
                    acc[...] += piece(line_buf, at, j)[...].astype(f32)

            piece(pair_buf, at, j)[...] = acc[...].astype(bf16)
            up_copy(at, j).start()

        @pl.when(row >= s)
        def _():
            at = row - s
            landing = top(j) if s == 1 else piece(line_buf, at, j)
            pair_up(s, at, j)
            if s < line - 1:

                @pl.when(row < line - 1)
                def _():
                    dn_copy(at, j, landing).wait_recv()
                    acc[...] += piece(line_buf, at, j)[...].astype(f32)

            piece(pair_buf, at, j)[...] = acc[...].astype(bf16)
            dn_copy(at, j, landing).start()

    def finish(j):
        mine = part(me, j)
        ac_copy(mine, row, j).wait_recv()
        acc[...] = mine[...].astype(f32) + piece(pair_buf, row, j)[...].astype(f32)

        @pl.when(row > 0)
        def _():
            up_copy(row, j).wait_recv()
            acc[...] += piece(line_buf, row, j)[...].astype(f32)

        @pl.when(row < line - 1)
        def _():
            dn_copy(row, j, top(j)).wait_recv()
            acc[...] += top(j)[...].astype(f32)

        out[j // chunks, :, columns(j)] = acc[...].astype(bf16)

    def step(t, carry):
        @pl.when(t < total)
        def _():
            make(t)

        j = t - slack

        @pl.when((j >= 0) & (j < total))
        def _():
            cross_over(j)

        for s in range(line - 1, 0, -1):
            j = t - slack * (line - s)

            @pl.when((j >= 0) & (j < total))
            def _():
                relay(s, j)

        j = t - slack * line

        @pl.when(j >= 0)
        def _():
            finish(j)

        for i in range(len(pieces)):

            @pl.when(t == (i * total) // (len(pieces) - 1) + slack)
            def _():
                for k in range(1, pairs_g):
                    far_copy(i, k).wait_recv()
                    hand_on(i, k).start()

        return carry

    lax.fori_loop(0, total + slack * line, step, 0)

    for i in range(len(pieces)):
        own[i].wait()
        twin_copy(i).wait()
        for k in range(1, pairs_g):
            far_copy(i, k).wait_send()
            hand_on(i, k).wait()

    def sent(ref, sem):
        remote(ref, ref, sem, ac_r.at[0, 0], partner).wait_send()

    both, half = terms.at[:, me], terms.at[0, me]
    sent(both, ac_s.at[row])
    for s in range(1, line):

        @pl.when(row + s < line)
        def _():
            sent(half if s == 1 else both, ac_s.at[row + s])
            sent(both, up_s.at[row + s])

        @pl.when(row >= s)
        def _():
            sent(half if s == 1 else both, ac_s.at[row - s])
            sent(both, dn_s.at[row - s])

    @pl.when(row < line - 1)
    def _():
        sent(half, ex_s.at[0])

    @pl.when(row > 0)
    def _():
        sent(half, ex_s.at[1])


def scatter_terms(blocks, groups, rank, mid, small, slot, pat, ox, od, gw, uw, dw, ag, au, bd):
    line = blocks // 2
    _, rows, units = mid.shape
    width, factors = ag.shape[1], ag.shape[0]
    own_rows = rows // blocks
    chunks = 8
    step_width = width // chunks
    depth = 3
    dma = pltpu.SemaphoreType.DMA
    vmem = pltpu.VMEM
    anywhere, inside = pl.BlockSpec(memory_space=pl.ANY), pl.BlockSpec(memory_space=vmem)
    whole = lambda value: jax.ShapeDtypeStruct((groups,) + value.shape, value.dtype)
    return pl.pallas_call(
        functools.partial(scatter_kernel, blocks, groups, rank, chunks),
        out_shape=(
            jax.ShapeDtypeStruct((2, own_rows, width), bf16),
            whole(ox),
            whole(od),
            whole(mid),
            whole(small),
        ),
        in_specs=[inside] * 4 + [anywhere] * 8,
        out_specs=(inside,) + (anywhere,) * 4,
        scratch_shapes=[
            vmem((2, blocks, own_rows, width), bf16),
            vmem((2, line, own_rows, width), bf16),
            vmem((2, line, own_rows, width), bf16),
            vmem((2, own_rows, width), bf16),
            vmem((2, 2, own_rows, width), bf16),
            vmem((2, own_rows, width), bf16),
            vmem((own_rows, step_width), f32),
            vmem((3, rows, factors), bf16),
            vmem((depth, step_width, units), bf16),
            vmem((depth, step_width, units), bf16),
            vmem((depth, max(units, factors), step_width), bf16),
            vmem((depth, factors, step_width), bf16),
            dma((4, depth)),
            dma((4,)),
            dma((line,)),
            dma((line, 2 * chunks)),
            dma((line,)),
            dma((line, 2 * chunks)),
            dma((line,)),
            dma((line, 2 * chunks)),
            dma((2,)),
            dma((2, 2 * chunks)),
            dma((4,)),
            dma((4,)),
            dma((4, groups // 2)),
            dma((4, groups // 2)),
            dma((4, groups // 2)),
            dma((4, groups // 2)),
        ],
        compiler_params=pltpu.CompilerParams(
            collective_id=3, has_side_effects=True, vmem_limit_bytes=vmem_grant
        ),
        cost_estimate=pl.CostEstimate(
            flops=6 * rows * width * (units + factors),
            bytes_accessed=6 * width * (units + factors),
            transcendentals=0,
        ),
        name="scatter_terms",
    )(mid, small, slot, pat, ox, od, gw, uw, dw, ag, au, bd)


def sum_kernel(blocks, c_ref, o_ref, land, send_sem, recv_sem):
    me = lax.axis_index("blk")
    barrier = pltpu.get_barrier_semaphore()
    for k in range(1, blocks):
        pl.semaphore_signal(
            barrier, inc=1, device_id={"blk": lax.rem(me + k, blocks)}, device_id_type=MESH
        )
    pl.semaphore_wait(barrier, blocks - 1)
    copies = []
    for k in range(1, blocks):
        copy = remote(
            c_ref, land.at[k], send_sem.at[k], recv_sem.at[k], lax.rem(me + k, blocks)
        )
        copy.start()
        copies.append(copy)
    acc = c_ref[...].astype(f32)
    for k in range(1, blocks):
        copies[k - 1].wait_recv()
        acc = acc + land[k].astype(f32)
    o_ref[...] = acc.astype(o_ref.dtype)
    for copy in copies:
        copy.wait_send()


def sum_over_blk(blocks, coeffs, collective_id):
    dma = pltpu.SemaphoreType.DMA
    return pl.pallas_call(
        functools.partial(sum_kernel, blocks),
        out_shape=jax.ShapeDtypeStruct(coeffs.shape, coeffs.dtype),
        in_specs=[pl.BlockSpec(memory_space=pltpu.VMEM)],
        out_specs=pl.BlockSpec(memory_space=pltpu.VMEM),
        scratch_shapes=[
            pltpu.VMEM((blocks,) + coeffs.shape, coeffs.dtype),
            dma((blocks,)),
            dma((blocks,)),
        ],
        compiler_params=pltpu.CompilerParams(
            collective_id=collective_id, has_side_effects=True, vmem_limit_bytes=8 * 2**20
        ),
        name="sum_over_blk",
    )(coeffs)


adapter_scale = 2.0


def silu_pair(gate_in):
    sigmoid_val = jax.nn.sigmoid(gate_in)
    return (gate_in * sigmoid_val, sigmoid_val * (1.0 + gate_in * (1.0 - sigmoid_val)))


def dot(a, b, dims=((1,), (0,))):
    return lax.dot_general(a, b, (dims, ((), ())), preferred_element_type=f32)


def ranks_pattern(rank, entries):
    column = lax.broadcasted_iota(jnp.int32, (rank, entries * rank), 1)
    row = lax.broadcasted_iota(jnp.int32, (rank, entries * rank), 0)
    return (column % rank == row).astype(bf16)


def lanes_entry(rank, first, count):
    return (lax.broadcasted_iota(jnp.int32, (1, count), 1) // rank) + first


def spread_kernel(coeffs, mask, pattern):
    return jnp.where(mask, dot(coeffs, pattern), 0.0).astype(bf16)


def select_kernel(full, mask, pattern):
    kept = jnp.where(mask, full, 0.0).astype(bf16)
    return dot(pattern, kept, ((1,), (1,)))


def middle_kernel(
    rank, gate, up, gh, coeffs, tenant, pat, bg, bu, ad, hid_o, gg_o, gu_o, low_o, sg, su, sh, low
):
    half, step = pl.program_id(0), pl.program_id(1)
    last = pl.num_programs(1) - 1
    count = bg.shape[0]
    mask = tenant[...] == lanes_entry(rank, step * (count // rank), count)

    @pl.when((half == 0) & (step == 0))
    def _():
        sg[...] = gate[...]
        su[...] = up[...]
        sh[...] = gh[...]

    @pl.when(half == 0)
    def _():
        for k, (acc, fac, scale) in enumerate(
            ((sg, bg, adapter_scale), (su, bu, adapter_scale), (sh, ad, 1.0))
        ):
            given = coeffs[:, k * rank : (k + 1) * rank]
            acc[...] += scale * dot(spread_kernel(given, mask, pat[...]), fac[...])

    @pl.when((half == 0) & (step == last))
    def _():
        act_val, act_slope = silu_pair(sg[...])
        up_val, grad_h = su[...], sh[...]
        hid_o[...] = (act_val * up_val).astype(bf16)
        gg_o[...] = (grad_h * up_val * act_slope).astype(bf16)
        gu_o[...] = (grad_h * act_val).astype(bf16)
        low[...] = jnp.zeros_like(low)

    @pl.when(half == 1)
    def _():
        for k, (rows, fac, scale) in enumerate(
            ((hid_o, ad, 1.0), (gg_o, bg, adapter_scale), (gu_o, bu, adapter_scale))
        ):
            full = dot(rows[...], fac[...], ((1,), (1,)))
            low[k * rank : (k + 1) * rank, :] += scale * select_kernel(full, mask, pat[...])

    @pl.when((half == 1) & (step == last))
    def _():
        low_o[...] = low[...].astype(bf16)


def middle_terms(rank, gate, up, gh, coeffs, tenant, bg, bu, ad):
    rows, units = gate.shape
    total = bg.shape[0]
    tile = min(1024, total)
    pat = ranks_pattern(rank, tile // rank)
    whole = lambda *shape: pl.BlockSpec(shape, lambda h, i: (0, 0))
    down = pl.BlockSpec((tile, units), lambda h, i: (i, 0))
    block = jax.ShapeDtypeStruct((rows, units), bf16)
    return pl.pallas_call(
        functools.partial(middle_kernel, rank),
        grid=(2, total // tile),
        out_shape=(block, block, block, jax.ShapeDtypeStruct((3 * rank, rows), bf16)),
        in_specs=[whole(rows, units)] * 3
        + [whole(rows, 3 * rank), whole(rows, 1), whole(*pat.shape)]
        + [down] * 3,
        out_specs=(whole(rows, units),) * 3 + (whole(3 * rank, rows),),
        scratch_shapes=[pltpu.VMEM((rows, units), f32)] * 3
        + [pltpu.VMEM((3 * rank, rows), f32)],
        compiler_params=pltpu.CompilerParams(vmem_limit_bytes=vmem_grant),
        cost_estimate=pl.CostEstimate(
            flops=12 * rows * total * units,
            bytes_accessed=12 * total * units,
            transcendentals=rows * units,
        ),
        name="middle_terms",
    )(gate, up, gh, coeffs, tenant, pat, bg, bu, ad)


def grads_kernel(rank, coeffs, owner, pat, *refs):
    count = len(refs) // 3
    values, outs, weights = refs[:count], refs[count : 2 * count], refs[2 * count :]

    @pl.when(pl.program_id(1) == 0)
    def _():
        entries = pat.shape[0]
        line = lax.broadcasted_iota(jnp.int32, (entries, 1), 0) // rank
        mask = line + pl.program_id(0) * (entries // rank) == owner[...]
        for k, ref in enumerate(weights):
            given = coeffs[:, k * rank : (k + 1) * rank]
            ref[...] = jnp.where(mask, dot(pat[...], given, ((1,), (1,))), 0.0).astype(bf16)

    for value, out, weight in zip(values, outs, weights):
        out[...] = dot(weight[...], value[...])


def outer_sums(rank, entries, coeffs, owner, values, columns, name):
    rows, width = values[0][0].shape[0], columns
    tall = min(256, entries * rank)
    tile = min(1024, width)
    pat = jnp.transpose(ranks_pattern(rank, tall // rank))
    whole = lambda *shape: pl.BlockSpec(shape, lambda i, j: (0, 0))
    out = jax.ShapeDtypeStruct((entries * rank, width), f32)
    found = pl.pallas_call(
        functools.partial(grads_kernel, rank),
        grid=(entries * rank // tall, width // tile),
        out_shape=(out,) * len(values),
        in_specs=[whole(rows, coeffs.shape[1]), whole(1, rows), whole(*pat.shape)]
        + [
            pl.BlockSpec((rows, tile), lambda i, j, at=start // tile: (0, at + j))
            for _, start in values
        ],
        out_specs=(pl.BlockSpec((tall, tile), lambda i, j: (i, j)),) * len(values),
        scratch_shapes=[pltpu.VMEM((tall, rows), bf16)] * len(values),
        compiler_params=pltpu.CompilerParams(vmem_limit_bytes=vmem_grant),
        name=name,
    )(coeffs, owner, pat, *[value for value, _ in values])
    return [part.reshape(entries, rank, width) for part in found]


def local(
    tokens,
    cotangent,
    gate_weight,
    up_weight,
    down_weight,
    a_gate,
    a_up,
    down_output_factors,
    b_gate,
    b_up,
    a_down,
    tenant_of_row,
    adapter_slot,
):
    own_rows, width = tokens.shape
    blocks = lax.axis_size("blk")
    grp_count = lax.axis_size("grp")
    blk_index = lax.axis_index("blk")
    grp_index = lax.axis_index("grp")
    per_owner, rank = a_gate.shape[:2]
    tenant_count, _, units = b_gate.shape
    capacity = 2 * own_rows
    group_rows = own_rows * blocks
    layout = tenant_of_row.reshape(blocks, grp_count, own_rows)
    all_tenants = jnp.transpose(layout, (1, 0, 2)).reshape(grp_count, group_rows)
    tenant_hot = all_tenants[:, :, None] == jnp.arange(tenant_count, dtype=jnp.int32)
    all_slots = jnp.sum(jnp.where(tenant_hot, adapter_slot, 0), axis=2)
    mine = all_slots // per_owner == blk_index
    order = jnp.arange(group_rows, dtype=jnp.int32)
    before = order[None, :] < order[:, None]
    within = jnp.sum((mine[:, None, :] & before[None]).astype(jnp.int32), axis=2)
    choose = mine[:, None, :] & (
        within[:, None, :] == jnp.arange(capacity, dtype=jnp.int32)[None, :, None]
    )
    choose_bf = choose.astype(bf16)
    picked_slot = jnp.max(jnp.where(choose, all_slots[:, None, :], -1), axis=2)
    tenants = lax.dynamic_index_in_dim(all_tenants, grp_index, 0, keepdims=False)
    slots = lax.dynamic_index_in_dim(all_slots, grp_index, 0, keepdims=False)
    choose_own = lax.dynamic_index_in_dim(choose_bf, grp_index, 0, keepdims=False)

    local_slot = (slots - blk_index * per_owner)[:, None]
    slot_pattern = ranks_pattern(rank, per_owner)

    own_slot = lax.dynamic_index_in_dim(picked_slot, grp_index, 0, keepdims=False)
    own_slot = (own_slot - blk_index * per_owner)[:, None]

    ag = a_gate.reshape(per_owner * rank, width)
    au = a_up.reshape(per_owner * rank, width)
    bd = down_output_factors.reshape(per_owner * rank, width)
    bg = b_gate.reshape(tenant_count * rank, units)
    bu = b_up.reshape(tenant_count * rank, units)
    ad = a_down.reshape(tenant_count * rank, units)

    gate_in, up_in, grad_in, low_in, own_x, own_dy = gather_terms(
        blocks,
        rank,
        tokens,
        cotangent,
        gate_weight,
        up_weight,
        down_weight,
        ag,
        au,
        bd,
        choose_own,
        own_slot,
        slot_pattern,
    )
    twice = jnp.asarray(adapter_scale, bf16)
    coeffs = jnp.transpose(low_in)
    hidden, grad_gate, grad_up, low_out = middle_terms(
        rank, gate_in, up_in, grad_in, coeffs, tenants[:, None], bg, bu, ad
    )
    low_out = sum_over_blk(blocks, low_out, 2)
    result, all_x, all_dy, all_mid, all_small = scatter_terms(
        blocks,
        grp_count,
        rank,
        jnp.stack((hidden, grad_gate, grad_up)),
        jnp.concatenate((low_in, low_out)),
        local_slot,
        slot_pattern,
        own_x,
        own_dy,
        gate_weight,
        up_weight,
        down_weight,
        ag,
        au,
        bd,
    )
    mixed, input_grad = result[0], result[1]
    all_x, all_dy = all_x.reshape(-1, width), all_dy.reshape(-1, width)
    all_small = jnp.transpose(all_small, (0, 2, 1))
    everyone = [all_mid[:, k].reshape(-1, units) for k in range(3)]
    picked = jnp.einsum(
        "gcn,gnk->gck",
        choose_bf,
        all_small[:, :, 3 * rank :],
        preferred_element_type=f32,
    ).astype(bf16)
    all_small = all_small.reshape(-1, 6 * rank)
    picked = picked.reshape(grp_count * capacity, 3 * rank)
    slots_dev = per_owner // grp_count
    first_slot = blk_index * per_owner + grp_index * slots_dev
    picked = jnp.concatenate((twice * picked[:, :rank], picked[:, rank:]), axis=1)
    grad_bd, grad_ag, grad_au = outer_sums(
        rank,
        slots_dev,
        picked,
        picked_slot.reshape(1, -1) - first_slot,
        ((all_dy, 0), (all_x, 0), (all_x, 0)),
        width,
        "slot_grads",
    )
    tenant_dev = tenant_count // grp_count
    given = jnp.concatenate(
        (twice * all_small[:, : 2 * rank], all_small[:, 2 * rank : 3 * rank]), axis=1
    )
    grad_bg, grad_bu, grad_ad = outer_sums(
        rank,
        tenant_dev,
        given,
        all_tenants.reshape(1, -1) - grp_index * tenant_dev,
        ((everyone[1], 0), (everyone[2], 0), (everyone[0], 0)),
        units,
        "tenant_grads",
    )
    return (mixed, input_grad, grad_ag, grad_au, grad_bd, grad_bg, grad_bu, grad_ad)


def solution(mesh):
    placed = (
        P(("blk", "grp"), None),
        P(("blk", "grp"), None),
        P(None, "blk"),
        P(None, "blk"),
        P("blk", None),
        P("blk", None, None),
        P("blk", None, None),
        P("blk", None, None),
        P(None, None, "blk"),
        P(None, None, "blk"),
        P(None, None, "blk"),
        P(),
        P(),
    )
    return jax.shard_map(
        local,
        mesh=mesh,
        in_specs=placed,
        out_specs=(
            P(("blk", "grp"), None),
            P(("blk", "grp"), None),
            P(("blk", "grp"), None, None),
            P(("blk", "grp"), None, None),
            P(("blk", "grp"), None, None),
            P("grp", None, "blk"),
            P("grp", None, "blk"),
            P("grp", None, "blk"),
        ),
        check_vma=False,
    )
```

```python
import functools

import jax
import jax.numpy as jnp
from jax import lax
from jax.experimental import pallas as pl
from jax.experimental.pallas import tpu as pltpu
from jax.sharding import PartitionSpec as P

MESH = pl.DeviceIdType.MESH
bf16 = jnp.bfloat16
vmem_grant = 60 * 2**20
f32 = jnp.float32
slack = 2


def remote(src, dst, send, recv, to):
    return pltpu.make_async_remote_copy(
        src_ref=src,
        dst_ref=dst,
        send_sem=send,
        recv_sem=recv,
        device_id={"blk": to},
        device_id_type=MESH,
    )


def place(blocks):
    me = lax.axis_index("blk")
    line = blocks // 2
    row = me // 2
    col = me - 2 * row
    partner = me + 1 - 2 * col
    return me, line, row, col, partner


adapter_scale = 2.0


def silu_pair(gate_in):
    sigmoid_val = jax.nn.sigmoid(gate_in)
    return (gate_in * sigmoid_val, sigmoid_val * (1.0 + gate_in * (1.0 - sigmoid_val)))


def dot(a, b, dims=((1,), (0,))):
    return lax.dot_general(a, b, (dims, ((), ())), preferred_element_type=f32)


across = ((1,), (1,))


def line_of(shape, axis):
    return lax.broadcasted_iota(jnp.int32, shape, axis)


def window_kernel(
    blocks,
    groups,
    rank,
    chunks,
    x_ref,
    d_ref,
    gw,
    uw,
    dw,
    ag,
    au,
    bd,
    bg,
    bu,
    ad,
    tenant_row,
    slot_row,
    out,
    all_x,
    all_d,
    all_h,
    all_g,
    all_u,
    all_small,
    held,
    pair_buf,
    line_buf,
    top_buf,
    ex_buf,
    cross_buf,
    acc,
    gate,
    up,
    gh,
    qa,
    qb,
    own_x,
    own_d,
    hid,
    gg,
    gu,
    extra,
    wide_g,
    wide_u,
    tall_a,
    tall_b,
    fac_g,
    fac_u,
    fac_d,
    pat,
    choose,
    own_slot,
    tenant_col,
    slot_col,
    give,
    land,
    sums,
    low,
    coef,
    small,
    own_sem,
    w_sem,
    f_sem,
    g_sems,
    r_sems,
    s_sems,
    t_sems,
    x_sems,
    y_sems,
    sum_s,
    sum_r,
    e_sems,
    v_sems,
):
    me, line, row, col, partner = place(blocks)
    above, below = me + 2, me - 2
    own_rows, width = x_ref.shape
    rows = blocks * own_rows
    step_width = width // chunks
    total = 2 * chunks
    depth = wide_g.shape[0]
    units, factors = dw.shape[0], bd.shape[0]
    count = bg.shape[0]
    tile = pat.shape[1]
    tiles = count // tile
    picks = choose.shape[0]
    group = lax.axis_index("grp")
    pairs_g, high = groups // 2, group // 2
    odd = group - 2 * high
    twin = group + 1 - 2 * odd
    filled = slack * line
    x_end = chunks - 1 + filled
    d_end = total - 1 + filled
    begin = d_end + 1
    finish_step = begin + total + filled

    up_s, up_r, dn_s, dn_r = g_sems.at[0], r_sems.at[0], g_sems.at[1], r_sems.at[1]
    ac_s, ac_r = g_sems.at[2], r_sems.at[2]
    ex_s, ex_r = x_sems.at[0], y_sems.at[0]
    bup_s, bup_r, bdn_s, bdn_r = s_sems.at[0], t_sems.at[0], s_sems.at[1], t_sems.at[1]
    bac_s, bac_r = s_sems.at[2], t_sems.at[2]
    bex_s, bex_r = x_sems.at[1], y_sems.at[1]

    def columns(j):
        return pl.ds(pl.multiple_of(lax.rem(j, chunks) * step_width, step_width), step_width)

    def doubled(j):
        return lax.rem(j, 2) == 1

    def plain(s, j):
        return lax.rem(j, 2) == 0 if s == 1 else j >= 0

    def loads(q, four):
        at, k = columns(q), lax.rem(q, depth)
        if four:
            moves = (
                (ag.at[:, at], tall_a.at[k, pl.ds(0, factors)]),
                (au.at[:, at], tall_b.at[k]),
                (gw.at[at, :], wide_g.at[k]),
                (uw.at[at, :], wide_u.at[k]),
            )
        else:
            moves = (
                (dw.at[:, at], tall_a.at[k, pl.ds(0, units)]),
                (bd.at[:, at], tall_b.at[k]),
            )
        return [
            pltpu.make_async_copy(src, dst, w_sem.at[i, k]) for i, (src, dst) in enumerate(moves)
        ]

    def fetch(q):
        outer = (q < chunks) | (q >= 3 * chunks)

        @pl.when(outer & (q < 4 * chunks))
        def _():
            for copy in loads(q, True):
                copy.start()

        @pl.when(jnp.logical_not(outer))
        def _():
            for copy in loads(q, False):
                copy.start()

    def held_part(block, j):
        return held.at[j // chunks, block, :, columns(j)]

    def g_up(block, s, j):
        ref = held_part(block, j)
        return remote(ref, ref, up_s.at[s], up_r.at[s, j], above)

    def g_dn(block, s, j):
        ref = held_part(block, j)
        return remote(ref, ref, dn_s.at[s], dn_r.at[s, j], below)

    def g_ac(at, j):
        ref = held_part(2 * at + col, j)
        return remote(ref, ref, ac_s.at[at], ac_r.at[at, j], partner)

    def g_ac_arrival(at, j):
        ref = held_part(2 * at + 1 - col, j)
        return remote(ref, ref, ac_s.at[at], ac_r.at[at, j], partner)

    def g_ex(direction, block, j, to):
        ref = held_part(block, j)
        return remote(ref, ref, ex_s.at[direction], ex_r.at[direction, j], to)

    def g_own(j):
        g_ac(row, j).start()

        @pl.when(row < line - 1)
        def _():
            g_up(me, 0, j).start()

        @pl.when(row > 0)
        def _():
            g_dn(me, 0, j).start()

    def g_relay(s, j):
        @pl.when(row >= s)
        def _():
            block = me - 2 * s
            g_up(block, s - 1, j).wait_recv()
            if s < line - 1:

                @pl.when(row < line - 1)
                def _():
                    g_up(block, s, j).start()

            @pl.when(plain(s, j))
            def _():
                g_ac(row - s, j).start()

        @pl.when(row + s < line)
        def _():
            block = me + 2 * s
            g_dn(block, s - 1, j).wait_recv()
            if s < line - 1:

                @pl.when(row > 0)
                def _():
                    g_dn(block, s, j).start()

            @pl.when(plain(s, j))
            def _():
                g_ac(row + s, j).start()

        if s == 1:
            g_ac_arrival(row, j).wait_recv()

            @pl.when(doubled(j))
            def _():
                @pl.when(row < line - 1)
                def _():
                    g_ex(0, partner, j, above).start()

                @pl.when(row > 0)
                def _():
                    g_ex(1, partner, j, below).start()

    def g_arrive(j):
        for s in range(1, line):

            @pl.when(plain(s, j) & (row >= s))
            def _():
                g_ac_arrival(row - s, j).wait_recv()

            @pl.when(plain(s, j) & (row + s < line))
            def _():
                g_ac_arrival(row + s, j).wait_recv()

        @pl.when(doubled(j) & (row > 0))
        def _():
            g_ex(0, partner - 2, j, above).wait_recv()

        @pl.when(doubled(j) & (row < line - 1))
        def _():
            g_ex(1, partner + 2, j, below).wait_recv()

    def take(j):
        g_arrive(j)
        at, k = columns(j), lax.rem(j, depth)

        @pl.when(j < chunks)
        def _():
            for copy in loads(j, True):
                copy.wait()
            value = held[0, :, :, at].reshape(rows, step_width)
            gate[...] += dot(value, wide_g[k])
            up[...] += dot(value, wide_u[k])
            mine = dot(choose[...], value).astype(bf16)
            own_x[:, at] = mine
            qa[...] += dot(mine, tall_a[k, :factors], across)
            qb[...] += dot(mine, tall_b[k], across)

        @pl.when(j >= chunks)
        def _():
            for copy in loads(j, False):
                copy.wait()
            value = held[1, :, :, at].reshape(rows, step_width)
            gh[...] += dot(value, tall_a[k, :units], across)
            mine = dot(choose[...], value).astype(bf16)
            own_d[:, at] = mine
            qb[...] += dot(mine, tall_b[k], across)

        fetch(j + depth)

    spans = ((0, 2 * rank), (2 * rank, rank), (3 * rank, rank), (4 * rank, 2 * rank))

    def spread(c):
        first, size = spans[c]
        return [
            remote(
                give.at[pl.ds(first, size)],
                land.at[k, pl.ds(first, size)],
                sum_s.at[c, k],
                sum_r.at[c, k],
                lax.rem(me + k, blocks),
            )
            for k in range(1, blocks)
        ]

    def send_sum(c):
        for copy in spread(c):
            copy.start()

    def take_sum(c):
        first, size = spans[c]
        value = give[first : first + size, :].astype(f32)
        for k, copy in enumerate(spread(c)):
            copy.wait_recv()
            value = value + land[k + 1, first : first + size, :].astype(f32)
        sums[first : first + size, :] = value.astype(bf16)

    def turned(first, size):
        same = line_of((rows, rows), 0) == line_of((rows, rows), 1)
        return dot(same.astype(bf16), sums[first : first + size, :], across).astype(bf16)

    def pick(ref, scale):
        mask = own_slot[...] == line_of((1, factors), 1) // rank
        kept = jnp.where(mask, scale * ref[...], 0.0).astype(bf16)
        found = dot(pat[:, :factors], kept, across).astype(bf16)
        return dot(found, choose[...]).astype(bf16)

    def tenant_mask(i):
        return tenant_col[...] == line_of((1, tile), 1) // rank + i * (tile // rank)

    def each_tile(first, last, body):
        def run(i, carry):
            body(i, tenant_mask(i), pl.ds(pl.multiple_of(i * tile, tile), tile))
            return carry

        lax.fori_loop(first, last, run, 0)

    def add_low_rank(sum_ref, fac, k, scale, mask, at):
        given = dot(coef[:, k * rank : (k + 1) * rank], pat[...])
        wide = jnp.where(mask, given, 0.0).astype(bf16)
        sum_ref[...] += scale * dot(wide, fac[at, :])

    def reduce_low_rank(values, fac, k, scale, mask, at):
        full = dot(values[...], fac[at, :], across)
        kept = jnp.where(mask, full, 0.0).astype(bf16)
        low[k * rank : (k + 1) * rank, :] += scale * dot(pat[...], kept, across)

    def ahead(i, mask, at):
        add_low_rank(gate, fac_g, 0, adapter_scale, mask, at)
        add_low_rank(up, fac_u, 1, adapter_scale, mask, at)

    def back_in(i, mask, at):
        add_low_rank(gh, fac_d, 2, 1.0, mask, at)

    def low_out(i, mask, at):
        reduce_low_rank(hid, fac_d, 0, 1.0, mask, at)

    def back_out(i, mask, at):
        reduce_low_rank(gg, fac_g, 1, adapter_scale, mask, at)
        reduce_low_rank(gu, fac_u, 2, adapter_scale, mask, at)

    def owned(k, first, scale):
        mask = slot_col[...] == line_of((1, factors), 1) // rank
        given = dot(turned(first, rank), pat[:, :factors])
        extra[k] = (scale * jnp.where(mask, given, 0.0)).astype(bf16)

    pieces = (
        (own_x, all_x),
        (hid, all_h),
        (own_d, all_d),
        (gg, all_g),
        (gu, all_u),
        (small, all_small),
    )

    def to_group(src, dst, send, recv, to):
        return pltpu.make_async_remote_copy(
            src_ref=src,
            dst_ref=dst,
            send_sem=send,
            recv_sem=recv,
            device_id={"grp": to},
            device_id_type=MESH,
        )

    def keep_copy(i):
        src, dst = pieces[i]
        return pltpu.make_async_copy(src, dst.at[group], own_sem.at[2 + i])

    def twin_copy(i):
        src, dst = pieces[i]
        return to_group(src, dst.at[group], e_sems.at[0, i, 0], v_sems.at[0, i, 0], twin)

    def far_copy(i, k):
        src, dst = pieces[i]
        to = 2 * lax.rem(high + k, pairs_g) + odd
        return to_group(src, dst.at[group], e_sems.at[1, i, k], v_sems.at[1, i, k], to)

    def hand_on(i, k):
        ref = pieces[i][1].at[2 * lax.rem(high + pairs_g - k, pairs_g) + odd]
        return to_group(ref, ref, e_sems.at[2, i, k], v_sems.at[2, i, k], twin)

    def share(i):
        for k in range(1, pairs_g):
            far_copy(i, k).start()
        twin_copy(i).start()
        keep_copy(i).start()

    def pass_on(i):
        for k in range(1, pairs_g):
            far_copy(i, k).wait_recv()
            hand_on(i, k).start()

    def part(block, j):
        return held.at[lax.rem(2 + j // chunks, 3), block, :, columns(j)]

    def piece(buf, at, j):
        return buf.at[j // chunks, at, :, columns(j)]

    def flat(buf, j):
        return buf.at[j // chunks, :, columns(j)]

    def s_ac(src, at, j):
        return remote(src, piece(pair_buf, at, j), bac_s.at[at], bac_r.at[at, j], partner)

    def s_up(at, j):
        return remote(
            piece(pair_buf, at, j), piece(line_buf, at, j), bup_s.at[at], bup_r.at[at, j], above
        )

    def s_dn(at, j, landing):
        return remote(piece(pair_buf, at, j), landing, bdn_s.at[at], bdn_r.at[at, j], below)

    def s_ex(direction, block, j, to):
        return remote(
            part(block, j),
            piece(ex_buf, direction, j),
            bex_s.at[direction],
            bex_r.at[direction, j],
            to,
        )

    def make(j):
        at, k = columns(j), lax.rem(j + total, depth)

        @pl.when(j < chunks)
        def _():
            for copy in loads(j + total, False):
                copy.wait()
            value = dot(hid[...], tall_a[k, :units]) + dot(extra[0], tall_b[k])
            held[2, :, :, at] = value.astype(bf16).reshape(blocks, own_rows, step_width)

        @pl.when(j >= chunks)
        def _():
            for copy in loads(j + total, True):
                copy.wait()
            value = (
                dot(gg[...], wide_g[k], across)
                + dot(gu[...], wide_u[k], across)
                + dot(extra[1], tall_a[k, :factors])
                + dot(extra[2], tall_b[k])
            )
            held[0, :, :, at] = value.astype(bf16).reshape(blocks, own_rows, step_width)

        for s in range(line - 1, 0, -1):
            for ok, to in ((row + s < line, row + s), (row >= s, row - s)):

                @pl.when(ok & plain(s, j))
                def _():
                    s_ac(part(2 * to + 1 - col, j), to, j).start()

        @pl.when(doubled(j))
        def _():
            @pl.when(row < line - 1)
            def _():
                s_ex(0, partner + 2, j, above).start()

            @pl.when(row > 0)
            def _():
                s_ex(1, partner - 2, j, below).start()

        @pl.when(lax.rem(j, 2) == 0)
        def _():
            s_ac(part(partner, j), row, j).start()

        fetch(j + total + depth)

    def cross_over(j):
        @pl.when(doubled(j))
        def _():
            acc[...] = part(partner, j)[...].astype(f32)

            @pl.when(row > 0)
            def _():
                s_ex(0, partner, j, above).wait_recv()
                acc[...] += piece(ex_buf, 0, j)[...].astype(f32)

            @pl.when(row < line - 1)
            def _():
                s_ex(1, partner, j, below).wait_recv()
                acc[...] += piece(ex_buf, 1, j)[...].astype(f32)

            flat(cross_buf, j)[...] = acc[...].astype(bf16)
            s_ac(flat(cross_buf, j), row, j).start()

    def pair_up(s, at, j):
        mine = part(2 * at + col, j)
        acc[...] = mine[...].astype(f32)

        @pl.when(plain(s, j))
        def _():
            s_ac(mine, at, j).wait_recv()
            acc[...] += piece(pair_buf, at, j)[...].astype(f32)

    def s_relay(s, j):
        @pl.when(row + s < line)
        def _():
            at = row + s
            pair_up(s, at, j)
            if s < line - 1:

                @pl.when(row > 0)
                def _():
                    s_up(at, j).wait_recv()
                    acc[...] += piece(line_buf, at, j)[...].astype(f32)

            piece(pair_buf, at, j)[...] = acc[...].astype(bf16)
            s_up(at, j).start()

        @pl.when(row >= s)
        def _():
            at = row - s
            landing = flat(top_buf, j) if s == 1 else piece(line_buf, at, j)
            pair_up(s, at, j)
            if s < line - 1:

                @pl.when(row < line - 1)
                def _():
                    s_dn(at, j, landing).wait_recv()
                    acc[...] += piece(line_buf, at, j)[...].astype(f32)

            piece(pair_buf, at, j)[...] = acc[...].astype(bf16)
            s_dn(at, j, landing).start()

    def finish(j):
        mine = part(me, j)
        s_ac(mine, row, j).wait_recv()
        acc[...] = mine[...].astype(f32) + piece(pair_buf, row, j)[...].astype(f32)

        @pl.when(row > 0)
        def _():
            s_up(row, j).wait_recv()
            acc[...] += piece(line_buf, row, j)[...].astype(f32)

        @pl.when(row < line - 1)
        def _():
            s_dn(row, j, flat(top_buf, j)).wait_recv()
            acc[...] += flat(top_buf, j)[...].astype(f32)

        out[j // chunks, :, columns(j)] = acc[...].astype(bf16)

    def sent(ref, sem):
        remote(ref, ref, sem, sum_r.at[0, 0], partner).wait_send()

    both, one = held.at[pl.ds(0, 2), me], held.at[0, me]

    def sent_sums(acs, exs):
        sent(both, acs.at[row])
        for s in range(1, line):
            for ok, at in ((row >= s, row - s), (row + s < line, row + s)):

                @pl.when(ok)
                def _():
                    sent(one if s == 1 else both, acs.at[at])

        @pl.when(row < line - 1)
        def _():
            sent(one, exs.at[0])

        @pl.when(row > 0)
        def _():
            sent(one, exs.at[1])

    def gather_sent():
        sent_sums(ac_s, ex_s)
        for s in range(line - 1):

            @pl.when((row >= s) & (row < line - 1))
            def _():
                sent(both, up_s.at[s])

            @pl.when((row + s < line) & (row > 0))
            def _():
                sent(both, dn_s.at[s])

    own = [
        pltpu.make_async_copy(ref, held.at[c, me], own_sem.at[c])
        for c, ref in enumerate((x_ref, d_ref))
    ]
    for copy in own:
        copy.start()
    barrier = pltpu.get_barrier_semaphore()
    for k in range(1, blocks):
        pl.semaphore_signal(
            barrier, inc=1, device_id={"blk": lax.rem(me + k, blocks)}, device_id_type=MESH
        )
    pl.semaphore_signal(barrier, inc=1, device_id={"grp": twin}, device_id_type=MESH)
    for k in range(1, pairs_g):
        to = 2 * lax.rem(high + k, pairs_g) + odd
        pl.semaphore_signal(barrier, inc=1, device_id={"grp": to}, device_id_type=MESH)
    for q in range(depth):
        fetch(q)
    tables = [
        pltpu.make_async_copy(src, dst, f_sem.at[i])
        for i, (src, dst) in enumerate(((bg, fac_g), (bu, fac_u), (ad, fac_d)))
    ]
    for copy in tables:
        copy.start()
    for copy in own:
        copy.wait()
    pl.semaphore_wait(barrier, blocks - 1 + pairs_g)
    g_own(0)

    for ref in (gate, up, gh, qa, qb, low):
        ref[...] = jnp.zeros_like(ref)
    pat[...] = (lax.rem(line_of((rank, tile), 1), rank) == line_of((rank, tile), 0)).astype(bf16)
    per_owner = factors // rank
    here = line_of((rows, 1), 0)
    source = (here // own_rows * groups + group) * own_rows + lax.rem(here, own_rows)
    every = tenant_row.shape[1]
    hit = line_of((1, every), 1) == source
    tenants = jnp.sum(jnp.where(hit, tenant_row[...].astype(f32), 0.0), axis=1, keepdims=True)
    tenant_col[...] = tenants.astype(jnp.int32)
    known = line_of((1, slot_row.shape[1]), 1) == tenant_col[...]
    slots = jnp.sum(jnp.where(known, slot_row[...].astype(f32), 0.0), axis=1, keepdims=True)
    local = slots.astype(jnp.int32) - me * per_owner
    slot_col[...] = local
    mine_col = ((local >= 0) & (local < per_owner)).astype(f32)
    first_i, second_i = line_of((rows, rows), 0), line_of((rows, rows), 1)
    same_i = first_i == second_i
    within = jnp.sum(jnp.where(first_i < second_i, mine_col, 0.0), axis=0, keepdims=True)
    mine_row = jnp.sum(jnp.where(same_i, mine_col, 0.0), axis=0, keepdims=True)
    local_row = jnp.sum(jnp.where(same_i, local.astype(f32), 0.0), axis=0, keepdims=True)
    tenant_line = jnp.sum(jnp.where(same_i, tenants, 0.0), axis=0, keepdims=True)
    chosen = (mine_row > 0.5) & (within == line_of((picks, 1), 0).astype(f32))
    choose[...] = chosen.astype(bf16)
    owned_at = jnp.sum(jnp.where(chosen, local_row + 1.0, 0.0), axis=1, keepdims=True) - 1.0
    own_slot[...] = owned_at.astype(jnp.int32)
    ids = line_of((rank, rows), 0)
    coarse = jnp.floor(tenant_line * (1.0 / 128.0))
    picked_row = jnp.sum(
        jnp.where(line_of((picks, rows), 0) == line_of((picks, rows), 1), owned_at, 0.0),
        axis=0,
        keepdims=True,
    )
    small[6 * rank :, :] = jnp.where(
        ids == 0,
        coarse,
        jnp.where(ids == 1, tenant_line - 128.0 * coarse, jnp.where(ids == 2, picked_row, 0.0)),
    ).astype(bf16)

    half = max(1, tiles // 2)

    def step(t, carry):
        def hook(at, body):
            pl.when(t == at)(body)

        @pl.when((t > 0) & (t < total))
        def _():
            g_own(t)

        for s in range(1, line):
            j = t - slack * s

            @pl.when((j >= 0) & (j < total))
            def _():
                g_relay(s, j)

        u = t - begin

        @pl.when((u >= 0) & (u < total))
        def _():
            make(u)

        j = t - filled

        @pl.when((j >= 0) & (j < total))
        def _():
            take(j)

        @functools.partial(hook, x_end)
        def _():
            give[:rank, :] = pick(qa, 1.0)
            give[rank : 2 * rank, :] = pick(qb, 1.0)
            send_sum(0)
            share(0)
            qb[...] = jnp.zeros_like(qb)

        @functools.partial(hook, x_end + 3)
        def _():
            for copy in tables:
                copy.wait()
            take_sum(0)
            coef[:, : 2 * rank] = turned(0, 2 * rank)
            each_tile(0, half, ahead)

        @functools.partial(hook, x_end + 4)
        def _():
            each_tile(half, tiles, ahead)

        @functools.partial(hook, x_end + 5)
        def _():
            act_val, act_slope = silu_pair(gate[...])
            hid[...] = (act_val * up[...]).astype(bf16)
            gate[...] = act_val
            up[...] = up[...] * act_slope
            each_tile(0, half, low_out)

        @functools.partial(hook, x_end + 6)
        def _():
            each_tile(half, tiles, low_out)
            give[3 * rank : 4 * rank, :] = low[:rank, :].astype(bf16)
            send_sum(2)
            share(1)

        @functools.partial(hook, d_end)
        def _():
            give[2 * rank : 3 * rank, :] = pick(qb, adapter_scale)
            send_sum(1)
            take_sum(2)
            owned(0, 3 * rank, adapter_scale)
            share(2)

        @functools.partial(hook, d_end + 2)
        def _():
            take_sum(1)
            coef[:, 2 * rank : 3 * rank] = turned(2 * rank, rank)
            each_tile(0, tiles, back_in)
            grad_h = gh[...]
            gg[...] = (grad_h * up[...]).astype(bf16)
            gu[...] = (grad_h * gate[...]).astype(bf16)

        @functools.partial(hook, d_end + 3)
        def _():
            share(3)
            share(4)
            each_tile(0, half, back_out)

        @functools.partial(hook, d_end + 4)
        def _():
            each_tile(half, tiles, back_out)
            give[4 * rank :, :] = low[rank:, :].astype(bf16)
            send_sum(3)

        @functools.partial(hook, d_end + 7)
        def _():
            gather_sent()
            take_sum(3)
            owned(1, 4 * rank, 1.0)
            owned(2, 5 * rank, 1.0)
            small[: 3 * rank, :] = sums[: 3 * rank, :]
            found = dot(sums[3 * rank :, :], choose[...], across)
            wide = (line_of((picks, rows), 0) == line_of((picks, rows), 1)).astype(bf16)
            small[3 * rank : 6 * rank, :] = dot(found.astype(bf16), wide).astype(bf16)
            share(5)

        for i, at in enumerate(
            (x_end + 8, x_end + 9, d_end + 8, d_end + 11, d_end + 12, d_end + 13)
        ):
            hook(at, functools.partial(pass_on, i))

        j = t - begin - slack

        @pl.when((j >= 0) & (j < total))
        def _():
            cross_over(j)

        for s in range(line - 1, 0, -1):
            j = t - begin - slack * (line - s)

            @pl.when((j >= 0) & (j < total))
            def _():
                s_relay(s, j)

        j = t - begin - filled

        @pl.when(j >= 0)
        def _():
            finish(j)

        return carry

    lax.fori_loop(0, finish_step, step, 0)

    for c in range(len(spans)):
        for copy in spread(c):
            copy.wait_send()
    for i in range(len(pieces)):
        keep_copy(i).wait()
        twin_copy(i).wait()
        for k in range(1, pairs_g):
            far_copy(i, k).wait_send()
            hand_on(i, k).wait()

    sent_sums(bac_s, bex_s)
    for s in range(1, line):

        @pl.when(row + s < line)
        def _():
            sent(both, bup_s.at[row + s])

        @pl.when(row >= s)
        def _():
            sent(both, bdn_s.at[row - s])


def window_terms(blocks, groups, x, dy, gw, uw, dw, ag, au, bd, bg, bu, ad, tenants, slots, rank):
    line = blocks // 2
    own_rows, width = x.shape
    rows, units = blocks * own_rows, gw.shape[1]
    factors, count = ag.shape[0], bg.shape[0]
    picks = 2 * own_rows
    chunks = 8
    step_width = width // chunks
    depth = 3
    tile = min(1024, count)
    dma = pltpu.SemaphoreType.DMA
    vmem = pltpu.VMEM
    anywhere, inside = pl.BlockSpec(memory_space=pl.ANY), pl.BlockSpec(memory_space=vmem)
    every = lambda *shape: jax.ShapeDtypeStruct((groups,) + shape, bf16)
    return pl.pallas_call(
        functools.partial(window_kernel, blocks, groups, rank, chunks),
        out_shape=(
            jax.ShapeDtypeStruct((2, own_rows, width), bf16),
            every(picks, width),
            every(picks, width),
            every(rows, units),
            every(rows, units),
            every(rows, units),
            every(7 * rank, rows),
        ),
        in_specs=[anywhere] * 11 + [inside] * 2,
        out_specs=(inside,) + (anywhere,) * 6,
        scratch_shapes=[
            vmem((3, blocks, own_rows, width), bf16),
            vmem((2, line, own_rows, width), bf16),
            vmem((2, line, own_rows, width), bf16),
            vmem((2, own_rows, width), bf16),
            vmem((2, 2, own_rows, width), bf16),
            vmem((2, own_rows, width), bf16),
            vmem((own_rows, step_width), f32),
            vmem((rows, units), f32),
            vmem((rows, units), f32),
            vmem((rows, units), f32),
            vmem((picks, factors), f32),
            vmem((picks, factors), f32),
            vmem((picks, width), bf16),
            vmem((picks, width), bf16),
            vmem((rows, units), bf16),
            vmem((rows, units), bf16),
            vmem((rows, units), bf16),
            vmem((3, rows, factors), bf16),
            vmem((depth, step_width, units), bf16),
            vmem((depth, step_width, units), bf16),
            vmem((depth, max(units, factors), step_width), bf16),
            vmem((depth, factors, step_width), bf16),
            vmem((count, units), bf16),
            vmem((count, units), bf16),
            vmem((count, units), bf16),
            vmem((rank, tile), bf16),
            vmem((picks, rows), bf16),
            vmem((picks, 1), jnp.int32),
            vmem((rows, 1), jnp.int32),
            vmem((rows, 1), jnp.int32),
            vmem((6 * rank, rows), bf16),
            vmem((blocks, 6 * rank, rows), bf16),
            vmem((6 * rank, rows), bf16),
            vmem((3 * rank, rows), f32),
            vmem((rows, 3 * rank), bf16),
            vmem((7 * rank, rows), bf16),
            dma((8,)),
            dma((4, depth)),
            dma((3,)),
            dma((3, line)),
            dma((3, line, 2 * chunks)),
            dma((3, line)),
            dma((3, line, 2 * chunks)),
            dma((2, 2)),
            dma((2, 2, 2 * chunks)),
            dma((4, blocks)),
            dma((4, blocks)),
            dma((3, 6, groups // 2)),
            dma((3, 6, groups // 2)),
        ],
        compiler_params=pltpu.CompilerParams(
            collective_id=0, has_side_effects=True, vmem_limit_bytes=vmem_grant
        ),
        cost_estimate=pl.CostEstimate(
            flops=12 * rows * width * (units + factors) + 12 * rows * count * units,
            bytes_accessed=12 * width * (units + factors) + 6 * count * units,
            transcendentals=rows * units,
        ),
        name="window_terms",
    )(x, dy, gw, uw, dw, ag, au, bd, bg, bu, ad, tenants, slots)


def grads_kernel(
    rank, small, x, d, hid, gg, gu, o_ag, o_au, o_bd, o_bg, o_bu, o_ad, slot_w, marks
):
    i = pl.program_id(0)
    groups, picks, _ = x.shape
    rows = hid.shape[1]
    tall = o_bg.shape[0]
    entries = tall // rank
    own = o_ag.shape[0]

    @pl.when(i == 0)
    def _():
        here = lax.axis_index("grp") * (own // rank)
        slot = jnp.concatenate([small[q, 6 * rank :, :picks] for q in range(groups)], axis=1)
        mask = (line_of((own, 1), 0) // rank + here).astype(f32) == slot[2:3].astype(f32)
        for k, scale in ((0, adapter_scale), (1, 1.0), (2, 1.0)):
            at = (3 + k) * rank
            value = jnp.concatenate(
                [small[q, at : at + rank, :picks] for q in range(groups)], axis=1
            )
            value = jnp.concatenate([value.astype(f32)] * (own // rank), axis=0)
            slot_w[k] = jnp.where(mask, scale * value, 0.0).astype(bf16)
        for q in range(groups):
            ids = small[q, 6 * rank :, :].astype(f32)
            marks[:, q * rows : (q + 1) * rows] = 128.0 * ids[0:1] + ids[1:2]

    value_x = x[...].reshape(groups * picks, -1)
    value_d = d[...].reshape(groups * picks, -1)
    o_bd[...] = dot(slot_w[0], value_d)
    o_ag[...] = dot(slot_w[1], value_x)
    o_au[...] = dot(slot_w[2], value_x)
    first = lax.axis_index("grp") * (entries * pl.num_programs(0)) + i * entries
    mask = (line_of((tall, 1), 0) // rank + first).astype(f32) == marks[...]
    for k, scale, values, ref in (
        (0, adapter_scale, gg, o_bg),
        (1, adapter_scale, gu, o_bu),
        (2, 1.0, hid, o_ad),
    ):
        given = jnp.concatenate(
            [small[q, k * rank : (k + 1) * rank, :] for q in range(groups)], axis=1
        )
        given = jnp.concatenate([given.astype(f32)] * entries, axis=0)
        weight = jnp.where(mask, scale * given, 0.0).astype(bf16)
        ref[...] = dot(weight, values[...].reshape(groups * rows, -1))


def outer_sums(rank, small, x, d, hid, gg, gu, slots, tenants):
    groups, picks, width = x.shape
    rows, units = hid.shape[1:]
    steps = 8
    wide, tall = width // steps, tenants * rank // steps
    own = slots * rank
    whole = lambda value: pl.BlockSpec(value.shape, lambda i: (0, 0, 0))
    cols = pl.BlockSpec((groups, picks, wide), lambda i: (0, 0, i))
    slot_out = pl.BlockSpec((own, wide), lambda i: (0, i))
    tenant_out = pl.BlockSpec((tall, units), lambda i: (i, 0))
    found = pl.pallas_call(
        functools.partial(grads_kernel, rank),
        grid=(steps,),
        out_shape=(jax.ShapeDtypeStruct((own, width), f32),) * 3
        + (jax.ShapeDtypeStruct((tenants * rank, units), f32),) * 3,
        in_specs=[whole(small), cols, cols, whole(hid), whole(gg), whole(gu)],
        out_specs=(slot_out,) * 3 + (tenant_out,) * 3,
        scratch_shapes=[
            pltpu.VMEM((3, own, groups * picks), bf16),
            pltpu.VMEM((1, groups * rows), f32),
        ],
        compiler_params=pltpu.CompilerParams(vmem_limit_bytes=vmem_grant),
        name="outer_sums",
    )(small, x, d, hid, gg, gu)
    return [part.reshape(-1, rank, part.shape[1]) for part in found]


def local(
    tokens,
    cotangent,
    gate_weight,
    up_weight,
    down_weight,
    a_gate,
    a_up,
    down_output_factors,
    b_gate,
    b_up,
    a_down,
    tenant_of_row,
    adapter_slot,
):
    width = tokens.shape[1]
    blocks = lax.axis_size("blk")
    groups = lax.axis_size("grp")
    per_owner, rank = a_gate.shape[:2]
    tenants, _, units = b_gate.shape
    slot_factors = [f.reshape(per_owner * rank, width) for f in (a_gate, a_up, down_output_factors)]
    tenant_factors = [f.reshape(tenants * rank, units) for f in (b_gate, b_up, a_down)]
    result, all_x, all_d, hid, gg, gu, small = window_terms(
        blocks,
        groups,
        tokens,
        cotangent,
        gate_weight,
        up_weight,
        down_weight,
        *slot_factors,
        *tenant_factors,
        tenant_of_row[None, :],
        adapter_slot[None, :],
        rank,
    )
    grads = outer_sums(
        rank, small, all_x, all_d, hid, gg, gu, per_owner // groups, tenants // groups
    )
    return (result[0], result[1], *grads)


def solution(mesh):
    placed = (
        P(("blk", "grp"), None),
        P(("blk", "grp"), None),
        P(None, "blk"),
        P(None, "blk"),
        P("blk", None),
        P("blk", None, None),
        P("blk", None, None),
        P("blk", None, None),
        P(None, None, "blk"),
        P(None, None, "blk"),
        P(None, None, "blk"),
        P(),
        P(),
    )
    return jax.shard_map(
        local,
        mesh=mesh,
        in_specs=placed,
        out_specs=(
            P(("blk", "grp"), None),
            P(("blk", "grp"), None),
            P(("blk", "grp"), None, None),
            P(("blk", "grp"), None, None),
            P(("blk", "grp"), None, None),
            P("grp", None, "blk"),
            P("grp", None, "blk"),
            P("grp", None, "blk"),
        ),
        check_vma=False,
    )
```

```python
import functools
import math

import jax
import jax.numpy as jnp
from jax import lax
from jax.experimental import pallas as pl
from jax.experimental.pallas import tpu as pltpu
from jax.sharding import PartitionSpec as P

MESH = pl.DeviceIdType.MESH
bf16 = jnp.bfloat16
vmem_grant = 60 * 2**20
f32 = jnp.float32
slack = 2


def remote(src, dst, send, recv, to):
    return pltpu.make_async_remote_copy(
        src_ref=src,
        dst_ref=dst,
        send_sem=send,
        recv_sem=recv,
        device_id={"blk": to},
        device_id_type=MESH,
    )


def place(blocks):
    me = lax.axis_index("blk")
    line = blocks // 2
    row = me // 2
    col = me - 2 * row
    partner = me + 1 - 2 * col
    return me, line, row, col, partner


adapter_scale = 2.0


def silu_pair(gate_in):
    sigmoid_val = jax.nn.sigmoid(gate_in)
    return (gate_in * sigmoid_val, sigmoid_val * (1.0 + gate_in * (1.0 - sigmoid_val)))


def dot(a, b, dims=((1,), (0,))):
    return lax.dot_general(a, b, (dims, ((), ())), preferred_element_type=f32)


across = ((1,), (1,))
lanes = 128


def fold(value):
    kept = value[:, :lanes]
    for k in range(1, value.shape[1] // lanes):
        kept = kept + value[:, k * lanes : (k + 1) * lanes]
    return kept


def repeat(value, width):
    return jnp.concatenate([value] * (width // lanes), axis=1)


def line_of(shape, axis):
    return lax.broadcasted_iota(jnp.int32, shape, axis)


def window_kernel(
    blocks,
    groups,
    rank,
    chunks,
    x_ref,
    d_ref,
    gw,
    uw,
    dw,
    ag,
    au,
    bd,
    bg,
    bu,
    ad,
    tenant_hbm,
    slot_hbm,
    out,
    all_x,
    all_d,
    all_h,
    all_g,
    all_u,
    all_small,
    held,
    pair_buf,
    line_buf,
    top_buf,
    ex_buf,
    cross_buf,
    acc,
    gate,
    up,
    gh,
    qa,
    qb,
    own_x,
    own_d,
    hid,
    gg,
    gu,
    extra,
    wide_g,
    wide_u,
    tall_a,
    tall_b,
    fac_g,
    fac_u,
    fac_d,
    pat,
    choose,
    own_slot,
    tenant_col,
    slot_col,
    give,
    land,
    sums,
    low,
    coef,
    small,
    tenant_row,
    slot_row,
    own_sem,
    w_sem,
    f_sem,
    g_sems,
    r_sems,
    s_sems,
    t_sems,
    x_sems,
    y_sems,
    sum_s,
    sum_r,
    e_sems,
    v_sems,
):
    me, line, row, col, partner = place(blocks)
    above, below = me + 2, me - 2
    own_rows, width = x_ref.shape
    rows = blocks * own_rows
    step_width = width // chunks
    total = 2 * chunks
    depth = wide_g.shape[0]
    units, factors = dw.shape[0], bd.shape[0]
    count = bg.shape[0]
    tile = min(1024, count)
    tiles = count // tile
    picks = choose.shape[0]
    group = lax.axis_index("grp")
    pairs_g, high = groups // 2, group // 2
    odd = group - 2 * high
    twin = group + 1 - 2 * odd
    filled = slack * line
    x_end = chunks - 1 + filled
    d_end = total - 1 + filled
    begin = d_end - 1
    finish_step = begin + total + filled

    up_s, up_r, dn_s, dn_r = g_sems.at[0], r_sems.at[0], g_sems.at[1], r_sems.at[1]
    ac_s, ac_r = g_sems.at[2], r_sems.at[2]
    ex_s, ex_r = x_sems.at[0], y_sems.at[0]
    bup_s, bup_r, bdn_s, bdn_r = s_sems.at[0], t_sems.at[0], s_sems.at[1], t_sems.at[1]
    bac_s, bac_r = s_sems.at[2], t_sems.at[2]
    bex_s, bex_r = x_sems.at[1], y_sems.at[1]

    def columns(j):
        return pl.ds(pl.multiple_of(lax.rem(j, chunks) * step_width, step_width), step_width)

    def doubled(j):
        return lax.rem(j, 2) == 1

    def plain(s, j):
        return lax.rem(j, 2) == 0 if s == 1 else j >= 0

    def loads(q, four):
        at, k = columns(q), lax.rem(q, depth)
        if four:
            moves = (
                (ag.at[:, at], tall_a.at[k, pl.ds(0, factors)]),
                (au.at[:, at], tall_b.at[k]),
                (gw.at[at, :], wide_g.at[k]),
                (uw.at[at, :], wide_u.at[k]),
            )
        else:
            moves = (
                (dw.at[:, at], tall_a.at[k, pl.ds(0, units)]),
                (bd.at[:, at], tall_b.at[k]),
            )
        return [
            pltpu.make_async_copy(src, dst, w_sem.at[i, k]) for i, (src, dst) in enumerate(moves)
        ]

    def fetch(q):
        outer = (q < chunks) | (q >= 3 * chunks)

        @pl.when(outer & (q < 4 * chunks))
        def _():
            for copy in loads(q, True):
                copy.start()

        @pl.when(jnp.logical_not(outer))
        def _():
            for copy in loads(q, False):
                copy.start()

    def held_part(block, j):
        return held.at[j // chunks, block, :, columns(j)]

    def g_up(block, s, j):
        ref = held_part(block, j)
        return remote(ref, ref, up_s.at[s], up_r.at[s, j], above)

    def g_dn(block, s, j):
        ref = held_part(block, j)
        return remote(ref, ref, dn_s.at[s], dn_r.at[s, j], below)

    def g_ac(at, j):
        ref = held_part(2 * at + col, j)
        return remote(ref, ref, ac_s.at[at], ac_r.at[at, j], partner)

    def g_ac_arrival(at, j):
        ref = held_part(2 * at + 1 - col, j)
        return remote(ref, ref, ac_s.at[at], ac_r.at[at, j], partner)

    def g_ex(direction, block, j, to):
        ref = held_part(block, j)
        return remote(ref, ref, ex_s.at[direction], ex_r.at[direction, j], to)

    def g_own(j):
        g_ac(row, j).start()

        @pl.when(row < line - 1)
        def _():
            g_up(me, 0, j).start()

        @pl.when(row > 0)
        def _():
            g_dn(me, 0, j).start()

    def g_relay(s, j):
        @pl.when(row >= s)
        def _():
            block = me - 2 * s
            g_up(block, s - 1, j).wait_recv()
            if s < line - 1:

                @pl.when(row < line - 1)
                def _():
                    g_up(block, s, j).start()

            @pl.when(plain(s, j))
            def _():
                g_ac(row - s, j).start()

        @pl.when(row + s < line)
        def _():
            block = me + 2 * s
            g_dn(block, s - 1, j).wait_recv()
            if s < line - 1:

                @pl.when(row > 0)
                def _():
                    g_dn(block, s, j).start()

            @pl.when(plain(s, j))
            def _():
                g_ac(row + s, j).start()

        if s == 1:
            g_ac_arrival(row, j).wait_recv()

            @pl.when(doubled(j))
            def _():
                @pl.when(row < line - 1)
                def _():
                    g_ex(0, partner, j, above).start()

                @pl.when(row > 0)
                def _():
                    g_ex(1, partner, j, below).start()

    def g_arrive(j):
        for s in range(1, line):

            @pl.when(plain(s, j) & (row >= s))
            def _():
                g_ac_arrival(row - s, j).wait_recv()

            @pl.when(plain(s, j) & (row + s < line))
            def _():
                g_ac_arrival(row + s, j).wait_recv()

        @pl.when(doubled(j) & (row > 0))
        def _():
            g_ex(0, partner - 2, j, above).wait_recv()

        @pl.when(doubled(j) & (row < line - 1))
        def _():
            g_ex(1, partner + 2, j, below).wait_recv()

    def take(j):
        g_arrive(j)
        at, k = columns(j), lax.rem(j, depth)

        @pl.when(j < chunks)
        def _():
            for copy in loads(j, True):
                copy.wait()
            value = held[0, :, :, at].reshape(rows, step_width)
            gate[...] += dot(value, wide_g[k])
            up[...] += dot(value, wide_u[k])
            mine = dot(choose[...], value).astype(bf16)
            own_x[:, at] = mine
            qa[...] += dot(mine, tall_a[k, :factors], across)
            qb[...] += dot(mine, tall_b[k], across)

        @pl.when(j >= chunks)
        def _():
            for copy in loads(j, False):
                copy.wait()
            value = held[1, :, :, at].reshape(rows, step_width)
            gh[...] += dot(value, tall_a[k, :units], across)
            mine = dot(choose[...], value).astype(bf16)
            own_d[:, at] = mine
            qb[...] += dot(mine, tall_b[k], across)

        fetch(j + depth)

    spans = ((0, 2 * rank), (2 * rank, rank), (3 * rank, rank), (4 * rank, 2 * rank))

    def spread(c):
        first, size = spans[c]
        return [
            remote(
                give.at[pl.ds(first, size)],
                land.at[k, pl.ds(first, size)],
                sum_s.at[c, k],
                sum_r.at[c, k],
                lax.rem(me + k, blocks),
            )
            for k in range(1, blocks)
        ]

    def send_sum(c):
        for copy in spread(c):
            copy.start()

    def take_sum(c):
        first, size = spans[c]
        value = give[first : first + size, :].astype(f32)
        for k, copy in enumerate(spread(c)):
            copy.wait_recv()
            value = value + land[k + 1, first : first + size, :].astype(f32)
        sums[first : first + size, :] = value.astype(bf16)

    def turned(first, size):
        same = line_of((rows, rows), 0) == line_of((rows, rows), 1)
        return dot(same.astype(bf16), sums[first : first + size, :], across).astype(bf16)

    def pick(ref, scale):
        mask = own_slot[...] == line_of((1, factors), 1) // rank
        kept = fold(jnp.where(mask, scale * ref[...], 0.0)).astype(bf16)
        found = dot(pat[...], kept, across).astype(bf16)
        return dot(found, choose[...]).astype(bf16)

    def tenant_mask(i):
        return tenant_col[...] == line_of((1, tile), 1) // rank + i * (tile // rank)

    def each_tile(first, last, body):
        def run(i, carry):
            body(i, tenant_mask(i), pl.ds(pl.multiple_of(i * tile, tile), tile))
            return carry

        lax.fori_loop(first, last, run, 0)

    def add_low_rank(sum_ref, fac, k, scale, mask, at):
        wide = jnp.where(mask, repeat(coef[k], tile), 0.0).astype(bf16)
        sum_ref[...] += scale * dot(wide, fac[at, :])

    def reduce_low_rank(values, fac, k, mask, at):
        full = dot(values[...], fac[at, :], across)
        low[k] += fold(jnp.where(mask, full, 0.0))

    def ahead(i, mask, at):
        add_low_rank(gate, fac_g, 0, adapter_scale, mask, at)
        add_low_rank(up, fac_u, 1, adapter_scale, mask, at)

    def back_in(i, mask, at):
        add_low_rank(gh, fac_d, 2, 1.0, mask, at)

    def low_out(i, mask, at):
        reduce_low_rank(hid, fac_d, 0, mask, at)

    def back_out(i, mask, at):
        reduce_low_rank(gg, fac_g, 1, mask, at)
        reduce_low_rank(gu, fac_u, 2, mask, at)

    def lowered(k, scale):
        return (scale * dot(pat[...], low[k].astype(bf16), across)).astype(bf16)

    def owned(k, first, scale):
        mask = slot_col[...] == line_of((1, factors), 1) // rank
        given = repeat(dot(turned(first, rank), pat[...]), factors)
        extra[k] = (scale * jnp.where(mask, given, 0.0)).astype(bf16)

    pieces = (
        (own_x, all_x),
        (hid, all_h),
        (own_d, all_d),
        (gg, all_g),
        (gu, all_u),
        (small, all_small),
    )

    def to_group(src, dst, send, recv, to):
        return pltpu.make_async_remote_copy(
            src_ref=src,
            dst_ref=dst,
            send_sem=send,
            recv_sem=recv,
            device_id={"grp": to},
            device_id_type=MESH,
        )

    def keep_copy(i):
        src, dst = pieces[i]
        return pltpu.make_async_copy(src, dst.at[group], own_sem.at[2 + i])

    def twin_copy(i):
        src, dst = pieces[i]
        return to_group(src, dst.at[group], e_sems.at[0, i, 0], v_sems.at[0, i, 0], twin)

    def far_copy(i, k):
        src, dst = pieces[i]
        to = 2 * lax.rem(high + k, pairs_g) + odd
        return to_group(src, dst.at[group], e_sems.at[1, i, k], v_sems.at[1, i, k], to)

    def hand_on(i, k):
        ref = pieces[i][1].at[2 * lax.rem(high + pairs_g - k, pairs_g) + odd]
        return to_group(ref, ref, e_sems.at[2, i, k], v_sems.at[2, i, k], twin)

    def share(i):
        for k in range(1, pairs_g):
            far_copy(i, k).start()
        twin_copy(i).start()
        keep_copy(i).start()

    def pass_on(i):
        for k in range(1, pairs_g):
            far_copy(i, k).wait_recv()
            hand_on(i, k).start()

    def part(block, j):
        return held.at[lax.rem(2 + j // chunks, 3), block, :, columns(j)]

    def piece(buf, at, j):
        return buf.at[j // chunks, at, :, columns(j)]

    def flat(buf, j):
        return buf.at[j // chunks, :, columns(j)]

    def s_ac(src, at, j):
        return remote(src, piece(pair_buf, at, j), bac_s.at[at], bac_r.at[at, j], partner)

    def s_up(at, j):
        return remote(
            piece(pair_buf, at, j), piece(line_buf, at, j), bup_s.at[at], bup_r.at[at, j], above
        )

    def s_dn(at, j, landing):
        return remote(piece(pair_buf, at, j), landing, bdn_s.at[at], bdn_r.at[at, j], below)

    def s_ex(direction, block, j, to):
        return remote(
            part(block, j),
            piece(ex_buf, direction, j),
            bex_s.at[direction],
            bex_r.at[direction, j],
            to,
        )

    def make(j):
        at, k = columns(j), lax.rem(j + total, depth)

        @pl.when(j < chunks)
        def _():
            for copy in loads(j + total, False):
                copy.wait()
            value = dot(hid[...], tall_a[k, :units]) + dot(extra[0], tall_b[k])
            held[2, :, :, at] = value.astype(bf16).reshape(blocks, own_rows, step_width)

        @pl.when(j >= chunks)
        def _():
            for copy in loads(j + total, True):
                copy.wait()
            value = (
                dot(gg[...], wide_g[k], across)
                + dot(gu[...], wide_u[k], across)
                + dot(extra[1], tall_a[k, :factors])
                + dot(extra[2], tall_b[k])
            )
            held[0, :, :, at] = value.astype(bf16).reshape(blocks, own_rows, step_width)

        for s in range(line - 1, 0, -1):
            for ok, to in ((row + s < line, row + s), (row >= s, row - s)):

                @pl.when(ok & plain(s, j))
                def _():
                    s_ac(part(2 * to + 1 - col, j), to, j).start()

        @pl.when(doubled(j))
        def _():
            @pl.when(row < line - 1)
            def _():
                s_ex(0, partner + 2, j, above).start()

            @pl.when(row > 0)
            def _():
                s_ex(1, partner - 2, j, below).start()

        @pl.when(lax.rem(j, 2) == 0)
        def _():
            s_ac(part(partner, j), row, j).start()

        fetch(j + total + depth)

    def cross_over(j):
        @pl.when(doubled(j))
        def _():
            acc[...] = part(partner, j)[...].astype(f32)

            @pl.when(row > 0)
            def _():
                s_ex(0, partner, j, above).wait_recv()
                acc[...] += piece(ex_buf, 0, j)[...].astype(f32)

            @pl.when(row < line - 1)
            def _():
                s_ex(1, partner, j, below).wait_recv()
                acc[...] += piece(ex_buf, 1, j)[...].astype(f32)

            flat(cross_buf, j)[...] = acc[...].astype(bf16)
            s_ac(flat(cross_buf, j), row, j).start()

    def pair_up(s, at, j):
        mine = part(2 * at + col, j)
        acc[...] = mine[...].astype(f32)

        @pl.when(plain(s, j))
        def _():
            s_ac(mine, at, j).wait_recv()
            acc[...] += piece(pair_buf, at, j)[...].astype(f32)

    def s_relay(s, j):
        @pl.when(row + s < line)
        def _():
            at = row + s
            pair_up(s, at, j)
            if s < line - 1:

                @pl.when(row > 0)
                def _():
                    s_up(at, j).wait_recv()
                    acc[...] += piece(line_buf, at, j)[...].astype(f32)

            piece(pair_buf, at, j)[...] = acc[...].astype(bf16)
            s_up(at, j).start()

        @pl.when(row >= s)
        def _():
            at = row - s
            landing = flat(top_buf, j) if s == 1 else piece(line_buf, at, j)
            pair_up(s, at, j)
            if s < line - 1:

                @pl.when(row < line - 1)
                def _():
                    s_dn(at, j, landing).wait_recv()
                    acc[...] += piece(line_buf, at, j)[...].astype(f32)

            piece(pair_buf, at, j)[...] = acc[...].astype(bf16)
            s_dn(at, j, landing).start()

    def finish(j):
        mine = part(me, j)
        s_ac(mine, row, j).wait_recv()
        acc[...] = mine[...].astype(f32) + piece(pair_buf, row, j)[...].astype(f32)

        @pl.when(row > 0)
        def _():
            s_up(row, j).wait_recv()
            acc[...] += piece(line_buf, row, j)[...].astype(f32)

        @pl.when(row < line - 1)
        def _():
            s_dn(row, j, flat(top_buf, j)).wait_recv()
            acc[...] += flat(top_buf, j)[...].astype(f32)

        out[j // chunks, :, columns(j)] = acc[...].astype(bf16)

    def sent(ref, sem):
        remote(ref, ref, sem, sum_r.at[0, 0], partner).wait_send()

    both, one = held.at[pl.ds(0, 2), me], held.at[0, me]

    def sent_sums(acs, exs):
        sent(both, acs.at[row])
        for s in range(1, line):
            for ok, at in ((row >= s, row - s), (row + s < line, row + s)):

                @pl.when(ok)
                def _():
                    sent(one if s == 1 else both, acs.at[at])

        @pl.when(row < line - 1)
        def _():
            sent(one, exs.at[0])

        @pl.when(row > 0)
        def _():
            sent(one, exs.at[1])

    def gather_sent():
        sent_sums(ac_s, ex_s)
        for s in range(line - 1):

            @pl.when((row >= s) & (row < line - 1))
            def _():
                sent(both, up_s.at[s])

            @pl.when((row + s < line) & (row > 0))
            def _():
                sent(both, dn_s.at[s])

    own = [
        pltpu.make_async_copy(ref, held.at[c, me], own_sem.at[c])
        for c, ref in enumerate((x_ref, d_ref))
    ]
    own += [
        pltpu.make_async_copy(src, dst, own_sem.at[8 + c])
        for c, (src, dst) in enumerate(((tenant_hbm, tenant_row), (slot_hbm, slot_row)))
    ]
    for copy in own:
        copy.start()
    barrier = pltpu.get_barrier_semaphore()
    for k in range(1, blocks):
        pl.semaphore_signal(
            barrier, inc=1, device_id={"blk": lax.rem(me + k, blocks)}, device_id_type=MESH
        )
    pl.semaphore_signal(barrier, inc=1, device_id={"grp": twin}, device_id_type=MESH)
    for k in range(1, pairs_g):
        to = 2 * lax.rem(high + k, pairs_g) + odd
        pl.semaphore_signal(barrier, inc=1, device_id={"grp": to}, device_id_type=MESH)
    for q in range(depth):
        fetch(q)
    tables = [
        pltpu.make_async_copy(src, dst, f_sem.at[i])
        for i, (src, dst) in enumerate(((bg, fac_g), (bu, fac_u), (ad, fac_d)))
    ]
    for copy in tables:
        copy.start()
    for copy in own:
        copy.wait()
    pl.semaphore_wait(barrier, blocks - 1 + pairs_g)
    g_own(0)

    for ref in (gate, up, gh, qa, qb, low):
        ref[...] = jnp.zeros_like(ref)
    pat[...] = (lax.rem(line_of(pat.shape, 1), rank) == line_of(pat.shape, 0)).astype(bf16)
    per_owner = factors // rank
    here = line_of((rows, 1), 0)
    source = (here // own_rows * groups + group) * own_rows + lax.rem(here, own_rows)
    every = tenant_row.shape[1]
    hit = line_of((1, every), 1) == source
    tenants = jnp.sum(jnp.where(hit, tenant_row[...].astype(f32), 0.0), axis=1, keepdims=True)
    tenant_col[...] = tenants.astype(jnp.int32)
    known = line_of((1, slot_row.shape[1]), 1) == tenant_col[...]
    slots = jnp.sum(jnp.where(known, slot_row[...].astype(f32), 0.0), axis=1, keepdims=True)
    local = slots.astype(jnp.int32) - me * per_owner
    slot_col[...] = local
    mine_col = ((local >= 0) & (local < per_owner)).astype(f32)
    first_i, second_i = line_of((rows, rows), 0), line_of((rows, rows), 1)
    same_i = first_i == second_i
    within = jnp.sum(jnp.where(first_i < second_i, mine_col, 0.0), axis=0, keepdims=True)
    mine_row = jnp.sum(jnp.where(same_i, mine_col, 0.0), axis=0, keepdims=True)
    local_row = jnp.sum(jnp.where(same_i, local.astype(f32), 0.0), axis=0, keepdims=True)
    tenant_line = jnp.sum(jnp.where(same_i, tenants, 0.0), axis=0, keepdims=True)
    chosen = (mine_row > 0.5) & (within == line_of((picks, 1), 0).astype(f32))
    choose[...] = chosen.astype(bf16)
    owned_at = jnp.sum(jnp.where(chosen, local_row + 1.0, 0.0), axis=1, keepdims=True) - 1.0
    own_slot[...] = owned_at.astype(jnp.int32)
    ids = line_of((rank, rows), 0)
    coarse = jnp.floor(tenant_line * (1.0 / 128.0))
    picked_row = jnp.sum(
        jnp.where(line_of((picks, rows), 0) == line_of((picks, rows), 1), owned_at, 0.0),
        axis=0,
        keepdims=True,
    )
    small[6 * rank :, :] = jnp.where(
        ids == 0,
        coarse,
        jnp.where(ids == 1, tenant_line - 128.0 * coarse, jnp.where(ids == 2, picked_row, 0.0)),
    ).astype(bf16)

    half = max(1, tiles // 2)

    def step(t, carry):
        def hook(at, body):
            pl.when(t == at)(body)

        @pl.when((t > 0) & (t < total))
        def _():
            g_own(t)

        for s in range(1, line):
            j = t - slack * s

            @pl.when((j >= 0) & (j < total))
            def _():
                g_relay(s, j)

        j = t - filled

        @pl.when((j >= 0) & (j < total))
        def _():
            take(j)

        @functools.partial(hook, x_end)
        def _():
            give[:rank, :] = pick(qa, 1.0)
            give[rank : 2 * rank, :] = pick(qb, 1.0)
            send_sum(0)
            share(0)
            qb[...] = jnp.zeros_like(qb)

        @functools.partial(hook, x_end + 2)
        def _():
            for copy in tables:
                copy.wait()
            take_sum(0)
            for k in range(2):
                coef[k] = dot(turned(k * rank, rank), pat[...])
            each_tile(0, half, ahead)

        @functools.partial(hook, x_end + 3)
        def _():
            each_tile(half, tiles, ahead)

        @functools.partial(hook, x_end + 4)
        def _():
            act_val, act_slope = silu_pair(gate[...])
            hid[...] = (act_val * up[...]).astype(bf16)
            gate[...] = act_val
            up[...] = up[...] * act_slope
            each_tile(0, half, low_out)

        @functools.partial(hook, x_end + 5)
        def _():
            each_tile(half, tiles, low_out)
            give[3 * rank : 4 * rank, :] = lowered(0, 1.0)
            send_sum(2)
            share(1)

        @functools.partial(hook, begin)
        def _():
            take_sum(2)
            owned(0, 3 * rank, adapter_scale)

        @functools.partial(hook, d_end)
        def _():
            give[2 * rank : 3 * rank, :] = pick(qb, adapter_scale)
            send_sum(1)
            share(2)

        @functools.partial(hook, d_end + 2)
        def _():
            take_sum(1)
            coef[2] = dot(turned(2 * rank, rank), pat[...])
            each_tile(0, tiles, back_in)
            grad_h = gh[...]
            gg[...] = (grad_h * up[...]).astype(bf16)
            gu[...] = (grad_h * gate[...]).astype(bf16)

        @functools.partial(hook, d_end + 3)
        def _():
            share(3)
            share(4)
            each_tile(0, half, back_out)

        @functools.partial(hook, d_end + 4)
        def _():
            each_tile(half, tiles, back_out)
            for k in range(2):
                give[(4 + k) * rank : (5 + k) * rank, :] = lowered(1 + k, adapter_scale)
            send_sum(3)

        @functools.partial(hook, begin + chunks)
        def _():
            gather_sent()
            take_sum(3)
            owned(1, 4 * rank, 1.0)
            owned(2, 5 * rank, 1.0)
            small[: 3 * rank, :] = sums[: 3 * rank, :]
            found = dot(sums[3 * rank :, :], choose[...], across)
            wide = (line_of((picks, rows), 0) == line_of((picks, rows), 1)).astype(bf16)
            small[3 * rank : 6 * rank, :] = dot(found.astype(bf16), wide).astype(bf16)
            share(5)

        for i, at in enumerate(
            (x_end + 8, x_end + 9, d_end + 8, d_end + 11, d_end + 12, d_end + 13)
        ):
            hook(at, functools.partial(pass_on, i))

        u = t - begin

        @pl.when((u >= 0) & (u < total))
        def _():
            make(u)

        j = t - begin - slack

        @pl.when((j >= 0) & (j < total))
        def _():
            cross_over(j)

        for s in range(line - 1, 0, -1):
            j = t - begin - slack * (line - s)

            @pl.when((j >= 0) & (j < total))
            def _():
                s_relay(s, j)

        j = t - begin - filled

        @pl.when(j >= 0)
        def _():
            finish(j)

        return carry

    lax.fori_loop(0, finish_step, step, 0)

    for c in range(len(spans)):
        for copy in spread(c):
            copy.wait_send()
    for i in range(len(pieces)):
        keep_copy(i).wait()
        twin_copy(i).wait()
        for k in range(1, pairs_g):
            far_copy(i, k).wait_send()
            hand_on(i, k).wait()

    sent_sums(bac_s, bex_s)
    for s in range(1, line):

        @pl.when(row + s < line)
        def _():
            sent(both, bup_s.at[row + s])

        @pl.when(row >= s)
        def _():
            sent(both, bdn_s.at[row - s])


def window_terms(blocks, groups, x, dy, gw, uw, dw, ag, au, bd, bg, bu, ad, tenants, slots, rank):
    line = blocks // 2
    own_rows, width = x.shape
    rows, units = blocks * own_rows, gw.shape[1]
    factors, count = ag.shape[0], bg.shape[0]
    picks = 2 * own_rows
    chunks = 8
    step_width = width // chunks
    depth = 3
    dma = pltpu.SemaphoreType.DMA
    vmem = pltpu.VMEM
    anywhere, inside = pl.BlockSpec(memory_space=pl.ANY), pl.BlockSpec(memory_space=vmem)
    held = [
        ((3, blocks, own_rows, width), bf16),
        ((2, line, own_rows, width), bf16),
        ((2, line, own_rows, width), bf16),
        ((2, own_rows, width), bf16),
        ((2, 2, own_rows, width), bf16),
        ((2, own_rows, width), bf16),
        ((own_rows, step_width), f32),
        ((rows, units), f32),
        ((rows, units), f32),
        ((rows, units), f32),
        ((picks, factors), f32),
        ((picks, factors), f32),
        ((picks, width), bf16),
        ((picks, width), bf16),
        ((rows, units), bf16),
        ((rows, units), bf16),
        ((rows, units), bf16),
        ((3, rows, factors), bf16),
        ((depth, step_width, units), bf16),
        ((depth, step_width, units), bf16),
        ((depth, max(units, factors), step_width), bf16),
        ((depth, factors, step_width), bf16),
        ((count, units), bf16),
        ((count, units), bf16),
        ((count, units), bf16),
        ((rank, lanes), bf16),
        ((picks, rows), bf16),
        ((picks, 1), jnp.int32),
        ((rows, 1), jnp.int32),
        ((rows, 1), jnp.int32),
        ((6 * rank, rows), bf16),
        ((blocks, 6 * rank, rows), bf16),
        ((6 * rank, rows), bf16),
        ((3, rows, lanes), f32),
        ((3, rows, lanes), f32),
        ((7 * rank, rows), bf16),
        (tenants.shape, jnp.int32),
        (slots.shape, jnp.int32),
    ]
    used = sum(math.prod(shape) * jnp.dtype(kind).itemsize for shape, kind in held) + 6 * 2**20
    roomy = used < 7 * vmem_grant // 8
    every = lambda *shape: jax.ShapeDtypeStruct((groups,) + shape, bf16)
    return pl.pallas_call(
        functools.partial(window_kernel, blocks, groups, rank, chunks),
        out_shape=(
            jax.ShapeDtypeStruct((2, own_rows, width), bf16),
            every(picks, width),
            every(picks, width),
            every(rows, units),
            every(rows, units),
            every(rows, units),
            every(7 * rank, rows),
        ),
        in_specs=[pl.BlockSpec(memory_space=pltpu.HBM)] * 13,
        out_specs=(inside,) + (inside if roomy else anywhere,) * 6,
        scratch_shapes=[vmem(shape, kind) for shape, kind in held]
        + [
            dma((10,)),
            dma((4, depth)),
            dma((3,)),
            dma((3, line)),
            dma((3, line, 2 * chunks)),
            dma((3, line)),
            dma((3, line, 2 * chunks)),
            dma((2, 2)),
            dma((2, 2, 2 * chunks)),
            dma((4, blocks)),
            dma((4, blocks)),
            dma((3, 6, groups // 2)),
            dma((3, 6, groups // 2)),
        ],
        compiler_params=pltpu.CompilerParams(
            collective_id=0,
            has_side_effects=True,
            vmem_limit_bytes=used if roomy else vmem_grant,
        ),
        cost_estimate=pl.CostEstimate(
            flops=12 * rows * width * (units + factors) + 12 * rows * count * units,
            bytes_accessed=12 * width * (units + factors) + 6 * count * units,
            transcendentals=rows * units,
        ),
        name="window_terms",
    )(x, dy, gw, uw, dw, ag, au, bd, bg, bu, ad, tenants, slots)


def grads_kernel(
    rank,
    small,
    x,
    d,
    hid,
    gg,
    gu,
    got,
    o_m,
    o_i,
    o_ag,
    o_au,
    o_bd,
    o_bg,
    o_bu,
    o_ad,
    slot_out,
    tenant_out,
    row_sem,
    slot_sem,
    tenant_sem,
):
    groups, picks, width = x.shape
    rows, units = hid.shape[1:]
    own = slot_out.shape[1]
    every = tenant_out.shape[1]
    tall = min(256, every)
    wide = min(1024, width)
    results = [
        pltpu.make_async_copy(got.at[i], ref, row_sem.at[i]) for i, ref in enumerate((o_m, o_i))
    ]
    for copy in results:
        copy.start()
    group = lax.axis_index("grp")
    ids = [small[q, 6 * rank :, :].astype(f32) for q in range(groups)]
    slot = jnp.concatenate([part[2:3, :picks] for part in ids], axis=1)
    mark = jnp.concatenate([128.0 * part[0:1] + part[1:2] for part in ids], axis=1)
    mask = (line_of((own, 1), 0) // rank + group * (own // rank)).astype(f32) == slot
    weights = []
    for k, scale in ((0, adapter_scale), (1, 1.0), (2, 1.0)):
        at = (3 + k) * rank
        value = jnp.concatenate([small[q, at : at + rank, :picks] for q in range(groups)], axis=1)
        value = jnp.concatenate([value.astype(f32)] * (own // rank), axis=0)
        weights.append(jnp.where(mask, scale * value, 0.0).astype(bf16))
    slot_refs = (o_bd, o_ag, o_au)

    def slot_step(i, carry):
        at = pl.ds(pl.multiple_of(i * wide, wide), wide)
        value_x = x[:, :, at].reshape(groups * picks, wide)
        value_d = d[:, :, at].reshape(groups * picks, wide)
        for k, value in enumerate((value_d, value_x, value_x)):
            slot_out[k, :, at] = dot(weights[k], value)
            pltpu.make_async_copy(
                slot_out.at[k, :, at], slot_refs[k].at[:, at], slot_sem.at[k]
            ).start()
        return carry

    lax.fori_loop(0, width // wide, slot_step, 0)
    given = []
    for k, scale in enumerate((adapter_scale, adapter_scale, 1.0)):
        value = jnp.concatenate(
            [small[q, k * rank : (k + 1) * rank, :] for q in range(groups)], axis=1
        )
        given.append(scale * value.astype(f32))
    tenant_refs = (o_bg, o_bu, o_ad)
    values = (gg, gu, hid)

    def tenant_step(i, carry):
        at = pl.ds(pl.multiple_of(i * tall, tall), tall)
        first = group * (every // rank) + i * (tall // rank)
        here = (line_of((tall, 1), 0) // rank + first).astype(f32) == mark
        for k in range(3):
            value = jnp.concatenate([given[k]] * (tall // rank), axis=0)
            weight = jnp.where(here, value, 0.0).astype(bf16)
            tenant_out[k, at, :] = dot(weight, values[k][...].reshape(groups * rows, units))
            pltpu.make_async_copy(
                tenant_out.at[k, at, :], tenant_refs[k].at[at, :], tenant_sem.at[k]
            ).start()
        return carry

    lax.fori_loop(0, every // tall, tenant_step, 0)
    for copy in results:
        copy.wait()
    for k in range(3):
        pltpu.make_async_copy(slot_out.at[k], slot_refs[k], slot_sem.at[k]).wait()
        pltpu.make_async_copy(tenant_out.at[k], tenant_refs[k], tenant_sem.at[k]).wait()


def outer_sums(rank, small, x, d, hid, gg, gu, got, slots, tenants):
    width, units = x.shape[2], hid.shape[2]
    own, every = slots * rank, tenants * rank
    dma = pltpu.SemaphoreType.DMA
    row = jax.ShapeDtypeStruct(got.shape[1:], bf16)
    found = pl.pallas_call(
        functools.partial(grads_kernel, rank),
        out_shape=(row,) * 2
        + (jax.ShapeDtypeStruct((own, width), f32),) * 3
        + (jax.ShapeDtypeStruct((every, units), f32),) * 3,
        in_specs=[pl.BlockSpec(memory_space=pltpu.VMEM)] * 7,
        out_specs=(pl.BlockSpec(memory_space=pl.ANY),) * 8,
        scratch_shapes=[
            pltpu.VMEM((3, own, width), f32),
            pltpu.VMEM((3, every, units), f32),
            dma((2,)),
            dma((3,)),
            dma((3,)),
        ],
        compiler_params=pltpu.CompilerParams(vmem_limit_bytes=40 * 2**20),
        name="outer_sums",
    )(small, x, d, hid, gg, gu, got)
    return (*found[:2], *(part.reshape(-1, rank, part.shape[1]) for part in found[2:]))


def local(
    tokens,
    cotangent,
    gate_weight,
    up_weight,
    down_weight,
    a_gate,
    a_up,
    down_output_factors,
    b_gate,
    b_up,
    a_down,
    tenant_of_row,
    adapter_slot,
):
    width = tokens.shape[1]
    blocks = lax.axis_size("blk")
    groups = lax.axis_size("grp")
    per_owner, rank = a_gate.shape[:2]
    tenants, _, units = b_gate.shape
    slot_factors = [f.reshape(per_owner * rank, width) for f in (a_gate, a_up, down_output_factors)]
    tenant_factors = [f.reshape(tenants * rank, units) for f in (b_gate, b_up, a_down)]
    result, all_x, all_d, hid, gg, gu, small = window_terms(
        blocks,
        groups,
        tokens,
        cotangent,
        gate_weight,
        up_weight,
        down_weight,
        *slot_factors,
        *tenant_factors,
        tenant_of_row[None, :],
        adapter_slot[None, :],
        rank,
    )
    return outer_sums(
        rank, small, all_x, all_d, hid, gg, gu, result, per_owner // groups, tenants // groups
    )


def solution(mesh):
    placed = (
        P(("blk", "grp"), None),
        P(("blk", "grp"), None),
        P(None, "blk"),
        P(None, "blk"),
        P("blk", None),
        P("blk", None, None),
        P("blk", None, None),
        P("blk", None, None),
        P(None, None, "blk"),
        P(None, None, "blk"),
        P(None, None, "blk"),
        P(),
        P(),
    )
    return jax.shard_map(
        local,
        mesh=mesh,
        in_specs=placed,
        out_specs=(
            P(("blk", "grp"), None),
            P(("blk", "grp"), None),
            P(("blk", "grp"), None, None),
            P(("blk", "grp"), None, None),
            P(("blk", "grp"), None, None),
            P("grp", None, "blk"),
            P("grp", None, "blk"),
            P("grp", None, "blk"),
        ),
        check_vma=False,
    )
```

```python
import functools
import math

import jax
import jax.numpy as jnp
from jax import lax
from jax.experimental import pallas as pl
from jax.experimental.pallas import tpu as pltpu
from jax.sharding import PartitionSpec as P

MESH = pl.DeviceIdType.MESH
bf16 = jnp.bfloat16
vmem_grant = 60 * 2**20
f32 = jnp.float32
slack = 2


def remote(src, dst, send, recv, to):
    return pltpu.make_async_remote_copy(
        src_ref=src,
        dst_ref=dst,
        send_sem=send,
        recv_sem=recv,
        device_id={"blk": to},
        device_id_type=MESH,
    )


def place(blocks):
    me = lax.axis_index("blk")
    line = blocks // 2
    row = me // 2
    col = me - 2 * row
    partner = me + 1 - 2 * col
    return me, line, row, col, partner


adapter_scale = 2.0


def silu_pair(gate_in):
    sigmoid_val = jax.nn.sigmoid(gate_in)
    return (gate_in * sigmoid_val, sigmoid_val * (1.0 + gate_in * (1.0 - sigmoid_val)))


def dot(a, b, dims=((1,), (0,))):
    return lax.dot_general(a, b, (dims, ((), ())), preferred_element_type=f32)


across = ((1,), (1,))
lanes = 128


def fold(value):
    kept = value[:, :lanes]
    for k in range(1, value.shape[1] // lanes):
        kept = kept + value[:, k * lanes : (k + 1) * lanes]
    return kept


def repeat(value, width):
    return jnp.concatenate([value] * (width // lanes), axis=1)


def line_of(shape, axis):
    return lax.broadcasted_iota(jnp.int32, shape, axis)


def window_kernel(
    blocks,
    groups,
    rank,
    chunks,
    x_ref,
    d_ref,
    gw,
    uw,
    dw,
    ag,
    au,
    bd,
    bg,
    bu,
    ad,
    tenant_hbm,
    slot_hbm,
    out,
    all_x,
    all_d,
    all_h,
    all_g,
    all_u,
    all_small,
    held,
    pair_buf,
    line_buf,
    top_buf,
    ex_buf,
    cross_buf,
    acc,
    gate,
    up,
    gh,
    qa,
    qb,
    own_x,
    own_d,
    hid,
    gg,
    gu,
    extra,
    wide_g,
    wide_u,
    tall_a,
    tall_b,
    fac_g,
    fac_u,
    fac_d,
    pat,
    choose,
    own_slot,
    tenant_col,
    slot_col,
    give,
    land,
    sums,
    low,
    coef,
    small,
    tenant_row,
    slot_row,
    own_sem,
    w_sem,
    f_sem,
    g_sems,
    r_sems,
    s_sems,
    t_sems,
    x_sems,
    y_sems,
    sum_s,
    sum_r,
    e_sems,
    v_sems,
):
    me, line, row, col, partner = place(blocks)
    above, below = me + 2, me - 2
    own_rows, width = x_ref.shape
    rows = blocks * own_rows
    step_width = width // chunks
    total = 2 * chunks
    depth = wide_g.shape[0]
    units, factors = dw.shape[0], bd.shape[0]
    count = bg.shape[0]
    tile = min(1024, count)
    tiles = count // tile
    picks = choose.shape[0]
    group = lax.axis_index("grp")
    pairs_g, high = groups // 2, group // 2
    odd = group - 2 * high
    twin = group + 1 - 2 * odd
    filled = slack * line
    x_end = chunks - 1 + filled
    d_end = total - 1 + filled
    begin = d_end - 1
    finish_step = begin + total + filled

    up_s, up_r, dn_s, dn_r = g_sems.at[0], r_sems.at[0], g_sems.at[1], r_sems.at[1]
    ac_s, ac_r = g_sems.at[2], r_sems.at[2]
    ex_s, ex_r = x_sems.at[0], y_sems.at[0]
    bup_s, bup_r, bdn_s, bdn_r = s_sems.at[0], t_sems.at[0], s_sems.at[1], t_sems.at[1]
    bac_s, bac_r = s_sems.at[2], t_sems.at[2]
    bex_s, bex_r = x_sems.at[1], y_sems.at[1]

    def columns(j):
        return pl.ds(pl.multiple_of(lax.rem(j, chunks) * step_width, step_width), step_width)

    def doubled(j):
        return lax.rem(j, 2) == 1

    def plain(s, j):
        return lax.rem(j, 2) == 0 if s == 1 else j >= 0

    def loads(q, four):
        at, k = columns(q), lax.rem(q, depth)
        if four:
            moves = (
                (ag.at[:, at], tall_a.at[k, pl.ds(0, factors)]),
                (au.at[:, at], tall_b.at[k]),
                (gw.at[at, :], wide_g.at[k]),
                (uw.at[at, :], wide_u.at[k]),
            )
        else:
            moves = (
                (dw.at[:, at], tall_a.at[k, pl.ds(0, units)]),
                (bd.at[:, at], tall_b.at[k]),
            )
        return [
            pltpu.make_async_copy(src, dst, w_sem.at[i, k]) for i, (src, dst) in enumerate(moves)
        ]

    def fetch(q):
        outer = (q < chunks) | (q >= 3 * chunks)

        @pl.when(outer & (q < 4 * chunks))
        def _():
            for copy in loads(q, True):
                copy.start()

        @pl.when(jnp.logical_not(outer))
        def _():
            for copy in loads(q, False):
                copy.start()

    def held_part(block, j):
        return held.at[j // chunks, block, :, columns(j)]

    def g_up(block, s, j):
        ref = held_part(block, j)
        return remote(ref, ref, up_s.at[s], up_r.at[s, j], above)

    def g_dn(block, s, j):
        ref = held_part(block, j)
        return remote(ref, ref, dn_s.at[s], dn_r.at[s, j], below)

    def g_ac(at, j):
        ref = held_part(2 * at + col, j)
        return remote(ref, ref, ac_s.at[at], ac_r.at[at, j], partner)

    def g_ac_arrival(at, j):
        ref = held_part(2 * at + 1 - col, j)
        return remote(ref, ref, ac_s.at[at], ac_r.at[at, j], partner)

    def g_ex(direction, block, j, to):
        ref = held_part(block, j)
        return remote(ref, ref, ex_s.at[direction], ex_r.at[direction, j], to)

    def g_own(j):
        g_ac(row, j).start()

        @pl.when(row < line - 1)
        def _():
            g_up(me, 0, j).start()

        @pl.when(row > 0)
        def _():
            g_dn(me, 0, j).start()

    def g_relay(s, j):
        @pl.when(row >= s)
        def _():
            block = me - 2 * s
            g_up(block, s - 1, j).wait_recv()
            if s < line - 1:

                @pl.when(row < line - 1)
                def _():
                    g_up(block, s, j).start()

            @pl.when(plain(s, j))
            def _():
                g_ac(row - s, j).start()

        @pl.when(row + s < line)
        def _():
            block = me + 2 * s
            g_dn(block, s - 1, j).wait_recv()
            if s < line - 1:

                @pl.when(row > 0)
                def _():
                    g_dn(block, s, j).start()

            @pl.when(plain(s, j))
            def _():
                g_ac(row + s, j).start()

        if s == 1:
            g_ac_arrival(row, j).wait_recv()

            @pl.when(doubled(j))
            def _():
                @pl.when(row < line - 1)
                def _():
                    g_ex(0, partner, j, above).start()

                @pl.when(row > 0)
                def _():
                    g_ex(1, partner, j, below).start()

    def g_arrive(j):
        for s in range(1, line):

            @pl.when(plain(s, j) & (row >= s))
            def _():
                g_ac_arrival(row - s, j).wait_recv()

            @pl.when(plain(s, j) & (row + s < line))
            def _():
                g_ac_arrival(row + s, j).wait_recv()

        @pl.when(doubled(j) & (row > 0))
        def _():
            g_ex(0, partner - 2, j, above).wait_recv()

        @pl.when(doubled(j) & (row < line - 1))
        def _():
            g_ex(1, partner + 2, j, below).wait_recv()

    def take(j):
        g_arrive(j)
        at, k = columns(j), lax.rem(j, depth)

        @pl.when(j < chunks)
        def _():
            for copy in loads(j, True):
                copy.wait()
            value = held[0, :, :, at].reshape(rows, step_width)
            gate[...] += dot(value, wide_g[k])
            up[...] += dot(value, wide_u[k])
            mine = dot(choose[...], value).astype(bf16)
            own_x[:, at] = mine
            qa[...] += dot(mine, tall_a[k, :factors], across)
            qb[...] += dot(mine, tall_b[k], across)

        @pl.when(j >= chunks)
        def _():
            for copy in loads(j, False):
                copy.wait()
            value = held[1, :, :, at].reshape(rows, step_width)
            gh[...] += dot(value, tall_a[k, :units], across)
            mine = dot(choose[...], value).astype(bf16)
            own_d[:, at] = mine
            qb[...] += dot(mine, tall_b[k], across)

        fetch(j + depth)

    spans = ((0, 2 * rank), (2 * rank, rank), (3 * rank, rank), (4 * rank, 2 * rank))

    def spread(c):
        first, size = spans[c]
        return [
            remote(
                give.at[pl.ds(first, size)],
                land.at[k, pl.ds(first, size)],
                sum_s.at[c, k],
                sum_r.at[c, k],
                lax.rem(me + k, blocks),
            )
            for k in range(1, blocks)
        ]

    def send_sum(c):
        for copy in spread(c):
            copy.start()

    def take_sum(c):
        first, size = spans[c]
        value = give[first : first + size, :].astype(f32)
        for k, copy in enumerate(spread(c)):
            copy.wait_recv()
            value = value + land[k + 1, first : first + size, :].astype(f32)
        sums[first : first + size, :] = value.astype(bf16)

    def turned(first, size):
        same = line_of((rows, rows), 0) == line_of((rows, rows), 1)
        return dot(same.astype(bf16), sums[first : first + size, :], across).astype(bf16)

    def pick(ref, scale):
        mask = own_slot[...] == line_of((1, factors), 1) // rank
        kept = fold(jnp.where(mask, scale * ref[...], 0.0)).astype(bf16)
        found = dot(pat[...], kept, across).astype(bf16)
        return dot(found, choose[...]).astype(bf16)

    def tenant_mask(i):
        return tenant_col[...] == line_of((1, tile), 1) // rank + i * (tile // rank)

    def each_tile(first, last, body):
        def run(i, carry):
            body(i, tenant_mask(i), pl.ds(pl.multiple_of(i * tile, tile), tile))
            return carry

        lax.fori_loop(first, last, run, 0)

    def add_low_rank(sum_ref, fac, k, scale, mask, at):
        wide = jnp.where(mask, repeat(coef[k], tile), 0.0).astype(bf16)
        sum_ref[...] += scale * dot(wide, fac[at, :])

    def reduce_low_rank(values, fac, k, mask, at):
        full = dot(values[...], fac[at, :], across)
        low[k] += fold(jnp.where(mask, full, 0.0))

    def ahead(i, mask, at):
        add_low_rank(gate, fac_g, 0, adapter_scale, mask, at)
        add_low_rank(up, fac_u, 1, adapter_scale, mask, at)

    def back_in(i, mask, at):
        add_low_rank(gh, fac_d, 2, 1.0, mask, at)

    def low_out(i, mask, at):
        reduce_low_rank(hid, fac_d, 0, mask, at)

    def back_out(i, mask, at):
        reduce_low_rank(gg, fac_g, 1, mask, at)
        reduce_low_rank(gu, fac_u, 2, mask, at)

    def lowered(k, scale):
        return (scale * dot(pat[...], low[k].astype(bf16), across)).astype(bf16)

    def owned(k, first, scale):
        mask = slot_col[...] == line_of((1, factors), 1) // rank
        given = repeat(dot(turned(first, rank), pat[...]), factors)
        extra[k] = (scale * jnp.where(mask, given, 0.0)).astype(bf16)

    pieces = (
        (own_x, all_x),
        (hid, all_h),
        (own_d, all_d),
        (gg, all_g),
        (gu, all_u),
        (small, all_small),
    )

    def to_group(src, dst, send, recv, to):
        return pltpu.make_async_remote_copy(
            src_ref=src,
            dst_ref=dst,
            send_sem=send,
            recv_sem=recv,
            device_id={"grp": to},
            device_id_type=MESH,
        )

    def keep_copy(i):
        src, dst = pieces[i]
        return pltpu.make_async_copy(src, dst.at[group], own_sem.at[2 + i])

    def twin_copy(i):
        src, dst = pieces[i]
        return to_group(src, dst.at[group], e_sems.at[0, i, 0], v_sems.at[0, i, 0], twin)

    def far_copy(i, k):
        src, dst = pieces[i]
        to = 2 * lax.rem(high + k, pairs_g) + odd
        return to_group(src, dst.at[group], e_sems.at[1, i, k], v_sems.at[1, i, k], to)

    def hand_on(i, k):
        ref = pieces[i][1].at[2 * lax.rem(high + pairs_g - k, pairs_g) + odd]
        return to_group(ref, ref, e_sems.at[2, i, k], v_sems.at[2, i, k], twin)

    def share(i):
        for k in range(1, pairs_g):
            far_copy(i, k).start()
        twin_copy(i).start()
        keep_copy(i).start()

    def pass_on(i):
        for k in range(1, pairs_g):
            far_copy(i, k).wait_recv()
            hand_on(i, k).start()

    def part(block, j):
        return held.at[lax.rem(2 + j // chunks, 3), block, :, columns(j)]

    def piece(buf, at, j):
        return buf.at[j // chunks, at, :, columns(j)]

    def flat(buf, j):
        return buf.at[j // chunks, :, columns(j)]

    def s_ac(src, at, j):
        return remote(src, piece(pair_buf, at, j), bac_s.at[at], bac_r.at[at, j], partner)

    def s_up(at, j):
        return remote(
            piece(pair_buf, at, j), piece(line_buf, at, j), bup_s.at[at], bup_r.at[at, j], above
        )

    def s_dn(at, j, landing):
        return remote(piece(pair_buf, at, j), landing, bdn_s.at[at], bdn_r.at[at, j], below)

    def s_ex(direction, block, j, to):
        return remote(
            part(block, j),
            piece(ex_buf, direction, j),
            bex_s.at[direction],
            bex_r.at[direction, j],
            to,
        )

    def make(j):
        at, k = columns(j), lax.rem(j + total, depth)

        @pl.when(j < chunks)
        def _():
            for copy in loads(j + total, False):
                copy.wait()
            value = dot(hid[...], tall_a[k, :units]) + dot(extra[0], tall_b[k])
            held[2, :, :, at] = value.astype(bf16).reshape(blocks, own_rows, step_width)

        @pl.when(j >= chunks)
        def _():
            for copy in loads(j + total, True):
                copy.wait()
            value = (
                dot(gg[...], wide_g[k], across)
                + dot(gu[...], wide_u[k], across)
                + dot(extra[1], tall_a[k, :factors])
                + dot(extra[2], tall_b[k])
            )
            held[0, :, :, at] = value.astype(bf16).reshape(blocks, own_rows, step_width)

        for s in range(line - 1, 0, -1):
            for ok, to in ((row + s < line, row + s), (row >= s, row - s)):

                @pl.when(ok & plain(s, j))
                def _():
                    s_ac(part(2 * to + 1 - col, j), to, j).start()

        @pl.when(doubled(j))
        def _():
            @pl.when(row < line - 1)
            def _():
                s_ex(0, partner + 2, j, above).start()

            @pl.when(row > 0)
            def _():
                s_ex(1, partner - 2, j, below).start()

        @pl.when(lax.rem(j, 2) == 0)
        def _():
            s_ac(part(partner, j), row, j).start()

        fetch(j + total + depth)

    def cross_over(j):
        @pl.when(doubled(j))
        def _():
            acc[...] = part(partner, j)[...].astype(f32)

            @pl.when(row > 0)
            def _():
                s_ex(0, partner, j, above).wait_recv()
                acc[...] += piece(ex_buf, 0, j)[...].astype(f32)

            @pl.when(row < line - 1)
            def _():
                s_ex(1, partner, j, below).wait_recv()
                acc[...] += piece(ex_buf, 1, j)[...].astype(f32)

            flat(cross_buf, j)[...] = acc[...].astype(bf16)
            s_ac(flat(cross_buf, j), row, j).start()

    def pair_up(s, at, j):
        mine = part(2 * at + col, j)
        acc[...] = mine[...].astype(f32)

        @pl.when(plain(s, j))
        def _():
            s_ac(mine, at, j).wait_recv()
            acc[...] += piece(pair_buf, at, j)[...].astype(f32)

    def s_relay(s, j):
        @pl.when(row + s < line)
        def _():
            at = row + s
            pair_up(s, at, j)
            if s < line - 1:

                @pl.when(row > 0)
                def _():
                    s_up(at, j).wait_recv()
                    acc[...] += piece(line_buf, at, j)[...].astype(f32)

            piece(pair_buf, at, j)[...] = acc[...].astype(bf16)
            s_up(at, j).start()

        @pl.when(row >= s)
        def _():
            at = row - s
            landing = flat(top_buf, j) if s == 1 else piece(line_buf, at, j)
            pair_up(s, at, j)
            if s < line - 1:

                @pl.when(row < line - 1)
                def _():
                    s_dn(at, j, landing).wait_recv()
                    acc[...] += piece(line_buf, at, j)[...].astype(f32)

            piece(pair_buf, at, j)[...] = acc[...].astype(bf16)
            s_dn(at, j, landing).start()

    def finish(j):
        mine = part(me, j)
        s_ac(mine, row, j).wait_recv()
        acc[...] = mine[...].astype(f32) + piece(pair_buf, row, j)[...].astype(f32)

        @pl.when(row > 0)
        def _():
            s_up(row, j).wait_recv()
            acc[...] += piece(line_buf, row, j)[...].astype(f32)

        @pl.when(row < line - 1)
        def _():
            s_dn(row, j, flat(top_buf, j)).wait_recv()
            acc[...] += flat(top_buf, j)[...].astype(f32)

        out[j // chunks, :, columns(j)] = acc[...].astype(bf16)

    def sent(ref, sem):
        remote(ref, ref, sem, sum_r.at[0, 0], partner).wait_send()

    both, one = held.at[pl.ds(0, 2), me], held.at[0, me]

    def sent_sums(acs, exs):
        sent(both, acs.at[row])
        for s in range(1, line):
            for ok, at in ((row >= s, row - s), (row + s < line, row + s)):

                @pl.when(ok)
                def _():
                    sent(one if s == 1 else both, acs.at[at])

        @pl.when(row < line - 1)
        def _():
            sent(one, exs.at[0])

        @pl.when(row > 0)
        def _():
            sent(one, exs.at[1])

    def gather_sent():
        sent_sums(ac_s, ex_s)
        for s in range(line - 1):

            @pl.when((row >= s) & (row < line - 1))
            def _():
                sent(both, up_s.at[s])

            @pl.when((row + s < line) & (row > 0))
            def _():
                sent(both, dn_s.at[s])

    own = [
        pltpu.make_async_copy(ref, held.at[c, me], own_sem.at[c])
        for c, ref in enumerate((x_ref, d_ref))
    ]
    own += [
        pltpu.make_async_copy(src, dst, own_sem.at[8 + c])
        for c, (src, dst) in enumerate(((tenant_hbm, tenant_row), (slot_hbm, slot_row)))
    ]
    for copy in own:
        copy.start()
    barrier = pltpu.get_barrier_semaphore()
    for k in range(1, blocks):
        pl.semaphore_signal(
            barrier, inc=1, device_id={"blk": lax.rem(me + k, blocks)}, device_id_type=MESH
        )
    pl.semaphore_signal(barrier, inc=1, device_id={"grp": twin}, device_id_type=MESH)
    for k in range(1, pairs_g):
        to = 2 * lax.rem(high + k, pairs_g) + odd
        pl.semaphore_signal(barrier, inc=1, device_id={"grp": to}, device_id_type=MESH)
    for q in range(depth):
        fetch(q)
    tables = [
        pltpu.make_async_copy(src, dst, f_sem.at[i])
        for i, (src, dst) in enumerate(((bg, fac_g), (bu, fac_u), (ad, fac_d)))
    ]
    for copy in tables:
        copy.start()
    for copy in own:
        copy.wait()
    pl.semaphore_wait(barrier, blocks - 1 + pairs_g)
    lead = min(2 * slack, total)
    for j in range(lead):
        g_own(j)

    for ref in (gate, up, gh, qa, qb, low):
        ref[...] = jnp.zeros_like(ref)
    pat[...] = (lax.rem(line_of(pat.shape, 1), rank) == line_of(pat.shape, 0)).astype(bf16)
    per_owner = factors // rank
    here = line_of((rows, 1), 0)
    source = (here // own_rows * groups + group) * own_rows + lax.rem(here, own_rows)
    every = tenant_row.shape[1]
    hit = line_of((1, every), 1) == source
    tenants = jnp.sum(jnp.where(hit, tenant_row[...].astype(f32), 0.0), axis=1, keepdims=True)
    tenant_col[...] = tenants.astype(jnp.int32)
    known = line_of((1, slot_row.shape[1]), 1) == tenant_col[...]
    slots = jnp.sum(jnp.where(known, slot_row[...].astype(f32), 0.0), axis=1, keepdims=True)
    local = slots.astype(jnp.int32) - me * per_owner
    slot_col[...] = local
    mine_col = ((local >= 0) & (local < per_owner)).astype(f32)
    first_i, second_i = line_of((rows, rows), 0), line_of((rows, rows), 1)
    same_i = first_i == second_i
    within = jnp.sum(jnp.where(first_i < second_i, mine_col, 0.0), axis=0, keepdims=True)
    mine_row = jnp.sum(jnp.where(same_i, mine_col, 0.0), axis=0, keepdims=True)
    local_row = jnp.sum(jnp.where(same_i, local.astype(f32), 0.0), axis=0, keepdims=True)
    tenant_line = jnp.sum(jnp.where(same_i, tenants, 0.0), axis=0, keepdims=True)
    chosen = (mine_row > 0.5) & (within == line_of((picks, 1), 0).astype(f32))
    choose[...] = chosen.astype(bf16)
    owned_at = jnp.sum(jnp.where(chosen, local_row + 1.0, 0.0), axis=1, keepdims=True) - 1.0
    own_slot[...] = owned_at.astype(jnp.int32)
    ids = line_of((rank, rows), 0)
    coarse = jnp.floor(tenant_line * (1.0 / 128.0))
    picked_row = jnp.sum(
        jnp.where(line_of((picks, rows), 0) == line_of((picks, rows), 1), owned_at, 0.0),
        axis=0,
        keepdims=True,
    )
    small[6 * rank :, :] = jnp.where(
        ids == 0,
        coarse,
        jnp.where(ids == 1, tenant_line - 128.0 * coarse, jnp.where(ids == 2, picked_row, 0.0)),
    ).astype(bf16)

    half = max(1, tiles // 2)

    def step(t, carry):
        def hook(at, body):
            pl.when(t == at)(body)

        @pl.when((t >= lead) & (t < total))
        def _():
            g_own(t)

        for s in range(1, line):
            j = t - slack * s

            @pl.when((j >= 0) & (j < total))
            def _():
                g_relay(s, j)

        j = t - filled

        @pl.when((j >= 0) & (j < total))
        def _():
            take(j)

        @functools.partial(hook, x_end)
        def _():
            give[:rank, :] = pick(qa, 1.0)
            give[rank : 2 * rank, :] = pick(qb, 1.0)
            send_sum(0)
            share(0)
            qb[...] = jnp.zeros_like(qb)

        @functools.partial(hook, x_end + 2)
        def _():
            for copy in tables:
                copy.wait()
            take_sum(0)
            for k in range(2):
                coef[k] = dot(turned(k * rank, rank), pat[...])
            each_tile(0, half, ahead)

        @functools.partial(hook, x_end + 3)
        def _():
            each_tile(half, tiles, ahead)

        @functools.partial(hook, x_end + 4)
        def _():
            act_val, act_slope = silu_pair(gate[...])
            hid[...] = (act_val * up[...]).astype(bf16)
            gate[...] = act_val
            up[...] = up[...] * act_slope
            each_tile(0, half, low_out)

        @functools.partial(hook, x_end + 5)
        def _():
            each_tile(half, tiles, low_out)
            give[3 * rank : 4 * rank, :] = lowered(0, 1.0)
            send_sum(2)
            share(1)

        @functools.partial(hook, begin)
        def _():
            take_sum(2)
            owned(0, 3 * rank, adapter_scale)

        @functools.partial(hook, d_end)
        def _():
            give[2 * rank : 3 * rank, :] = pick(qb, adapter_scale)
            send_sum(1)
            share(2)

        @functools.partial(hook, d_end + 2)
        def _():
            take_sum(1)
            coef[2] = dot(turned(2 * rank, rank), pat[...])
            each_tile(0, half, back_in)

        @functools.partial(hook, d_end + 3)
        def _():
            each_tile(half, tiles, back_in)
            grad_h = gh[...]
            gg[...] = (grad_h * up[...]).astype(bf16)
            gu[...] = (grad_h * gate[...]).astype(bf16)
            share(3)
            share(4)

        @functools.partial(hook, d_end + 4)
        def _():
            each_tile(0, half, back_out)

        @functools.partial(hook, d_end + 5)
        def _():
            each_tile(half, tiles, back_out)
            for k in range(2):
                give[(4 + k) * rank : (5 + k) * rank, :] = lowered(1 + k, adapter_scale)
            send_sum(3)

        @functools.partial(hook, begin + chunks)
        def _():
            gather_sent()
            take_sum(3)
            owned(1, 4 * rank, 1.0)
            owned(2, 5 * rank, 1.0)
            small[: 3 * rank, :] = sums[: 3 * rank, :]
            found = dot(sums[3 * rank :, :], choose[...], across)
            wide = (line_of((picks, rows), 0) == line_of((picks, rows), 1)).astype(bf16)
            small[3 * rank : 6 * rank, :] = dot(found.astype(bf16), wide).astype(bf16)
            share(5)

        for i, at in enumerate(
            (x_end + 8, x_end + 9, d_end + 8, d_end + 11, d_end + 12, d_end + 13)
        ):
            hook(at, functools.partial(pass_on, i))

        u = t - begin

        @pl.when((u >= 0) & (u < total))
        def _():
            make(u)

        j = t - begin - slack

        @pl.when((j >= 0) & (j < total))
        def _():
            cross_over(j)

        for s in range(line - 1, 0, -1):
            j = t - begin - slack * (line - s)

            @pl.when((j >= 0) & (j < total))
            def _():
                s_relay(s, j)

        j = t - begin - filled

        @pl.when(j >= 0)
        def _():
            finish(j)

        return carry

    lax.fori_loop(0, finish_step, step, 0)

    for c in range(len(spans)):
        for copy in spread(c):
            copy.wait_send()
    for i in range(len(pieces)):
        keep_copy(i).wait()
        twin_copy(i).wait()
        for k in range(1, pairs_g):
            far_copy(i, k).wait_send()
            hand_on(i, k).wait()

    sent_sums(bac_s, bex_s)
    for s in range(1, line):

        @pl.when(row + s < line)
        def _():
            sent(both, bup_s.at[row + s])

        @pl.when(row >= s)
        def _():
            sent(both, bdn_s.at[row - s])


def window_terms(blocks, groups, x, dy, gw, uw, dw, ag, au, bd, bg, bu, ad, tenants, slots, rank):
    line = blocks // 2
    own_rows, width = x.shape
    rows, units = blocks * own_rows, gw.shape[1]
    factors, count = ag.shape[0], bg.shape[0]
    picks = 2 * own_rows
    chunks = 8
    step_width = width // chunks
    depth = 3
    dma = pltpu.SemaphoreType.DMA
    vmem = pltpu.VMEM
    anywhere, inside = pl.BlockSpec(memory_space=pl.ANY), pl.BlockSpec(memory_space=vmem)
    held = [
        ((3, blocks, own_rows, width), bf16),
        ((2, line, own_rows, width), bf16),
        ((2, line, own_rows, width), bf16),
        ((2, own_rows, width), bf16),
        ((2, 2, own_rows, width), bf16),
        ((2, own_rows, width), bf16),
        ((own_rows, step_width), f32),
        ((rows, units), f32),
        ((rows, units), f32),
        ((rows, units), f32),
        ((picks, factors), f32),
        ((picks, factors), f32),
        ((picks, width), bf16),
        ((picks, width), bf16),
        ((rows, units), bf16),
        ((rows, units), bf16),
        ((rows, units), bf16),
        ((3, rows, factors), bf16),
        ((depth, step_width, units), bf16),
        ((depth, step_width, units), bf16),
        ((depth, max(units, factors), step_width), bf16),
        ((depth, factors, step_width), bf16),
        ((count, units), bf16),
        ((count, units), bf16),
        ((count, units), bf16),
        ((rank, lanes), bf16),
        ((picks, rows), bf16),
        ((picks, 1), jnp.int32),
        ((rows, 1), jnp.int32),
        ((rows, 1), jnp.int32),
        ((6 * rank, rows), bf16),
        ((blocks, 6 * rank, rows), bf16),
        ((6 * rank, rows), bf16),
        ((3, rows, lanes), f32),
        ((3, rows, lanes), f32),
        ((7 * rank, rows), bf16),
        (tenants.shape, jnp.int32),
        (slots.shape, jnp.int32),
    ]
    used = sum(math.prod(shape) * jnp.dtype(kind).itemsize for shape, kind in held) + 6 * 2**20
    roomy = used < 7 * vmem_grant // 8
    every = lambda *shape: jax.ShapeDtypeStruct((groups,) + shape, bf16)
    return pl.pallas_call(
        functools.partial(window_kernel, blocks, groups, rank, chunks),
        out_shape=(
            jax.ShapeDtypeStruct((2, own_rows, width), bf16),
            every(picks, width),
            every(picks, width),
            every(rows, units),
            every(rows, units),
            every(rows, units),
            every(7 * rank, rows),
        ),
        in_specs=[pl.BlockSpec(memory_space=pltpu.HBM)] * 13,
        out_specs=(inside,) + (inside if roomy else anywhere,) * 6,
        scratch_shapes=[vmem(shape, kind) for shape, kind in held]
        + [
            dma((10,)),
            dma((4, depth)),
            dma((3,)),
            dma((3, line)),
            dma((3, line, 2 * chunks)),
            dma((3, line)),
            dma((3, line, 2 * chunks)),
            dma((2, 2)),
            dma((2, 2, 2 * chunks)),
            dma((4, blocks)),
            dma((4, blocks)),
            dma((3, 6, groups // 2)),
            dma((3, 6, groups // 2)),
        ],
        compiler_params=pltpu.CompilerParams(
            collective_id=0,
            has_side_effects=True,
            vmem_limit_bytes=used if roomy else vmem_grant,
        ),
        cost_estimate=pl.CostEstimate(
            flops=12 * rows * width * (units + factors) + 12 * rows * count * units,
            bytes_accessed=12 * width * (units + factors) + 6 * count * units,
            transcendentals=rows * units,
        ),
        name="window_terms",
    )(
        *(
            pltpu.with_memory_space_constraint(value, pltpu.HBM)
            for value in (x, dy, gw, uw, dw, ag, au, bd, bg, bu, ad, tenants, slots)
        )
    )


def grads_kernel(
    rank,
    small,
    x,
    d,
    hid,
    gg,
    gu,
    got,
    o_m,
    o_i,
    o_ag,
    o_au,
    o_bd,
    o_bg,
    o_bu,
    o_ad,
    slot_out,
    tenant_out,
    row_sem,
    slot_sem,
    tenant_sem,
):
    groups, picks, width = x.shape
    rows, units = hid.shape[1:]
    own = slot_out.shape[1]
    every = tenant_out.shape[1]
    tall = min(256, every)
    wide = min(1024, width)
    results = [
        pltpu.make_async_copy(got.at[i], ref, row_sem.at[i]) for i, ref in enumerate((o_m, o_i))
    ]
    for copy in results:
        copy.start()
    group = lax.axis_index("grp")
    ids = [small[q, 6 * rank :, :].astype(f32) for q in range(groups)]
    slot = jnp.concatenate([part[2:3, :picks] for part in ids], axis=1)
    mark = jnp.concatenate([128.0 * part[0:1] + part[1:2] for part in ids], axis=1)
    mask = (line_of((own, 1), 0) // rank + group * (own // rank)).astype(f32) == slot
    weights = []
    for k, scale in ((0, adapter_scale), (1, 1.0), (2, 1.0)):
        at = (3 + k) * rank
        value = jnp.concatenate([small[q, at : at + rank, :picks] for q in range(groups)], axis=1)
        value = jnp.concatenate([value.astype(f32)] * (own // rank), axis=0)
        weights.append(jnp.where(mask, scale * value, 0.0).astype(bf16))
    slot_refs = (o_bd, o_ag, o_au)

    def slot_step(i, carry):
        at = pl.ds(pl.multiple_of(i * wide, wide), wide)
        value_x = x[:, :, at].reshape(groups * picks, wide)
        value_d = d[:, :, at].reshape(groups * picks, wide)
        for k, value in enumerate((value_d, value_x, value_x)):
            slot_out[k, :, at] = dot(weights[k], value)
            pltpu.make_async_copy(
                slot_out.at[k, :, at], slot_refs[k].at[:, at], slot_sem.at[k]
            ).start()
        return carry

    lax.fori_loop(0, width // wide, slot_step, 0)
    given = []
    for k, scale in enumerate((adapter_scale, adapter_scale, 1.0)):
        value = jnp.concatenate(
            [small[q, k * rank : (k + 1) * rank, :] for q in range(groups)], axis=1
        )
        given.append(scale * value.astype(f32))
    tenant_refs = (o_bg, o_bu, o_ad)
    values = (gg, gu, hid)

    def tenant_step(i, carry):
        at = pl.ds(pl.multiple_of(i * tall, tall), tall)
        first = group * (every // rank) + i * (tall // rank)
        here = (line_of((tall, 1), 0) // rank + first).astype(f32) == mark
        for k in range(3):
            value = jnp.concatenate([given[k]] * (tall // rank), axis=0)
            weight = jnp.where(here, value, 0.0).astype(bf16)
            tenant_out[k, at, :] = dot(weight, values[k][...].reshape(groups * rows, units))
            pltpu.make_async_copy(
                tenant_out.at[k, at, :], tenant_refs[k].at[at, :], tenant_sem.at[k]
            ).start()
        return carry

    lax.fori_loop(0, every // tall, tenant_step, 0)
    for copy in results:
        copy.wait()
    for k in range(3):
        pltpu.make_async_copy(slot_out.at[k], slot_refs[k], slot_sem.at[k]).wait()
        pltpu.make_async_copy(tenant_out.at[k], tenant_refs[k], tenant_sem.at[k]).wait()


def outer_sums(rank, small, x, d, hid, gg, gu, got, slots, tenants):
    width, units = x.shape[2], hid.shape[2]
    own, every = slots * rank, tenants * rank
    dma = pltpu.SemaphoreType.DMA
    row = jax.ShapeDtypeStruct(got.shape[1:], bf16)
    found = pl.pallas_call(
        functools.partial(grads_kernel, rank),
        out_shape=(row,) * 2
        + (jax.ShapeDtypeStruct((own, width), f32),) * 3
        + (jax.ShapeDtypeStruct((every, units), f32),) * 3,
        in_specs=[pl.BlockSpec(memory_space=pltpu.VMEM)] * 7,
        out_specs=(pl.BlockSpec(memory_space=pl.ANY),) * 8,
        scratch_shapes=[
            pltpu.VMEM((3, own, width), f32),
            pltpu.VMEM((3, every, units), f32),
            dma((2,)),
            dma((3,)),
            dma((3,)),
        ],
        compiler_params=pltpu.CompilerParams(vmem_limit_bytes=40 * 2**20),
        name="outer_sums",
    )(small, x, d, hid, gg, gu, got)
    return (*found[:2], *(part.reshape(-1, rank, part.shape[1]) for part in found[2:]))


def local(
    tokens,
    cotangent,
    gate_weight,
    up_weight,
    down_weight,
    a_gate,
    a_up,
    down_output_factors,
    b_gate,
    b_up,
    a_down,
    tenant_of_row,
    adapter_slot,
):
    width = tokens.shape[1]
    blocks = lax.axis_size("blk")
    groups = lax.axis_size("grp")
    per_owner, rank = a_gate.shape[:2]
    tenants, _, units = b_gate.shape
    slot_factors = [f.reshape(per_owner * rank, width) for f in (a_gate, a_up, down_output_factors)]
    tenant_factors = [f.reshape(tenants * rank, units) for f in (b_gate, b_up, a_down)]
    result, all_x, all_d, hid, gg, gu, small = window_terms(
        blocks,
        groups,
        tokens,
        cotangent,
        gate_weight,
        up_weight,
        down_weight,
        *slot_factors,
        *tenant_factors,
        tenant_of_row[None, :],
        adapter_slot[None, :],
        rank,
    )
    return outer_sums(
        rank, small, all_x, all_d, hid, gg, gu, result, per_owner // groups, tenants // groups
    )


def solution(mesh):
    placed = (
        P(("blk", "grp"), None),
        P(("blk", "grp"), None),
        P(None, "blk"),
        P(None, "blk"),
        P("blk", None),
        P("blk", None, None),
        P("blk", None, None),
        P("blk", None, None),
        P(None, None, "blk"),
        P(None, None, "blk"),
        P(None, None, "blk"),
        P(),
        P(),
    )
    return jax.shard_map(
        local,
        mesh=mesh,
        in_specs=placed,
        out_specs=(
            P(("blk", "grp"), None),
            P(("blk", "grp"), None),
            P(("blk", "grp"), None, None),
            P(("blk", "grp"), None, None),
            P(("blk", "grp"), None, None),
            P("grp", None, "blk"),
            P("grp", None, "blk"),
            P("grp", None, "blk"),
        ),
        check_vma=False,
    )
```

```python
import functools
import math

import jax
import jax.numpy as jnp
from jax import lax
from jax.experimental import pallas as pl
from jax.experimental.pallas import tpu as pltpu
from jax.sharding import PartitionSpec as P

MESH = pl.DeviceIdType.MESH
bf16 = jnp.bfloat16
vmem_grant = 60 * 2**20
f32 = jnp.float32
slack = 2


def remote(src, dst, send, recv, to):
    return pltpu.make_async_remote_copy(
        src_ref=src,
        dst_ref=dst,
        send_sem=send,
        recv_sem=recv,
        device_id={"blk": to},
        device_id_type=MESH,
    )


def place(blocks):
    me = lax.axis_index("blk")
    line = blocks // 2
    row = me // 2
    col = me - 2 * row
    partner = me + 1 - 2 * col
    return me, line, row, col, partner


adapter_scale = 2.0


def silu_pair(gate_in):
    sigmoid_val = jax.nn.sigmoid(gate_in)
    return (gate_in * sigmoid_val, sigmoid_val * (1.0 + gate_in * (1.0 - sigmoid_val)))


def dot(a, b, dims=((1,), (0,))):
    return lax.dot_general(a, b, (dims, ((), ())), preferred_element_type=f32)


across = ((1,), (1,))
lanes = 128


def fold(value):
    kept = value[:, :lanes]
    for k in range(1, value.shape[1] // lanes):
        kept = kept + value[:, k * lanes : (k + 1) * lanes]
    return kept


def repeat(value, width):
    return jnp.concatenate([value] * (width // lanes), axis=1)


def line_of(shape, axis):
    return lax.broadcasted_iota(jnp.int32, shape, axis)


def window_kernel(
    blocks,
    groups,
    rank,
    chunks,
    x_ref,
    d_ref,
    gw,
    uw,
    dw,
    ag,
    au,
    bd,
    bg,
    bu,
    ad,
    tenant_hbm,
    slot_hbm,
    out,
    all_x,
    all_d,
    all_h,
    all_g,
    all_u,
    all_small,
    held,
    pair_buf,
    line_buf,
    top_buf,
    ex_buf,
    cross_buf,
    acc,
    gate,
    up,
    gh,
    qa,
    qb,
    own_x,
    own_d,
    hid,
    gg,
    gu,
    extra,
    wide_g,
    wide_u,
    tall_a,
    tall_b,
    fac_g,
    fac_u,
    fac_d,
    pat,
    choose,
    own_slot,
    tenant_col,
    slot_col,
    give,
    land,
    sums,
    low,
    coef,
    small,
    tenant_row,
    slot_row,
    own_sem,
    w_sem,
    f_sem,
    g_sems,
    r_sems,
    s_sems,
    t_sems,
    x_sems,
    y_sems,
    sum_s,
    sum_r,
    e_sems,
    v_sems,
):
    me, line, row, col, partner = place(blocks)
    above, below = me + 2, me - 2
    own_rows, width = x_ref.shape
    rows = blocks * own_rows
    step_width = width // chunks
    total = 2 * chunks
    depth = wide_g.shape[0]
    units, factors = dw.shape[0], bd.shape[0]
    count = bg.shape[0]
    tile = min(1024, count)
    tiles = count // tile
    picks = choose.shape[0]
    group = lax.axis_index("grp")
    pairs_g, high = groups // 2, group // 2
    odd = group - 2 * high
    twin = group + 1 - 2 * odd
    filled = slack * line
    x_end = chunks - 1 + filled
    d_end = total - 1 + filled
    begin = d_end - 1
    finish_step = begin + total + filled

    up_s, up_r, dn_s, dn_r = g_sems.at[0], r_sems.at[0], g_sems.at[1], r_sems.at[1]
    ac_s, ac_r = g_sems.at[2], r_sems.at[2]
    ex_s, ex_r = x_sems.at[0], y_sems.at[0]
    bup_s, bup_r, bdn_s, bdn_r = s_sems.at[0], t_sems.at[0], s_sems.at[1], t_sems.at[1]
    bac_s, bac_r = s_sems.at[2], t_sems.at[2]
    bex_s, bex_r = x_sems.at[1], y_sems.at[1]

    def columns(j):
        return pl.ds(pl.multiple_of(lax.rem(j, chunks) * step_width, step_width), step_width)

    def doubled(j):
        return lax.rem(j, 2) == 1

    def plain(s, j):
        return lax.rem(j, 2) == 0 if s == 1 else j >= 0

    def loads(q, four):
        at, k = columns(q), lax.rem(q, depth)
        if four:
            moves = (
                (ag.at[:, at], tall_a.at[k, pl.ds(0, factors)]),
                (au.at[:, at], tall_b.at[k]),
                (gw.at[at, :], wide_g.at[k]),
                (uw.at[at, :], wide_u.at[k]),
            )
        else:
            moves = (
                (dw.at[:, at], tall_a.at[k, pl.ds(0, units)]),
                (bd.at[:, at], tall_b.at[k]),
            )
        return [
            pltpu.make_async_copy(src, dst, w_sem.at[i, k]) for i, (src, dst) in enumerate(moves)
        ]

    def fetch(q):
        outer = (q < chunks) | (q >= 3 * chunks)

        @pl.when(outer & (q < 4 * chunks))
        def _():
            for copy in loads(q, True):
                copy.start()

        @pl.when(jnp.logical_not(outer))
        def _():
            for copy in loads(q, False):
                copy.start()

    def held_part(block, j):
        return held.at[j // chunks, block, :, columns(j)]

    def g_up(block, s, j):
        ref = held_part(block, j)
        return remote(ref, ref, up_s.at[s], up_r.at[s, j], above)

    def g_dn(block, s, j):
        ref = held_part(block, j)
        return remote(ref, ref, dn_s.at[s], dn_r.at[s, j], below)

    def g_ac(at, j):
        ref = held_part(2 * at + col, j)
        return remote(ref, ref, ac_s.at[at], ac_r.at[at, j], partner)

    def g_ac_arrival(at, j):
        ref = held_part(2 * at + 1 - col, j)
        return remote(ref, ref, ac_s.at[at], ac_r.at[at, j], partner)

    def g_ex(direction, block, j, to):
        ref = held_part(block, j)
        return remote(ref, ref, ex_s.at[direction], ex_r.at[direction, j], to)

    def g_own(j):
        g_ac(row, j).start()

        @pl.when(row < line - 1)
        def _():
            g_up(me, 0, j).start()

        @pl.when(row > 0)
        def _():
            g_dn(me, 0, j).start()

    def g_relay(s, j):
        @pl.when(row >= s)
        def _():
            block = me - 2 * s
            g_up(block, s - 1, j).wait_recv()
            if s < line - 1:

                @pl.when(row < line - 1)
                def _():
                    g_up(block, s, j).start()

            @pl.when(plain(s, j))
            def _():
                g_ac(row - s, j).start()

        @pl.when(row + s < line)
        def _():
            block = me + 2 * s
            g_dn(block, s - 1, j).wait_recv()
            if s < line - 1:

                @pl.when(row > 0)
                def _():
                    g_dn(block, s, j).start()

            @pl.when(plain(s, j))
            def _():
                g_ac(row + s, j).start()

        if s == 1:
            g_ac_arrival(row, j).wait_recv()

            @pl.when(doubled(j))
            def _():
                @pl.when(row < line - 1)
                def _():
                    g_ex(0, partner, j, above).start()

                @pl.when(row > 0)
                def _():
                    g_ex(1, partner, j, below).start()

    def g_arrive(j):
        for s in range(1, line):

            @pl.when(plain(s, j) & (row >= s))
            def _():
                g_ac_arrival(row - s, j).wait_recv()

            @pl.when(plain(s, j) & (row + s < line))
            def _():
                g_ac_arrival(row + s, j).wait_recv()

        @pl.when(doubled(j) & (row > 0))
        def _():
            g_ex(0, partner - 2, j, above).wait_recv()

        @pl.when(doubled(j) & (row < line - 1))
        def _():
            g_ex(1, partner + 2, j, below).wait_recv()

    def take(j):
        g_arrive(j)
        at, k = columns(j), lax.rem(j, depth)

        @pl.when(j < chunks)
        def _():
            for copy in loads(j, True):
                copy.wait()
            value = held[0, :, :, at].reshape(rows, step_width)
            gate[...] += dot(value, wide_g[k])
            up[...] += dot(value, wide_u[k])
            mine = dot(choose[...], value).astype(bf16)
            own_x[:, at] = mine
            qa[...] += dot(mine, tall_a[k, :factors], across)
            qb[...] += dot(mine, tall_b[k], across)

        @pl.when(j >= chunks)
        def _():
            for copy in loads(j, False):
                copy.wait()
            value = held[1, :, :, at].reshape(rows, step_width)
            gh[...] += dot(value, tall_a[k, :units], across)
            mine = dot(choose[...], value).astype(bf16)
            own_d[:, at] = mine
            qb[...] += dot(mine, tall_b[k], across)

        fetch(j + depth)

    spans = ((0, 2 * rank), (2 * rank, rank), (3 * rank, rank), (4 * rank, 2 * rank))

    def spread(c):
        first, size = spans[c]
        return [
            remote(
                give.at[pl.ds(first, size)],
                land.at[k, pl.ds(first, size)],
                sum_s.at[c, k],
                sum_r.at[c, k],
                lax.rem(me + k, blocks),
            )
            for k in range(1, blocks)
        ]

    def send_sum(c):
        for copy in spread(c):
            copy.start()

    def take_sum(c):
        first, size = spans[c]
        value = give[first : first + size, :].astype(f32)
        for k, copy in enumerate(spread(c)):
            copy.wait_recv()
            value = value + land[k + 1, first : first + size, :].astype(f32)
        sums[first : first + size, :] = value.astype(bf16)

    def turned(first, size):
        same = line_of((rows, rows), 0) == line_of((rows, rows), 1)
        return dot(same.astype(bf16), sums[first : first + size, :], across).astype(bf16)

    def pick(ref, scale):
        mask = own_slot[...] == line_of((1, factors), 1) // rank
        kept = fold(jnp.where(mask, scale * ref[...], 0.0)).astype(bf16)
        found = dot(pat[...], kept, across).astype(bf16)
        return dot(found, choose[...]).astype(bf16)

    def tenant_mask(i):
        return tenant_col[...] == line_of((1, tile), 1) // rank + i * (tile // rank)

    def each_tile(first, last, body):
        def run(i, carry):
            body(i, tenant_mask(i), pl.ds(pl.multiple_of(i * tile, tile), tile))
            return carry

        lax.fori_loop(first, last, run, 0)

    def add_low_rank(sum_ref, fac, k, scale, mask, at):
        wide = jnp.where(mask, repeat(coef[k], tile), 0.0).astype(bf16)
        sum_ref[...] += scale * dot(wide, fac[at, :])

    def reduce_low_rank(values, fac, k, mask, at):
        full = dot(values[...], fac[at, :], across)
        low[k] += fold(jnp.where(mask, full, 0.0))

    def ahead(i, mask, at):
        add_low_rank(gate, fac_g, 0, adapter_scale, mask, at)
        add_low_rank(up, fac_u, 1, adapter_scale, mask, at)

    def back_in(i, mask, at):
        add_low_rank(gh, fac_d, 2, 1.0, mask, at)

    def low_out(i, mask, at):
        reduce_low_rank(hid, fac_d, 0, mask, at)

    def back_out(i, mask, at):
        reduce_low_rank(gg, fac_g, 1, mask, at)
        reduce_low_rank(gu, fac_u, 2, mask, at)

    def lowered(k, scale):
        return (scale * dot(pat[...], low[k].astype(bf16), across)).astype(bf16)

    def owned(k, first, scale):
        mask = slot_col[...] == line_of((1, factors), 1) // rank
        given = repeat(dot(turned(first, rank), pat[...]), factors)
        extra[k] = (scale * jnp.where(mask, given, 0.0)).astype(bf16)

    pieces = (
        (own_x, all_x),
        (hid, all_h),
        (own_d, all_d),
        (gg, all_g),
        (gu, all_u),
        (small, all_small),
    )

    def to_group(src, dst, send, recv, to):
        return pltpu.make_async_remote_copy(
            src_ref=src,
            dst_ref=dst,
            send_sem=send,
            recv_sem=recv,
            device_id={"grp": to},
            device_id_type=MESH,
        )

    def keep_copy(i):
        src, dst = pieces[i]
        return pltpu.make_async_copy(src, dst.at[group], own_sem.at[2 + i])

    def twin_copy(i):
        src, dst = pieces[i]
        return to_group(src, dst.at[group], e_sems.at[0, i, 0], v_sems.at[0, i, 0], twin)

    def far_copy(i, k):
        src, dst = pieces[i]
        to = 2 * lax.rem(high + k, pairs_g) + odd
        return to_group(src, dst.at[group], e_sems.at[1, i, k], v_sems.at[1, i, k], to)

    def hand_on(i, k):
        ref = pieces[i][1].at[2 * lax.rem(high + pairs_g - k, pairs_g) + odd]
        return to_group(ref, ref, e_sems.at[2, i, k], v_sems.at[2, i, k], twin)

    def share(i):
        for k in range(1, pairs_g):
            far_copy(i, k).start()
        twin_copy(i).start()
        keep_copy(i).start()

    def pass_on(i):
        for k in range(1, pairs_g):
            far_copy(i, k).wait_recv()
            hand_on(i, k).start()

    def part(block, j):
        return held.at[lax.rem(2 + j // chunks, 3), block, :, columns(j)]

    def piece(buf, at, j):
        return buf.at[j // chunks, at, :, columns(j)]

    def flat(buf, j):
        return buf.at[j // chunks, :, columns(j)]

    def s_ac(src, at, j):
        return remote(src, piece(pair_buf, at, j), bac_s.at[at], bac_r.at[at, j], partner)

    def s_up(at, j):
        return remote(
            piece(pair_buf, at, j), piece(line_buf, at, j), bup_s.at[at], bup_r.at[at, j], above
        )

    def s_dn(at, j, landing):
        return remote(piece(pair_buf, at, j), landing, bdn_s.at[at], bdn_r.at[at, j], below)

    def s_ex(direction, block, j, to):
        return remote(
            part(block, j),
            piece(ex_buf, direction, j),
            bex_s.at[direction],
            bex_r.at[direction, j],
            to,
        )

    def make(j):
        at, k = columns(j), lax.rem(j + total, depth)

        @pl.when(j < chunks)
        def _():
            for copy in loads(j + total, False):
                copy.wait()
            value = dot(hid[...], tall_a[k, :units]) + dot(extra[0], tall_b[k])
            held[2, :, :, at] = value.astype(bf16).reshape(blocks, own_rows, step_width)

        @pl.when(j >= chunks)
        def _():
            for copy in loads(j + total, True):
                copy.wait()
            value = (
                dot(gg[...], wide_g[k], across)
                + dot(gu[...], wide_u[k], across)
                + dot(extra[1], tall_a[k, :factors])
                + dot(extra[2], tall_b[k])
            )
            held[0, :, :, at] = value.astype(bf16).reshape(blocks, own_rows, step_width)

        for s in range(line - 1, 0, -1):
            for ok, to in ((row + s < line, row + s), (row >= s, row - s)):

                @pl.when(ok & plain(s, j))
                def _():
                    s_ac(part(2 * to + 1 - col, j), to, j).start()

        @pl.when(doubled(j))
        def _():
            @pl.when(row < line - 1)
            def _():
                s_ex(0, partner + 2, j, above).start()

            @pl.when(row > 0)
            def _():
                s_ex(1, partner - 2, j, below).start()

        @pl.when(lax.rem(j, 2) == 0)
        def _():
            s_ac(part(partner, j), row, j).start()

        fetch(j + total + depth)

    def cross_over(j):
        @pl.when(doubled(j))
        def _():
            acc[...] = part(partner, j)[...].astype(f32)

            @pl.when(row > 0)
            def _():
                s_ex(0, partner, j, above).wait_recv()
                acc[...] += piece(ex_buf, 0, j)[...].astype(f32)

            @pl.when(row < line - 1)
            def _():
                s_ex(1, partner, j, below).wait_recv()
                acc[...] += piece(ex_buf, 1, j)[...].astype(f32)

            flat(cross_buf, j)[...] = acc[...].astype(bf16)
            s_ac(flat(cross_buf, j), row, j).start()

    def pair_up(s, at, j):
        mine = part(2 * at + col, j)
        acc[...] = mine[...].astype(f32)

        @pl.when(plain(s, j))
        def _():
            s_ac(mine, at, j).wait_recv()
            acc[...] += piece(pair_buf, at, j)[...].astype(f32)

    def s_relay(s, j):
        @pl.when(row + s < line)
        def _():
            at = row + s
            pair_up(s, at, j)
            if s < line - 1:

                @pl.when(row > 0)
                def _():
                    s_up(at, j).wait_recv()
                    acc[...] += piece(line_buf, at, j)[...].astype(f32)

            piece(pair_buf, at, j)[...] = acc[...].astype(bf16)
            s_up(at, j).start()

        @pl.when(row >= s)
        def _():
            at = row - s
            landing = flat(top_buf, j) if s == 1 else piece(line_buf, at, j)
            pair_up(s, at, j)
            if s < line - 1:

                @pl.when(row < line - 1)
                def _():
                    s_dn(at, j, landing).wait_recv()
                    acc[...] += piece(line_buf, at, j)[...].astype(f32)

            piece(pair_buf, at, j)[...] = acc[...].astype(bf16)
            s_dn(at, j, landing).start()

    def finish(j):
        mine = part(me, j)
        s_ac(mine, row, j).wait_recv()
        acc[...] = mine[...].astype(f32) + piece(pair_buf, row, j)[...].astype(f32)

        @pl.when(row > 0)
        def _():
            s_up(row, j).wait_recv()
            acc[...] += piece(line_buf, row, j)[...].astype(f32)

        @pl.when(row < line - 1)
        def _():
            s_dn(row, j, flat(top_buf, j)).wait_recv()
            acc[...] += flat(top_buf, j)[...].astype(f32)

        out[j // chunks, :, columns(j)] = acc[...].astype(bf16)

    def sent(ref, sem):
        remote(ref, ref, sem, sum_r.at[0, 0], partner).wait_send()

    both, one = held.at[pl.ds(0, 2), me], held.at[0, me]

    def sent_sums(acs, exs):
        sent(both, acs.at[row])
        for s in range(1, line):
            for ok, at in ((row >= s, row - s), (row + s < line, row + s)):

                @pl.when(ok)
                def _():
                    sent(one if s == 1 else both, acs.at[at])

        @pl.when(row < line - 1)
        def _():
            sent(one, exs.at[0])

        @pl.when(row > 0)
        def _():
            sent(one, exs.at[1])

    def gather_sent():
        sent_sums(ac_s, ex_s)
        for s in range(line - 1):

            @pl.when((row >= s) & (row < line - 1))
            def _():
                sent(both, up_s.at[s])

            @pl.when((row + s < line) & (row > 0))
            def _():
                sent(both, dn_s.at[s])

    own = [
        pltpu.make_async_copy(ref, held.at[c, me], own_sem.at[c])
        for c, ref in enumerate((x_ref, d_ref))
    ]
    own += [
        pltpu.make_async_copy(src, dst, own_sem.at[8 + c])
        for c, (src, dst) in enumerate(((tenant_hbm, tenant_row), (slot_hbm, slot_row)))
    ]
    for copy in own:
        copy.start()
    barrier = pltpu.get_barrier_semaphore()
    for k in range(1, blocks):
        pl.semaphore_signal(
            barrier, inc=1, device_id={"blk": lax.rem(me + k, blocks)}, device_id_type=MESH
        )
    pl.semaphore_signal(barrier, inc=1, device_id={"grp": twin}, device_id_type=MESH)
    for k in range(1, pairs_g):
        to = 2 * lax.rem(high + k, pairs_g) + odd
        pl.semaphore_signal(barrier, inc=1, device_id={"grp": to}, device_id_type=MESH)
    for q in range(depth):
        fetch(q)
    tables = [
        pltpu.make_async_copy(src, dst, f_sem.at[i])
        for i, (src, dst) in enumerate(((bg, fac_g), (bu, fac_u), (ad, fac_d)))
    ]
    for copy in tables:
        copy.start()
    for copy in own:
        copy.wait()
    pl.semaphore_wait(barrier, blocks - 1 + pairs_g)
    lead = min(2 * slack, total)
    for j in range(lead):
        g_own(j)

    for ref in (gate, up, gh, qa, qb, low):
        ref[...] = jnp.zeros_like(ref)
    pat[...] = (lax.rem(line_of(pat.shape, 1), rank) == line_of(pat.shape, 0)).astype(bf16)
    per_owner = factors // rank
    here = line_of((rows, 1), 0)
    source = (here // own_rows * groups + group) * own_rows + lax.rem(here, own_rows)
    every = tenant_row.shape[1]
    hit = line_of((1, every), 1) == source
    tenants = jnp.sum(jnp.where(hit, tenant_row[...].astype(f32), 0.0), axis=1, keepdims=True)
    tenant_col[...] = tenants.astype(jnp.int32)
    known = line_of((1, slot_row.shape[1]), 1) == tenant_col[...]
    slots = jnp.sum(jnp.where(known, slot_row[...].astype(f32), 0.0), axis=1, keepdims=True)
    local = slots.astype(jnp.int32) - me * per_owner
    slot_col[...] = local
    mine_col = ((local >= 0) & (local < per_owner)).astype(f32)
    first_i, second_i = line_of((rows, rows), 0), line_of((rows, rows), 1)
    same_i = first_i == second_i
    within = jnp.sum(jnp.where(first_i < second_i, mine_col, 0.0), axis=0, keepdims=True)
    mine_row = jnp.sum(jnp.where(same_i, mine_col, 0.0), axis=0, keepdims=True)
    local_row = jnp.sum(jnp.where(same_i, local.astype(f32), 0.0), axis=0, keepdims=True)
    tenant_line = jnp.sum(jnp.where(same_i, tenants, 0.0), axis=0, keepdims=True)
    chosen = (mine_row > 0.5) & (within == line_of((picks, 1), 0).astype(f32))
    choose[...] = chosen.astype(bf16)
    owned_at = jnp.sum(jnp.where(chosen, local_row + 1.0, 0.0), axis=1, keepdims=True) - 1.0
    own_slot[...] = owned_at.astype(jnp.int32)
    ids = line_of((rank, rows), 0)
    coarse = jnp.floor(tenant_line * (1.0 / 128.0))
    picked_row = jnp.sum(
        jnp.where(line_of((picks, rows), 0) == line_of((picks, rows), 1), owned_at, 0.0),
        axis=0,
        keepdims=True,
    )
    small[6 * rank :, :] = jnp.where(
        ids == 0,
        coarse,
        jnp.where(ids == 1, tenant_line - 128.0 * coarse, jnp.where(ids == 2, picked_row, 0.0)),
    ).astype(bf16)

    half = max(1, tiles // 2)

    def step(t, carry):
        def hook(at, body):
            pl.when(t == at)(body)

        @pl.when((t >= lead) & (t < total))
        def _():
            g_own(t)

        for s in range(1, line):
            j = t - slack * s

            @pl.when((j >= 0) & (j < total))
            def _():
                g_relay(s, j)

        j = t - filled

        @pl.when((j >= 0) & (j < total))
        def _():
            take(j)

        @functools.partial(hook, x_end)
        def _():
            give[:rank, :] = pick(qa, 1.0)
            give[rank : 2 * rank, :] = pick(qb, 1.0)
            send_sum(0)
            share(0)
            qb[...] = jnp.zeros_like(qb)

        @functools.partial(hook, x_end + 2)
        def _():
            for copy in tables:
                copy.wait()
            take_sum(0)
            for k in range(2):
                coef[k] = dot(turned(k * rank, rank), pat[...])
            each_tile(0, half, ahead)

        @functools.partial(hook, x_end + 3)
        def _():
            each_tile(half, tiles, ahead)

        @functools.partial(hook, x_end + 4)
        def _():
            act_val, act_slope = silu_pair(gate[...])
            hid[...] = (act_val * up[...]).astype(bf16)
            gate[...] = act_val
            up[...] = up[...] * act_slope
            each_tile(0, half, low_out)

        @functools.partial(hook, x_end + 5)
        def _():
            each_tile(half, tiles, low_out)
            give[3 * rank : 4 * rank, :] = lowered(0, 1.0)
            send_sum(2)
            share(1)

        @functools.partial(hook, begin)
        def _():
            take_sum(2)
            owned(0, 3 * rank, adapter_scale)

        @functools.partial(hook, d_end)
        def _():
            give[2 * rank : 3 * rank, :] = pick(qb, adapter_scale)
            send_sum(1)
            share(2)

        @functools.partial(hook, d_end + 3)
        def _():
            take_sum(1)
            coef[2] = dot(turned(2 * rank, rank), pat[...])
            each_tile(0, tiles, back_in)
            grad_h = gh[...]
            gg[...] = (grad_h * up[...]).astype(bf16)
            gu[...] = (grad_h * gate[...]).astype(bf16)
            share(3)
            share(4)

        @functools.partial(hook, d_end + 4)
        def _():
            each_tile(0, half, back_out)

        @functools.partial(hook, d_end + 5)
        def _():
            each_tile(half, tiles, back_out)
            for k in range(2):
                give[(4 + k) * rank : (5 + k) * rank, :] = lowered(1 + k, adapter_scale)
            send_sum(3)

        @functools.partial(hook, begin + chunks)
        def _():
            gather_sent()
            take_sum(3)
            owned(1, 4 * rank, 1.0)
            owned(2, 5 * rank, 1.0)
            small[: 3 * rank, :] = sums[: 3 * rank, :]
            found = dot(sums[3 * rank :, :], choose[...], across)
            wide = (line_of((picks, rows), 0) == line_of((picks, rows), 1)).astype(bf16)
            small[3 * rank : 6 * rank, :] = dot(found.astype(bf16), wide).astype(bf16)
            share(5)

        for i, at in enumerate(
            (x_end + 8, x_end + 9, d_end + 8, d_end + 11, d_end + 12, d_end + 13)
        ):
            hook(at, functools.partial(pass_on, i))

        u = t - begin

        @pl.when((u >= 0) & (u < total))
        def _():
            make(u)

        j = t - begin - slack

        @pl.when((j >= 0) & (j < total))
        def _():
            cross_over(j)

        for s in range(line - 1, 0, -1):
            j = t - begin - slack * (line - s)

            @pl.when((j >= 0) & (j < total))
            def _():
                s_relay(s, j)

        j = t - begin - filled

        @pl.when(j >= 0)
        def _():
            finish(j)

        return carry

    lax.fori_loop(0, finish_step, step, 0)

    for c in range(len(spans)):
        for copy in spread(c):
            copy.wait_send()
    for i in range(len(pieces)):
        keep_copy(i).wait()
        twin_copy(i).wait()
        for k in range(1, pairs_g):
            far_copy(i, k).wait_send()
            hand_on(i, k).wait()

    sent_sums(bac_s, bex_s)
    for s in range(1, line):

        @pl.when(row + s < line)
        def _():
            sent(both, bup_s.at[row + s])

        @pl.when(row >= s)
        def _():
            sent(both, bdn_s.at[row - s])


def window_terms(blocks, groups, x, dy, gw, uw, dw, ag, au, bd, bg, bu, ad, tenants, slots, rank):
    line = blocks // 2
    own_rows, width = x.shape
    rows, units = blocks * own_rows, gw.shape[1]
    factors, count = ag.shape[0], bg.shape[0]
    picks = 2 * own_rows
    chunks = 8
    step_width = width // chunks
    depth = 3
    dma = pltpu.SemaphoreType.DMA
    vmem = pltpu.VMEM
    anywhere, inside = pl.BlockSpec(memory_space=pl.ANY), pl.BlockSpec(memory_space=vmem)
    held = [
        ((3, blocks, own_rows, width), bf16),
        ((2, line, own_rows, width), bf16),
        ((2, line, own_rows, width), bf16),
        ((2, own_rows, width), bf16),
        ((2, 2, own_rows, width), bf16),
        ((2, own_rows, width), bf16),
        ((own_rows, step_width), f32),
        ((rows, units), f32),
        ((rows, units), f32),
        ((rows, units), f32),
        ((picks, factors), f32),
        ((picks, factors), f32),
        ((picks, width), bf16),
        ((picks, width), bf16),
        ((rows, units), bf16),
        ((rows, units), bf16),
        ((rows, units), bf16),
        ((3, rows, factors), bf16),
        ((depth, step_width, units), bf16),
        ((depth, step_width, units), bf16),
        ((depth, max(units, factors), step_width), bf16),
        ((depth, factors, step_width), bf16),
        ((count, units), bf16),
        ((count, units), bf16),
        ((count, units), bf16),
        ((rank, lanes), bf16),
        ((picks, rows), bf16),
        ((picks, 1), jnp.int32),
        ((rows, 1), jnp.int32),
        ((rows, 1), jnp.int32),
        ((6 * rank, rows), bf16),
        ((blocks, 6 * rank, rows), bf16),
        ((6 * rank, rows), bf16),
        ((3, rows, lanes), f32),
        ((3, rows, lanes), f32),
        ((7 * rank, rows), bf16),
        (tenants.shape, jnp.int32),
        (slots.shape, jnp.int32),
    ]
    used = sum(math.prod(shape) * jnp.dtype(kind).itemsize for shape, kind in held) + 6 * 2**20
    roomy = used < 7 * vmem_grant // 8
    every = lambda *shape: jax.ShapeDtypeStruct((groups,) + shape, bf16)
    return pl.pallas_call(
        functools.partial(window_kernel, blocks, groups, rank, chunks),
        out_shape=(
            jax.ShapeDtypeStruct((2, own_rows, width), bf16),
            every(picks, width),
            every(picks, width),
            every(rows, units),
            every(rows, units),
            every(rows, units),
            every(7 * rank, rows),
        ),
        in_specs=[pl.BlockSpec(memory_space=pltpu.HBM)] * 13,
        out_specs=(inside,) + (inside if roomy else anywhere,) * 6,
        scratch_shapes=[vmem(shape, kind) for shape, kind in held]
        + [
            dma((10,)),
            dma((4, depth)),
            dma((3,)),
            dma((3, line)),
            dma((3, line, 2 * chunks)),
            dma((3, line)),
            dma((3, line, 2 * chunks)),
            dma((2, 2)),
            dma((2, 2, 2 * chunks)),
            dma((4, blocks)),
            dma((4, blocks)),
            dma((3, 6, groups // 2)),
            dma((3, 6, groups // 2)),
        ],
        compiler_params=pltpu.CompilerParams(
            collective_id=0,
            has_side_effects=True,
            vmem_limit_bytes=used if roomy else vmem_grant,
        ),
        cost_estimate=pl.CostEstimate(
            flops=12 * rows * width * (units + factors) + 12 * rows * count * units,
            bytes_accessed=12 * width * (units + factors) + 6 * count * units,
            transcendentals=rows * units,
        ),
        name="window_terms",
    )(
        *(
            pltpu.with_memory_space_constraint(value, pltpu.HBM)
            for value in (x, dy, gw, uw, dw, ag, au, bd, bg, bu, ad, tenants, slots)
        )
    )


def grads_kernel(
    rank,
    small,
    x,
    d,
    hid,
    gg,
    gu,
    got,
    o_m,
    o_i,
    o_ag,
    o_au,
    o_bd,
    o_bg,
    o_bu,
    o_ad,
    slot_out,
    tenant_out,
    row_sem,
    slot_sem,
    tenant_sem,
):
    groups, picks, width = x.shape
    rows, units = hid.shape[1:]
    own = slot_out.shape[1]
    every = tenant_out.shape[1]
    tall = min(256, every)
    wide = min(1024, width)
    results = [
        pltpu.make_async_copy(got.at[i], ref, row_sem.at[i]) for i, ref in enumerate((o_m, o_i))
    ]
    for copy in results:
        copy.start()
    group = lax.axis_index("grp")
    ids = [small[q, 6 * rank :, :].astype(f32) for q in range(groups)]
    slot = jnp.concatenate([part[2:3, :picks] for part in ids], axis=1)
    mark = jnp.concatenate([128.0 * part[0:1] + part[1:2] for part in ids], axis=1)
    mask = (line_of((own, 1), 0) // rank + group * (own // rank)).astype(f32) == slot
    weights = []
    for k, scale in ((0, adapter_scale), (1, 1.0), (2, 1.0)):
        at = (3 + k) * rank
        value = jnp.concatenate([small[q, at : at + rank, :picks] for q in range(groups)], axis=1)
        value = jnp.concatenate([value.astype(f32)] * (own // rank), axis=0)
        weights.append(jnp.where(mask, scale * value, 0.0).astype(bf16))
    slot_refs = (o_bd, o_ag, o_au)

    def slot_step(i, carry):
        at = pl.ds(pl.multiple_of(i * wide, wide), wide)
        value_x = x[:, :, at].reshape(groups * picks, wide)
        value_d = d[:, :, at].reshape(groups * picks, wide)
        for k, value in enumerate((value_d, value_x, value_x)):
            slot_out[k, :, at] = dot(weights[k], value)
            pltpu.make_async_copy(
                slot_out.at[k, :, at], slot_refs[k].at[:, at], slot_sem.at[k]
            ).start()
        return carry

    lax.fori_loop(0, width // wide, slot_step, 0)
    given = []
    for k, scale in enumerate((adapter_scale, adapter_scale, 1.0)):
        value = jnp.concatenate(
            [small[q, k * rank : (k + 1) * rank, :] for q in range(groups)], axis=1
        )
        given.append(scale * value.astype(f32))
    tenant_refs = (o_bg, o_bu, o_ad)
    values = (gg, gu, hid)

    def tenant_step(i, carry):
        at = pl.ds(pl.multiple_of(i * tall, tall), tall)
        first = group * (every // rank) + i * (tall // rank)
        here = (line_of((tall, 1), 0) // rank + first).astype(f32) == mark
        for k in range(3):
            value = jnp.concatenate([given[k]] * (tall // rank), axis=0)
            weight = jnp.where(here, value, 0.0).astype(bf16)
            tenant_out[k, at, :] = dot(weight, values[k][...].reshape(groups * rows, units))
            pltpu.make_async_copy(
                tenant_out.at[k, at, :], tenant_refs[k].at[at, :], tenant_sem.at[k]
            ).start()
        return carry

    lax.fori_loop(0, every // tall, tenant_step, 0)
    for copy in results:
        copy.wait()
    for k in range(3):
        pltpu.make_async_copy(slot_out.at[k], slot_refs[k], slot_sem.at[k]).wait()
        pltpu.make_async_copy(tenant_out.at[k], tenant_refs[k], tenant_sem.at[k]).wait()


def outer_sums(rank, small, x, d, hid, gg, gu, got, slots, tenants):
    width, units = x.shape[2], hid.shape[2]
    own, every = slots * rank, tenants * rank
    dma = pltpu.SemaphoreType.DMA
    row = jax.ShapeDtypeStruct(got.shape[1:], bf16)
    found = pl.pallas_call(
        functools.partial(grads_kernel, rank),
        out_shape=(row,) * 2
        + (jax.ShapeDtypeStruct((own, width), f32),) * 3
        + (jax.ShapeDtypeStruct((every, units), f32),) * 3,
        in_specs=[pl.BlockSpec(memory_space=pltpu.VMEM)] * 7,
        out_specs=(pl.BlockSpec(memory_space=pl.ANY),) * 8,
        scratch_shapes=[
            pltpu.VMEM((3, own, width), f32),
            pltpu.VMEM((3, every, units), f32),
            dma((2,)),
            dma((3,)),
            dma((3,)),
        ],
        compiler_params=pltpu.CompilerParams(vmem_limit_bytes=40 * 2**20),
        name="outer_sums",
    )(small, x, d, hid, gg, gu, got)
    return (*found[:2], *(part.reshape(-1, rank, part.shape[1]) for part in found[2:]))


def local(
    tokens,
    cotangent,
    gate_weight,
    up_weight,
    down_weight,
    a_gate,
    a_up,
    down_output_factors,
    b_gate,
    b_up,
    a_down,
    tenant_of_row,
    adapter_slot,
):
    width = tokens.shape[1]
    blocks = lax.axis_size("blk")
    groups = lax.axis_size("grp")
    per_owner, rank = a_gate.shape[:2]
    tenants, _, units = b_gate.shape
    slot_factors = [f.reshape(per_owner * rank, width) for f in (a_gate, a_up, down_output_factors)]
    tenant_factors = [f.reshape(tenants * rank, units) for f in (b_gate, b_up, a_down)]
    result, all_x, all_d, hid, gg, gu, small = window_terms(
        blocks,
        groups,
        tokens,
        cotangent,
        gate_weight,
        up_weight,
        down_weight,
        *slot_factors,
        *tenant_factors,
        tenant_of_row[None, :],
        adapter_slot[None, :],
        rank,
    )
    return outer_sums(
        rank, small, all_x, all_d, hid, gg, gu, result, per_owner // groups, tenants // groups
    )


def solution(mesh):
    placed = (
        P(("blk", "grp"), None),
        P(("blk", "grp"), None),
        P(None, "blk"),
        P(None, "blk"),
        P("blk", None),
        P("blk", None, None),
        P("blk", None, None),
        P("blk", None, None),
        P(None, None, "blk"),
        P(None, None, "blk"),
        P(None, None, "blk"),
        P(),
        P(),
    )
    return jax.shard_map(
        local,
        mesh=mesh,
        in_specs=placed,
        out_specs=(
            P(("blk", "grp"), None),
            P(("blk", "grp"), None),
            P(("blk", "grp"), None, None),
            P(("blk", "grp"), None, None),
            P(("blk", "grp"), None, None),
            P("grp", None, "blk"),
            P("grp", None, "blk"),
            P("grp", None, "blk"),
        ),
        check_vma=False,
    )
```

```python
import functools
import math

import jax
import jax.numpy as jnp
from jax import lax
from jax.experimental import pallas as pl
from jax.experimental.pallas import tpu as pltpu
from jax.sharding import PartitionSpec as P

MESH = pl.DeviceIdType.MESH
bf16 = jnp.bfloat16
vmem_grant = 60 * 2**20
f32 = jnp.float32
slack = 2


def remote(src, dst, send, recv, to):
    return pltpu.make_async_remote_copy(
        src_ref=src,
        dst_ref=dst,
        send_sem=send,
        recv_sem=recv,
        device_id={"blk": to},
        device_id_type=MESH,
    )


def place(blocks):
    me = lax.axis_index("blk")
    line = blocks // 2
    row = me // 2
    col = me - 2 * row
    partner = me + 1 - 2 * col
    return me, line, row, col, partner


adapter_scale = 2.0


def silu_pair(gate_in):
    sigmoid_val = jax.nn.sigmoid(gate_in)
    return (gate_in * sigmoid_val, sigmoid_val * (1.0 + gate_in * (1.0 - sigmoid_val)))


def dot(a, b, dims=((1,), (0,))):
    return lax.dot_general(a, b, (dims, ((), ())), preferred_element_type=f32)


across = ((1,), (1,))
lanes = 128


def fold(value):
    kept = value[:, :lanes]
    for k in range(1, value.shape[1] // lanes):
        kept = kept + value[:, k * lanes : (k + 1) * lanes]
    return kept


def repeat(value, width):
    return jnp.concatenate([value] * (width // lanes), axis=1)


def line_of(shape, axis):
    return lax.broadcasted_iota(jnp.int32, shape, axis)


def window_kernel(
    blocks,
    groups,
    rank,
    chunks,
    x_ref,
    d_ref,
    gw,
    uw,
    dw,
    ag,
    au,
    bd,
    bg,
    bu,
    ad,
    tenant_hbm,
    slot_hbm,
    out,
    all_x,
    all_d,
    all_h,
    all_g,
    all_u,
    all_small,
    held,
    pair_buf,
    line_buf,
    top_buf,
    ex_buf,
    cross_buf,
    acc,
    gate,
    up,
    gh,
    qa,
    qb,
    own_x,
    own_d,
    hid,
    gg,
    gu,
    extra,
    wide_g,
    wide_u,
    tall_a,
    tall_b,
    fac_g,
    fac_u,
    fac_d,
    pat,
    choose,
    own_slot,
    tenant_col,
    slot_col,
    give,
    land,
    sums,
    low,
    coef,
    small,
    tenant_row,
    slot_row,
    own_sem,
    w_sem,
    f_sem,
    g_sems,
    r_sems,
    s_sems,
    t_sems,
    x_sems,
    y_sems,
    sum_s,
    sum_r,
    e_sems,
    v_sems,
):
    me, line, row, col, partner = place(blocks)
    above, below = me + 2, me - 2
    own_rows, width = x_ref.shape
    rows = blocks * own_rows
    step_width = width // chunks
    total = 2 * chunks
    depth = wide_g.shape[0]
    units, factors = dw.shape[0], bd.shape[0]
    count = bg.shape[0]
    tile = min(1024, count)
    tiles = count // tile
    picks = choose.shape[0]
    group = lax.axis_index("grp")
    pairs_g, high = groups // 2, group // 2
    odd = group - 2 * high
    twin = group + 1 - 2 * odd
    filled = slack * line
    x_end = chunks - 1 + filled
    d_end = total - 1 + filled
    begin = d_end - 1
    finish_step = begin + total + filled

    up_s, up_r, dn_s, dn_r = g_sems.at[0], r_sems.at[0], g_sems.at[1], r_sems.at[1]
    ac_s, ac_r = g_sems.at[2], r_sems.at[2]
    ex_s, ex_r = x_sems.at[0], y_sems.at[0]
    bup_s, bup_r, bdn_s, bdn_r = s_sems.at[0], t_sems.at[0], s_sems.at[1], t_sems.at[1]
    bac_s, bac_r = s_sems.at[2], t_sems.at[2]
    bex_s, bex_r = x_sems.at[1], y_sems.at[1]

    def columns(j):
        return pl.ds(pl.multiple_of(lax.rem(j, chunks) * step_width, step_width), step_width)

    def doubled(j):
        return lax.rem(j, 2) == 1

    def plain(s, j):
        return lax.rem(j, 2) == 0 if s == 1 else j >= 0

    def loads(q, four):
        at, k = columns(q), lax.rem(q, depth)
        if four:
            moves = (
                (ag.at[:, at], tall_a.at[k, pl.ds(0, factors)]),
                (au.at[:, at], tall_b.at[k]),
                (gw.at[at, :], wide_g.at[k]),
                (uw.at[at, :], wide_u.at[k]),
            )
        else:
            moves = (
                (dw.at[:, at], tall_a.at[k, pl.ds(0, units)]),
                (bd.at[:, at], tall_b.at[k]),
            )
        return [
            pltpu.make_async_copy(src, dst, w_sem.at[i, k]) for i, (src, dst) in enumerate(moves)
        ]

    def fetch(q):
        outer = (q < chunks) | (q >= 3 * chunks)

        @pl.when(outer & (q < 4 * chunks))
        def _():
            for copy in loads(q, True):
                copy.start()

        @pl.when(jnp.logical_not(outer))
        def _():
            for copy in loads(q, False):
                copy.start()

    def held_part(block, j):
        return held.at[j // chunks, block, :, columns(j)]

    def g_up(block, s, j):
        ref = held_part(block, j)
        return remote(ref, ref, up_s.at[s], up_r.at[s, j], above)

    def g_dn(block, s, j):
        ref = held_part(block, j)
        return remote(ref, ref, dn_s.at[s], dn_r.at[s, j], below)

    def g_ac(at, j):
        ref = held_part(2 * at + col, j)
        return remote(ref, ref, ac_s.at[at], ac_r.at[at, j], partner)

    def g_ac_arrival(at, j):
        ref = held_part(2 * at + 1 - col, j)
        return remote(ref, ref, ac_s.at[at], ac_r.at[at, j], partner)

    def g_ex(direction, block, j, to):
        ref = held_part(block, j)
        return remote(ref, ref, ex_s.at[direction], ex_r.at[direction, j], to)

    def g_own(j):
        g_ac(row, j).start()

        @pl.when(row < line - 1)
        def _():
            g_up(me, 0, j).start()

        @pl.when(row > 0)
        def _():
            g_dn(me, 0, j).start()

    def g_relay(s, j):
        @pl.when(row >= s)
        def _():
            block = me - 2 * s
            g_up(block, s - 1, j).wait_recv()
            if s < line - 1:

                @pl.when(row < line - 1)
                def _():
                    g_up(block, s, j).start()

            @pl.when(plain(s, j))
            def _():
                g_ac(row - s, j).start()

        @pl.when(row + s < line)
        def _():
            block = me + 2 * s
            g_dn(block, s - 1, j).wait_recv()
            if s < line - 1:

                @pl.when(row > 0)
                def _():
                    g_dn(block, s, j).start()

            @pl.when(plain(s, j))
            def _():
                g_ac(row + s, j).start()

        if s == 1:
            g_ac_arrival(row, j).wait_recv()

            @pl.when(doubled(j))
            def _():
                @pl.when(row < line - 1)
                def _():
                    g_ex(0, partner, j, above).start()

                @pl.when(row > 0)
                def _():
                    g_ex(1, partner, j, below).start()

    def g_arrive(j):
        for s in range(1, line):

            @pl.when(plain(s, j) & (row >= s))
            def _():
                g_ac_arrival(row - s, j).wait_recv()

            @pl.when(plain(s, j) & (row + s < line))
            def _():
                g_ac_arrival(row + s, j).wait_recv()

        @pl.when(doubled(j) & (row > 0))
        def _():
            g_ex(0, partner - 2, j, above).wait_recv()

        @pl.when(doubled(j) & (row < line - 1))
        def _():
            g_ex(1, partner + 2, j, below).wait_recv()

    def take(j):
        g_arrive(j)
        at, k = columns(j), lax.rem(j, depth)

        @pl.when(j < chunks)
        def _():
            for copy in loads(j, True):
                copy.wait()
            value = held[0, :, :, at].reshape(rows, step_width)
            gate[...] += dot(value, wide_g[k])
            up[...] += dot(value, wide_u[k])
            mine = dot(choose[...], value).astype(bf16)
            own_x[:, at] = mine
            qa[...] += dot(mine, tall_a[k, :factors], across)
            qb[...] += dot(mine, tall_b[k], across)

        @pl.when(j >= chunks)
        def _():
            for copy in loads(j, False):
                copy.wait()
            value = held[1, :, :, at].reshape(rows, step_width)
            gh[...] += dot(value, tall_a[k, :units], across)
            mine = dot(choose[...], value).astype(bf16)
            own_d[:, at] = mine
            qb[...] += dot(mine, tall_b[k], across)

        fetch(j + depth)

    spans = ((0, 2 * rank), (2 * rank, rank), (3 * rank, rank), (4 * rank, 2 * rank))

    def spread(c):
        first, size = spans[c]
        return [
            remote(
                give.at[pl.ds(first, size)],
                land.at[k, pl.ds(first, size)],
                sum_s.at[c, k],
                sum_r.at[c, k],
                lax.rem(me + k, blocks),
            )
            for k in range(1, blocks)
        ]

    def send_sum(c):
        for copy in spread(c):
            copy.start()

    def take_sum(c):
        first, size = spans[c]
        value = give[first : first + size, :].astype(f32)
        for k, copy in enumerate(spread(c)):
            copy.wait_recv()
            value = value + land[k + 1, first : first + size, :].astype(f32)
        sums[first : first + size, :] = value.astype(bf16)

    def turned(first, size):
        same = line_of((rows, rows), 0) == line_of((rows, rows), 1)
        return dot(same.astype(bf16), sums[first : first + size, :], across).astype(bf16)

    def pick(ref, scale):
        mask = own_slot[...] == line_of((1, factors), 1) // rank
        kept = fold(jnp.where(mask, scale * ref[...], 0.0)).astype(bf16)
        found = dot(pat[...], kept, across).astype(bf16)
        return dot(found, choose[...]).astype(bf16)

    def tenant_mask(i):
        return tenant_col[...] == line_of((1, tile), 1) // rank + i * (tile // rank)

    def each_tile(first, last, body):
        def run(i, carry):
            body(i, tenant_mask(i), pl.ds(pl.multiple_of(i * tile, tile), tile))
            return carry

        lax.fori_loop(first, last, run, 0)

    def add_low_rank(sum_ref, fac, k, scale, mask, at):
        wide = jnp.where(mask, repeat(coef[k], tile), 0.0).astype(bf16)
        sum_ref[...] += scale * dot(wide, fac[at, :])

    def reduce_low_rank(values, fac, k, mask, at):
        full = dot(values[...], fac[at, :], across)
        low[k] += fold(jnp.where(mask, full, 0.0))

    def ahead(i, mask, at):
        add_low_rank(gate, fac_g, 0, adapter_scale, mask, at)
        add_low_rank(up, fac_u, 1, adapter_scale, mask, at)

    def back_in(i, mask, at):
        add_low_rank(gh, fac_d, 2, 1.0, mask, at)

    def low_out(i, mask, at):
        reduce_low_rank(hid, fac_d, 0, mask, at)

    def back_out(i, mask, at):
        reduce_low_rank(gg, fac_g, 1, mask, at)
        reduce_low_rank(gu, fac_u, 2, mask, at)

    def lowered(k, scale):
        return (scale * dot(pat[...], low[k].astype(bf16), across)).astype(bf16)

    def owned(k, first, scale):
        mask = slot_col[...] == line_of((1, factors), 1) // rank
        given = repeat(dot(turned(first, rank), pat[...]), factors)
        extra[k] = (scale * jnp.where(mask, given, 0.0)).astype(bf16)

    pieces = (
        (own_x, all_x),
        (hid, all_h),
        (own_d, all_d),
        (gg, all_g),
        (gu, all_u),
        (small, all_small),
    )

    def to_group(src, dst, send, recv, to):
        return pltpu.make_async_remote_copy(
            src_ref=src,
            dst_ref=dst,
            send_sem=send,
            recv_sem=recv,
            device_id={"grp": to},
            device_id_type=MESH,
        )

    def keep_copy(i):
        src, dst = pieces[i]
        return pltpu.make_async_copy(src, dst.at[group], own_sem.at[2 + i])

    def twin_copy(i):
        src, dst = pieces[i]
        return to_group(src, dst.at[group], e_sems.at[0, i, 0], v_sems.at[0, i, 0], twin)

    def far_copy(i, k):
        src, dst = pieces[i]
        to = 2 * lax.rem(high + k, pairs_g) + odd
        return to_group(src, dst.at[group], e_sems.at[1, i, k], v_sems.at[1, i, k], to)

    def hand_on(i, k):
        ref = pieces[i][1].at[2 * lax.rem(high + pairs_g - k, pairs_g) + odd]
        return to_group(ref, ref, e_sems.at[2, i, k], v_sems.at[2, i, k], twin)

    def share(i):
        for k in range(1, pairs_g):
            far_copy(i, k).start()
        twin_copy(i).start()
        keep_copy(i).start()

    def pass_on(i):
        for k in range(1, pairs_g):
            far_copy(i, k).wait_recv()
            hand_on(i, k).start()

    def part(block, j):
        return held.at[lax.rem(2 + j // chunks, 3), block, :, columns(j)]

    def piece(buf, at, j):
        return buf.at[j // chunks, at, :, columns(j)]

    def flat(buf, j):
        return buf.at[j // chunks, :, columns(j)]

    def s_ac(src, at, j):
        return remote(src, piece(pair_buf, at, j), bac_s.at[at], bac_r.at[at, j], partner)

    def s_up(at, j):
        return remote(
            piece(pair_buf, at, j), piece(line_buf, at, j), bup_s.at[at], bup_r.at[at, j], above
        )

    def s_dn(at, j, landing):
        return remote(piece(pair_buf, at, j), landing, bdn_s.at[at], bdn_r.at[at, j], below)

    def s_ex(direction, block, j, to):
        return remote(
            part(block, j),
            piece(ex_buf, direction, j),
            bex_s.at[direction],
            bex_r.at[direction, j],
            to,
        )

    def make(j):
        at, k = columns(j), lax.rem(j + total, depth)

        @pl.when(j < chunks)
        def _():
            for copy in loads(j + total, False):
                copy.wait()
            value = dot(hid[...], tall_a[k, :units]) + dot(extra[0], tall_b[k])
            held[2, :, :, at] = value.astype(bf16).reshape(blocks, own_rows, step_width)

        @pl.when(j >= chunks)
        def _():
            for copy in loads(j + total, True):
                copy.wait()
            value = (
                dot(gg[...], wide_g[k], across)
                + dot(gu[...], wide_u[k], across)
                + dot(extra[1], tall_a[k, :factors])
                + dot(extra[2], tall_b[k])
            )
            held[0, :, :, at] = value.astype(bf16).reshape(blocks, own_rows, step_width)

        for s in range(line - 1, 0, -1):
            for ok, to in ((row + s < line, row + s), (row >= s, row - s)):

                @pl.when(ok & plain(s, j))
                def _():
                    s_ac(part(2 * to + 1 - col, j), to, j).start()

        @pl.when(doubled(j))
        def _():
            @pl.when(row < line - 1)
            def _():
                s_ex(0, partner + 2, j, above).start()

            @pl.when(row > 0)
            def _():
                s_ex(1, partner - 2, j, below).start()

        @pl.when(lax.rem(j, 2) == 0)
        def _():
            s_ac(part(partner, j), row, j).start()

        fetch(j + total + depth)

    def cross_over(j):
        @pl.when(doubled(j))
        def _():
            acc[...] = part(partner, j)[...].astype(f32)

            @pl.when(row > 0)
            def _():
                s_ex(0, partner, j, above).wait_recv()
                acc[...] += piece(ex_buf, 0, j)[...].astype(f32)

            @pl.when(row < line - 1)
            def _():
                s_ex(1, partner, j, below).wait_recv()
                acc[...] += piece(ex_buf, 1, j)[...].astype(f32)

            flat(cross_buf, j)[...] = acc[...].astype(bf16)
            s_ac(flat(cross_buf, j), row, j).start()

    def pair_up(s, at, j):
        mine = part(2 * at + col, j)
        acc[...] = mine[...].astype(f32)

        @pl.when(plain(s, j))
        def _():
            s_ac(mine, at, j).wait_recv()
            acc[...] += piece(pair_buf, at, j)[...].astype(f32)

    def s_relay(s, j):
        @pl.when(row + s < line)
        def _():
            at = row + s
            pair_up(s, at, j)
            if s < line - 1:

                @pl.when(row > 0)
                def _():
                    s_up(at, j).wait_recv()
                    acc[...] += piece(line_buf, at, j)[...].astype(f32)

            piece(pair_buf, at, j)[...] = acc[...].astype(bf16)
            s_up(at, j).start()

        @pl.when(row >= s)
        def _():
            at = row - s
            landing = flat(top_buf, j) if s == 1 else piece(line_buf, at, j)
            pair_up(s, at, j)
            if s < line - 1:

                @pl.when(row < line - 1)
                def _():
                    s_dn(at, j, landing).wait_recv()
                    acc[...] += piece(line_buf, at, j)[...].astype(f32)

            piece(pair_buf, at, j)[...] = acc[...].astype(bf16)
            s_dn(at, j, landing).start()

    def finish(j):
        mine = part(me, j)
        s_ac(mine, row, j).wait_recv()
        acc[...] = mine[...].astype(f32) + piece(pair_buf, row, j)[...].astype(f32)

        @pl.when(row > 0)
        def _():
            s_up(row, j).wait_recv()
            acc[...] += piece(line_buf, row, j)[...].astype(f32)

        @pl.when(row < line - 1)
        def _():
            s_dn(row, j, flat(top_buf, j)).wait_recv()
            acc[...] += flat(top_buf, j)[...].astype(f32)

        out[j // chunks, :, columns(j)] = acc[...].astype(bf16)

    def sent(ref, sem):
        remote(ref, ref, sem, sum_r.at[0, 0], partner).wait_send()

    both, one = held.at[pl.ds(0, 2), me], held.at[0, me]

    def sent_sums(acs, exs):
        sent(both, acs.at[row])
        for s in range(1, line):
            for ok, at in ((row >= s, row - s), (row + s < line, row + s)):

                @pl.when(ok)
                def _():
                    sent(one if s == 1 else both, acs.at[at])

        @pl.when(row < line - 1)
        def _():
            sent(one, exs.at[0])

        @pl.when(row > 0)
        def _():
            sent(one, exs.at[1])

    def gather_sent():
        sent_sums(ac_s, ex_s)
        for s in range(line - 1):

            @pl.when((row >= s) & (row < line - 1))
            def _():
                sent(both, up_s.at[s])

            @pl.when((row + s < line) & (row > 0))
            def _():
                sent(both, dn_s.at[s])

    own = [
        pltpu.make_async_copy(ref, held.at[c, me], own_sem.at[c])
        for c, ref in enumerate((x_ref, d_ref))
    ]
    own += [
        pltpu.make_async_copy(src, dst, own_sem.at[8 + c])
        for c, (src, dst) in enumerate(((tenant_hbm, tenant_row), (slot_hbm, slot_row)))
    ]
    for copy in own:
        copy.start()
    barrier = pltpu.get_barrier_semaphore()
    for k in range(1, blocks):
        pl.semaphore_signal(
            barrier, inc=1, device_id={"blk": lax.rem(me + k, blocks)}, device_id_type=MESH
        )
    pl.semaphore_signal(barrier, inc=1, device_id={"grp": twin}, device_id_type=MESH)
    for k in range(1, pairs_g):
        to = 2 * lax.rem(high + k, pairs_g) + odd
        pl.semaphore_signal(barrier, inc=1, device_id={"grp": to}, device_id_type=MESH)
    for q in range(depth):
        fetch(q)
    tables = [
        pltpu.make_async_copy(src, dst, f_sem.at[i])
        for i, (src, dst) in enumerate(((bg, fac_g), (bu, fac_u), (ad, fac_d)))
    ]
    for copy in tables:
        copy.start()
    for copy in own:
        copy.wait()
    pl.semaphore_wait(barrier, blocks - 1 + pairs_g)
    lead = min(2 * slack, total)
    for j in range(lead):
        g_own(j)

    for ref in (gate, up, gh, qa, qb, low):
        ref[...] = jnp.zeros_like(ref)
    pat[...] = (lax.rem(line_of(pat.shape, 1), rank) == line_of(pat.shape, 0)).astype(bf16)
    per_owner = factors // rank
    here = line_of((rows, 1), 0)
    source = (here // own_rows * groups + group) * own_rows + lax.rem(here, own_rows)
    every = tenant_row.shape[1]
    hit = line_of((1, every), 1) == source
    tenants = jnp.sum(jnp.where(hit, tenant_row[...].astype(f32), 0.0), axis=1, keepdims=True)
    tenant_col[...] = tenants.astype(jnp.int32)
    known = line_of((1, slot_row.shape[1]), 1) == tenant_col[...]
    slots = jnp.sum(jnp.where(known, slot_row[...].astype(f32), 0.0), axis=1, keepdims=True)
    local = slots.astype(jnp.int32) - me * per_owner
    slot_col[...] = local
    mine_col = ((local >= 0) & (local < per_owner)).astype(f32)
    first_i, second_i = line_of((rows, rows), 0), line_of((rows, rows), 1)
    same_i = first_i == second_i
    within = jnp.sum(jnp.where(first_i < second_i, mine_col, 0.0), axis=0, keepdims=True)
    mine_row = jnp.sum(jnp.where(same_i, mine_col, 0.0), axis=0, keepdims=True)
    local_row = jnp.sum(jnp.where(same_i, local.astype(f32), 0.0), axis=0, keepdims=True)
    tenant_line = jnp.sum(jnp.where(same_i, tenants, 0.0), axis=0, keepdims=True)
    chosen = (mine_row > 0.5) & (within == line_of((picks, 1), 0).astype(f32))
    choose[...] = chosen.astype(bf16)
    owned_at = jnp.sum(jnp.where(chosen, local_row + 1.0, 0.0), axis=1, keepdims=True) - 1.0
    own_slot[...] = owned_at.astype(jnp.int32)
    ids = line_of((rank, rows), 0)
    coarse = jnp.floor(tenant_line * (1.0 / 128.0))
    picked_row = jnp.sum(
        jnp.where(line_of((picks, rows), 0) == line_of((picks, rows), 1), owned_at, 0.0),
        axis=0,
        keepdims=True,
    )
    small[6 * rank :, :] = jnp.where(
        ids == 0,
        coarse,
        jnp.where(ids == 1, tenant_line - 128.0 * coarse, jnp.where(ids == 2, picked_row, 0.0)),
    ).astype(bf16)

    half = max(1, tiles // 2)

    def step(t, carry):
        def hook(at, body):
            pl.when(t == at)(body)

        @pl.when((t >= lead) & (t < total))
        def _():
            g_own(t)

        for s in range(1, line):
            j = t - slack * s

            @pl.when((j >= 0) & (j < total))
            def _():
                g_relay(s, j)

        j = t - filled

        @pl.when((j >= 0) & (j < total))
        def _():
            take(j)

        @functools.partial(hook, x_end)
        def _():
            give[:rank, :] = pick(qa, 1.0)
            give[rank : 2 * rank, :] = pick(qb, 1.0)
            send_sum(0)
            share(0)
            qb[...] = jnp.zeros_like(qb)

        @functools.partial(hook, x_end + 3)
        def _():
            for copy in tables:
                copy.wait()
            take_sum(0)
            for k in range(2):
                coef[k] = dot(turned(k * rank, rank), pat[...])
            each_tile(0, tiles, ahead)

        @functools.partial(hook, x_end + 4)
        def _():
            act_val, act_slope = silu_pair(gate[...])
            hid[...] = (act_val * up[...]).astype(bf16)
            gate[...] = act_val
            up[...] = up[...] * act_slope
            each_tile(0, half, low_out)

        @functools.partial(hook, x_end + 5)
        def _():
            each_tile(half, tiles, low_out)
            give[3 * rank : 4 * rank, :] = lowered(0, 1.0)
            send_sum(2)
            share(1)

        @functools.partial(hook, begin)
        def _():
            take_sum(2)
            owned(0, 3 * rank, adapter_scale)

        @functools.partial(hook, d_end)
        def _():
            give[2 * rank : 3 * rank, :] = pick(qb, adapter_scale)
            send_sum(1)
            share(2)

        @functools.partial(hook, d_end + 3)
        def _():
            take_sum(1)
            coef[2] = dot(turned(2 * rank, rank), pat[...])
            each_tile(0, tiles, back_in)
            grad_h = gh[...]
            gg[...] = (grad_h * up[...]).astype(bf16)
            gu[...] = (grad_h * gate[...]).astype(bf16)
            share(3)
            share(4)

        @functools.partial(hook, d_end + 4)
        def _():
            each_tile(0, half, back_out)

        @functools.partial(hook, d_end + 5)
        def _():
            each_tile(half, tiles, back_out)
            for k in range(2):
                give[(4 + k) * rank : (5 + k) * rank, :] = lowered(1 + k, adapter_scale)
            send_sum(3)

        @functools.partial(hook, begin + chunks)
        def _():
            gather_sent()
            take_sum(3)
            owned(1, 4 * rank, 1.0)
            owned(2, 5 * rank, 1.0)
            small[: 3 * rank, :] = sums[: 3 * rank, :]
            found = dot(sums[3 * rank :, :], choose[...], across)
            wide = (line_of((picks, rows), 0) == line_of((picks, rows), 1)).astype(bf16)
            small[3 * rank : 6 * rank, :] = dot(found.astype(bf16), wide).astype(bf16)
            share(5)

        for i, at in enumerate(
            (x_end + 8, x_end + 9, d_end + 8, d_end + 11, d_end + 12, d_end + 13)
        ):
            hook(at, functools.partial(pass_on, i))

        u = t - begin

        @pl.when((u >= 0) & (u < total))
        def _():
            make(u)

        j = t - begin - slack

        @pl.when((j >= 0) & (j < total))
        def _():
            cross_over(j)

        for s in range(line - 1, 0, -1):
            j = t - begin - slack * (line - s)

            @pl.when((j >= 0) & (j < total))
            def _():
                s_relay(s, j)

        j = t - begin - filled

        @pl.when(j >= 0)
        def _():
            finish(j)

        return carry

    lax.fori_loop(0, finish_step, step, 0)

    for c in range(len(spans)):
        for copy in spread(c):
            copy.wait_send()
    for i in range(len(pieces)):
        keep_copy(i).wait()
        twin_copy(i).wait()
        for k in range(1, pairs_g):
            far_copy(i, k).wait_send()
            hand_on(i, k).wait()

    sent_sums(bac_s, bex_s)
    for s in range(1, line):

        @pl.when(row + s < line)
        def _():
            sent(both, bup_s.at[row + s])

        @pl.when(row >= s)
        def _():
            sent(both, bdn_s.at[row - s])


def window_terms(blocks, groups, x, dy, gw, uw, dw, ag, au, bd, bg, bu, ad, tenants, slots, rank):
    line = blocks // 2
    own_rows, width = x.shape
    rows, units = blocks * own_rows, gw.shape[1]
    factors, count = ag.shape[0], bg.shape[0]
    picks = 2 * own_rows
    chunks = 8
    step_width = width // chunks
    depth = 3
    dma = pltpu.SemaphoreType.DMA
    vmem = pltpu.VMEM
    anywhere, inside = pl.BlockSpec(memory_space=pl.ANY), pl.BlockSpec(memory_space=vmem)
    held = [
        ((3, blocks, own_rows, width), bf16),
        ((2, line, own_rows, width), bf16),
        ((2, line, own_rows, width), bf16),
        ((2, own_rows, width), bf16),
        ((2, 2, own_rows, width), bf16),
        ((2, own_rows, width), bf16),
        ((own_rows, step_width), f32),
        ((rows, units), f32),
        ((rows, units), f32),
        ((rows, units), f32),
        ((picks, factors), f32),
        ((picks, factors), f32),
        ((picks, width), bf16),
        ((picks, width), bf16),
        ((rows, units), bf16),
        ((rows, units), bf16),
        ((rows, units), bf16),
        ((3, rows, factors), bf16),
        ((depth, step_width, units), bf16),
        ((depth, step_width, units), bf16),
        ((depth, max(units, factors), step_width), bf16),
        ((depth, factors, step_width), bf16),
        ((count, units), bf16),
        ((count, units), bf16),
        ((count, units), bf16),
        ((rank, lanes), bf16),
        ((picks, rows), bf16),
        ((picks, 1), jnp.int32),
        ((rows, 1), jnp.int32),
        ((rows, 1), jnp.int32),
        ((6 * rank, rows), bf16),
        ((blocks, 6 * rank, rows), bf16),
        ((6 * rank, rows), bf16),
        ((3, rows, lanes), f32),
        ((3, rows, lanes), f32),
        ((7 * rank, rows), bf16),
        (tenants.shape, jnp.int32),
        (slots.shape, jnp.int32),
    ]
    used = sum(math.prod(shape) * jnp.dtype(kind).itemsize for shape, kind in held) + 6 * 2**20
    roomy = used < 7 * vmem_grant // 8
    every = lambda *shape: jax.ShapeDtypeStruct((groups,) + shape, bf16)
    return pl.pallas_call(
        functools.partial(window_kernel, blocks, groups, rank, chunks),
        out_shape=(
            jax.ShapeDtypeStruct((2, own_rows, width), bf16),
            every(picks, width),
            every(picks, width),
            every(rows, units),
            every(rows, units),
            every(rows, units),
            every(7 * rank, rows),
        ),
        in_specs=[pl.BlockSpec(memory_space=pltpu.HBM)] * 13,
        out_specs=(inside,) + (inside if roomy else anywhere,) * 6,
        scratch_shapes=[vmem(shape, kind) for shape, kind in held]
        + [
            dma((10,)),
            dma((4, depth)),
            dma((3,)),
            dma((3, line)),
            dma((3, line, 2 * chunks)),
            dma((3, line)),
            dma((3, line, 2 * chunks)),
            dma((2, 2)),
            dma((2, 2, 2 * chunks)),
            dma((4, blocks)),
            dma((4, blocks)),
            dma((3, 6, groups // 2)),
            dma((3, 6, groups // 2)),
        ],
        compiler_params=pltpu.CompilerParams(
            collective_id=0,
            has_side_effects=True,
            vmem_limit_bytes=used if roomy else vmem_grant,
        ),
        cost_estimate=pl.CostEstimate(
            flops=12 * rows * width * (units + factors) + 12 * rows * count * units,
            bytes_accessed=12 * width * (units + factors) + 6 * count * units,
            transcendentals=rows * units,
        ),
        name="window_terms",
    )(
        *(
            pltpu.with_memory_space_constraint(value, pltpu.HBM)
            for value in (x, dy, gw, uw, dw, ag, au, bd, bg, bu, ad, tenants, slots)
        )
    )


def grads_kernel(
    rank,
    small,
    x,
    d,
    hid,
    gg,
    gu,
    got,
    o_m,
    o_i,
    o_ag,
    o_au,
    o_bd,
    o_bg,
    o_bu,
    o_ad,
    slot_out,
    tenant_out,
    row_sem,
    slot_sem,
    tenant_sem,
):
    groups, picks, width = x.shape
    rows, units = hid.shape[1:]
    own = slot_out.shape[1]
    every = tenant_out.shape[1]
    tall = min(256, every)
    wide = min(1024, width)
    results = [
        pltpu.make_async_copy(got.at[i], ref, row_sem.at[i]) for i, ref in enumerate((o_m, o_i))
    ]
    for copy in results:
        copy.start()
    group = lax.axis_index("grp")
    ids = [small[q, 6 * rank :, :].astype(f32) for q in range(groups)]
    slot = jnp.concatenate([part[2:3, :picks] for part in ids], axis=1)
    mark = jnp.concatenate([128.0 * part[0:1] + part[1:2] for part in ids], axis=1)
    mask = (line_of((own, 1), 0) // rank + group * (own // rank)).astype(f32) == slot
    weights = []
    for k, scale in ((0, adapter_scale), (1, 1.0), (2, 1.0)):
        at = (3 + k) * rank
        value = jnp.concatenate([small[q, at : at + rank, :picks] for q in range(groups)], axis=1)
        value = jnp.concatenate([value.astype(f32)] * (own // rank), axis=0)
        weights.append(jnp.where(mask, scale * value, 0.0).astype(bf16))
    slot_refs = (o_bd, o_ag, o_au)

    def slot_step(i, carry):
        at = pl.ds(pl.multiple_of(i * wide, wide), wide)
        value_x = x[:, :, at].reshape(groups * picks, wide)
        value_d = d[:, :, at].reshape(groups * picks, wide)
        for k, value in enumerate((value_d, value_x, value_x)):
            slot_out[k, :, at] = dot(weights[k], value)
            pltpu.make_async_copy(
                slot_out.at[k, :, at], slot_refs[k].at[:, at], slot_sem.at[k]
            ).start()
        return carry

    lax.fori_loop(0, width // wide, slot_step, 0)
    given = []
    for k, scale in enumerate((adapter_scale, adapter_scale, 1.0)):
        value = jnp.concatenate(
            [small[q, k * rank : (k + 1) * rank, :] for q in range(groups)], axis=1
        )
        given.append(scale * value.astype(f32))
    tenant_refs = (o_bg, o_bu, o_ad)
    values = (gg, gu, hid)

    def tenant_step(i, carry):
        at = pl.ds(pl.multiple_of(i * tall, tall), tall)
        first = group * (every // rank) + i * (tall // rank)
        here = (line_of((tall, 1), 0) // rank + first).astype(f32) == mark
        for k in range(3):
            value = jnp.concatenate([given[k]] * (tall // rank), axis=0)
            weight = jnp.where(here, value, 0.0).astype(bf16)
            tenant_out[k, at, :] = dot(weight, values[k][...].reshape(groups * rows, units))
            pltpu.make_async_copy(
                tenant_out.at[k, at, :], tenant_refs[k].at[at, :], tenant_sem.at[k]
            ).start()
        return carry

    lax.fori_loop(0, every // tall, tenant_step, 0)
    for copy in results:
        copy.wait()
    for k in range(3):
        pltpu.make_async_copy(slot_out.at[k], slot_refs[k], slot_sem.at[k]).wait()
        pltpu.make_async_copy(tenant_out.at[k], tenant_refs[k], tenant_sem.at[k]).wait()


def outer_sums(rank, small, x, d, hid, gg, gu, got, slots, tenants):
    width, units = x.shape[2], hid.shape[2]
    own, every = slots * rank, tenants * rank
    dma = pltpu.SemaphoreType.DMA
    row = jax.ShapeDtypeStruct(got.shape[1:], bf16)
    found = pl.pallas_call(
        functools.partial(grads_kernel, rank),
        out_shape=(row,) * 2
        + (jax.ShapeDtypeStruct((own, width), f32),) * 3
        + (jax.ShapeDtypeStruct((every, units), f32),) * 3,
        in_specs=[pl.BlockSpec(memory_space=pltpu.VMEM)] * 7,
        out_specs=(pl.BlockSpec(memory_space=pl.ANY),) * 8,
        scratch_shapes=[
            pltpu.VMEM((3, own, width), f32),
            pltpu.VMEM((3, every, units), f32),
            dma((2,)),
            dma((3,)),
            dma((3,)),
        ],
        compiler_params=pltpu.CompilerParams(vmem_limit_bytes=40 * 2**20),
        name="outer_sums",
    )(small, x, d, hid, gg, gu, got)
    return (*found[:2], *(part.reshape(-1, rank, part.shape[1]) for part in found[2:]))


def local(
    tokens,
    cotangent,
    gate_weight,
    up_weight,
    down_weight,
    a_gate,
    a_up,
    down_output_factors,
    b_gate,
    b_up,
    a_down,
    tenant_of_row,
    adapter_slot,
):
    width = tokens.shape[1]
    blocks = lax.axis_size("blk")
    groups = lax.axis_size("grp")
    per_owner, rank = a_gate.shape[:2]
    tenants, _, units = b_gate.shape
    slot_factors = [f.reshape(per_owner * rank, width) for f in (a_gate, a_up, down_output_factors)]
    tenant_factors = [f.reshape(tenants * rank, units) for f in (b_gate, b_up, a_down)]
    result, all_x, all_d, hid, gg, gu, small = window_terms(
        blocks,
        groups,
        tokens,
        cotangent,
        gate_weight,
        up_weight,
        down_weight,
        *slot_factors,
        *tenant_factors,
        tenant_of_row[None, :],
        adapter_slot[None, :],
        rank,
    )
    return outer_sums(
        rank, small, all_x, all_d, hid, gg, gu, result, per_owner // groups, tenants // groups
    )


def solution(mesh):
    placed = (
        P(("blk", "grp"), None),
        P(("blk", "grp"), None),
        P(None, "blk"),
        P(None, "blk"),
        P("blk", None),
        P("blk", None, None),
        P("blk", None, None),
        P("blk", None, None),
        P(None, None, "blk"),
        P(None, None, "blk"),
        P(None, None, "blk"),
        P(),
        P(),
    )
    return jax.shard_map(
        local,
        mesh=mesh,
        in_specs=placed,
        out_specs=(
            P(("blk", "grp"), None),
            P(("blk", "grp"), None),
            P(("blk", "grp"), None, None),
            P(("blk", "grp"), None, None),
            P(("blk", "grp"), None, None),
            P("grp", None, "blk"),
            P("grp", None, "blk"),
            P("grp", None, "blk"),
        ),
        check_vma=False,
    )
```
